256 devices in a mesh: seq: 32 (over z, y_hi, core), vocab: 8 (over x, y_lo).
Axes of the slice: x: 4, y: 4 (y_hi: 2, y_lo: 2; y = y_hi * 2 + y_lo), z: 8, core: 2. Of those that a mesh axis runs over, the one named last changes fastest.
Arguments:
- tokens: bfloat16 [16384, 2048], P('seq'), may hold values from -6 to 6
- attention_gain: bfloat16 [2048], replicated, may hold values from 0.099609375 to 1.8984375
- query_weight: bfloat16 [2048, 2048], P(None, 'vocab')
- key_weight: bfloat16 [2048, 1024], P(None, 'vocab')
- value_weight: bfloat16 [2048, 1024], P(None, 'vocab'), may hold values from -0.125 to 0.125
- out_weight: bfloat16 [2048, 2048], P('vocab'), may hold values from -0.125 to 0.125
- forward_gain: bfloat16 [2048], replicated, may hold values from 0.099609375 to 1.8984375
- gate_weight: bfloat16 [2048, 4096], P(None, 'vocab'), may hold values from -0.125 to 0.125
- up_weight: bfloat16 [2048, 4096], P(None, 'vocab'), may hold values from -0.125 to 0.125
- down_weight: bfloat16 [4096, 2048], P('vocab'), may hold values from -0.09375 to 0.09375
- final_gain: bfloat16 [2048], replicated, may hold values from 0.099609375 to 1.8984375
- head_weight: bfloat16 [92160, 2048], P(('seq', 'vocab')), may hold values from -0.375 to 0.375
- segment_ids: int32 [16384], replicated, may hold values from 0 to 3, as said below
- token_order: int32 [16384], P('seq'), may hold values from 0 to 16383, as said below
- live_blocks: int32 [32, 32], P('seq'), may hold values from 0 to 1, as said below
- cache_slots: int32 [16384], P('seq'), may hold values from 0 to 511, as said below
Outputs:
- hidden_out: bfloat16 [16384, 2048], P('seq', 'vocab')
- kv_cache: bfloat16 [16384, 2, 1024], P('seq', None, 'vocab')
- final_rms: float32 [4], replicated
- top_logit: float32 [4], replicated
The draws below stay inside these ranges and needn't reach their ends.
Inputs may be any that keep to these rules, and one draw needn't show every extreme that they name: `segment_ids`: Non-decreasing; each request covers 1 to 8192 consecutive positions, one request exactly 8192. `token_order`: each initial position appears in exactly one slot. The 512 slots of each slot block hold two runs of 256 consecutive initial positions, each run starting at a multiple of 256 and increasing along the slots. live_blocks[b, s] is 1 exactly when some slot of block b and some slot of block (b - s) mod 32 share a request with the key's position not after the query's. `cache_slots`: within each slot block of 512 slots the values are a permutation.
All inputs are finite; a program needn't handle non-finite values.
Results may differ from the reference program's by a relative error of at most 0.02.
Values may be sent and summed in bfloat16 or wider, within the bound.
A program may use at most 128 MiB of HBM per device.

```python
import math
import jax
import jax.numpy as jnp
from jax import lax

D = 2048
H = 16
KVH = 8
HD = 128
FF = 4096
TOK_DEV = 512
REQS = 4
TOKENS = 16384
MAX_LEN = 8192
VOCAB = 92160
N_SEQ = 32
N_VOCAB = 8


def place_run(run_map, wanted, target):
    where_now = jnp.argmax((run_map == wanted).astype(jnp.int32)).astype(jnp.int32)
    there = run_map[target]
    run_map = run_map.at[where_now].set(there)
    return run_map.at[target].set(wanted).astype(jnp.int32)


def layout_tables(key):
    base = jax.random.fold_in(key, 101)
    rest = TOKENS - MAX_LEN
    first = jax.random.randint(jax.random.fold_in(base, 1), (), 1, rest - 1)
    second = jax.random.randint(jax.random.fold_in(base, 2), (), 1, rest - first)
    third = rest - first - second
    others = jnp.stack([first, second, third]).astype(jnp.int32)
    longest = jax.random.randint(jax.random.fold_in(base, 3), (), 0, REQS)
    places = jnp.arange(REQS, dtype=jnp.int32)
    picked = jnp.clip(places - (places > longest).astype(jnp.int32), 0, REQS - 2)
    lengths = jnp.where(places == longest, MAX_LEN, others[picked]).astype(jnp.int32)
    ends = jnp.cumsum(lengths).astype(jnp.int32)
    starts = ends - lengths
    cells = jnp.arange(TOKENS, dtype=jnp.int32)
    segment = jnp.sum((cells[:, None] >= ends[None, :]).astype(jnp.int32), axis=1).astype(jnp.int32)
    blocks = TOKENS // TOK_DEV
    half = TOK_DEV // 2
    run_map = jax.random.permutation(jax.random.fold_in(base, 4), 2 * blocks).astype(jnp.int32)
    long_run = ((jnp.sum(jnp.where(places == longest, ends, 0)) - 1) // half).astype(jnp.int32)
    final_run = (TOKENS - 1) // half
    run_map = place_run(run_map, long_run, 2 * (blocks // 2) + 1)
    run_map = jnp.where(final_run != long_run, place_run(run_map, jnp.int32(final_run), 0), run_map).astype(jnp.int32)
    order = (run_map[:, None] * half + jnp.arange(half, dtype=jnp.int32)[None, :]).reshape(TOKENS)
    query_low = run_map[:, None] * half
    key_low = run_map[None, :] * half
    first_query = jnp.maximum(query_low, key_low)
    inside = first_query <= query_low + half - 1
    first_segment = segment[jnp.minimum(first_query, TOKENS - 1)]
    reaches = starts[first_segment] <= key_low + half - 1
    pair_live = (inside & reaches).reshape(blocks, 2, blocks, 2)
    block_live = jnp.any(jnp.any(pair_live, axis=3), axis=1)
    steps = jnp.arange(blocks, dtype=jnp.int32)
    source = (steps[:, None] - steps[None, :]) % blocks
    live = block_live[steps[:, None], source].astype(jnp.int32)
    return (segment, order.astype(jnp.int32), live)


def attention_tables(key):
    base = jax.random.fold_in(key, 202)
    key_part = jax.random.normal(jax.random.fold_in(base, 1), (D, KVH * HD), jnp.float32) * D ** (-0.5)
    query_part = jax.random.normal(jax.random.fold_in(base, 2), (D, H * HD), jnp.float32) * D ** (-0.5)
    return (query_part, key_part)


def draw_segment_ids(key, part):
    return layout_tables(key)[0]


def draw_token_order(key, part):
    return layout_tables(key)[1]


def draw_live_blocks(key, part):
    return layout_tables(key)[2]


def draw_cache_slots(key, part):
    blocks = TOKENS // TOK_DEV
    block_keys = jax.random.split(jax.random.fold_in(key, 303), blocks)
    slots = jax.vmap(lambda block_key: jax.random.permutation(block_key, TOK_DEV))(block_keys)
    return slots.reshape(TOKENS).astype(jnp.int32)


def draw_query_weight(key, part):
    return attention_tables(key)[0].astype(jnp.bfloat16)


def draw_key_weight(key, part):
    return attention_tables(key)[1].astype(jnp.bfloat16)


def levels(key, extent, cuts, smallest, top_value):
    level, own = 1.0, jax.random.fold_in(key, 6)
    for axis_at, parts in cuts:
        draws = jnp.exp(jax.random.uniform(jax.random.fold_in(own, axis_at), (parts,), jnp.float32, smallest / len(cuts), top_value / len(cuts)))
        level = level * jnp.repeat(draws, extent[axis_at] // parts).reshape([-1 if axis == axis_at else 1 for axis in range(len(extent))])
    return level


def normal_values(own_key, extent, scale, bound, cuts=(), held_as=jnp.bfloat16):
    values = scale * jax.random.normal(own_key, extent, jnp.float32)
    if cuts:
        values = values * levels(own_key, extent, cuts, -0.22, 0.18)
    return jnp.clip(values, -bound, bound).astype(held_as)


def setup_inputs(seed: int = 0) -> dict:
    key_list = jax.random.split(jax.random.key(seed), 17)
    return {
        "tokens": normal_values(key_list[0], (TOKENS, D), 1.0, 6.0, ((0, 32),)),
        "attention_gain": jnp.clip(1.0 + 0.18 * jax.random.normal(key_list[1], (D,), jnp.float32), 0.099609375, 1.8984375).astype(jnp.bfloat16),
        "query_weight": draw_query_weight(jax.random.fold_in(key_list[16], 71), 0),
        "key_weight": draw_key_weight(jax.random.fold_in(key_list[16], 71), 0),
        "value_weight": normal_values(key_list[4], (D, KVH * HD), D ** -0.5, 0.125, ((1, 8),)),
        "out_weight": normal_values(key_list[5], (H * HD, D), (H * HD) ** -0.5, 0.125, ((0, 8),)),
        "forward_gain": jnp.clip(1.0 + 0.18 * jax.random.normal(key_list[6], (D,), jnp.float32), 0.099609375, 1.8984375).astype(jnp.bfloat16),
        "gate_weight": normal_values(key_list[7], (D, FF), D ** -0.5, 0.125, ((1, 8),)),
        "up_weight": normal_values(key_list[8], (D, FF), D ** -0.5, 0.125, ((1, 8),)),
        "down_weight": normal_values(key_list[9], (FF, D), FF ** -0.5, 0.09375, ((0, 8),)),
        "final_gain": jnp.clip(1.0 + 0.18 * jax.random.normal(key_list[10], (D,), jnp.float32), 0.099609375, 1.8984375).astype(jnp.bfloat16),
        "head_weight": normal_values(key_list[11], (VOCAB, D), (D // 9) ** -0.5, 0.375, ((0, 256),)),
        "segment_ids": draw_segment_ids(jax.random.fold_in(key_list[16], 71), 0),
        "token_order": draw_token_order(jax.random.fold_in(key_list[16], 71), 0),
        "live_blocks": draw_live_blocks(jax.random.fold_in(key_list[16], 71), 0),
        "cache_slots": draw_cache_slots(jax.random.fold_in(key_list[16], 71), 0),
    }


epsilon = 1e-06
rope_base = 1000000.0
neg_fill = -1e+30

def rms_scale(values, gain):
    mean_square = lax.optimization_barrier(jnp.mean(values * values, axis=-1, keepdims=True))
    return values * lax.rsqrt(mean_square + epsilon) * gain.astype(jnp.float32)

def rotate(values, position):
    half = values.shape[-1] // 2
    inverse = rope_base ** (-jnp.arange(half, dtype=jnp.float32) * 2.0 / values.shape[-1])
    angle = position.astype(jnp.float32)[:, None] * inverse[None, :]
    angle = jnp.concatenate([angle, angle], axis=-1)[:, None, :]
    first = values[..., :half]
    second = values[..., half:]
    turned = jnp.concatenate([-second, first], axis=-1)
    return values * jnp.cos(angle) + turned * jnp.sin(angle)

def reference(tokens, attention_gain, query_weight, key_weight, value_weight, out_weight, forward_gain, gate_weight, up_weight, down_weight, final_gain, head_weight, segment_ids, token_order, live_blocks, cache_slots):
    total = tokens.shape[0]
    tok_rows = total // N_SEQ
    group = H // KVH
    request = jnp.arange(REQS, dtype=jnp.int32)
    counts = lax.optimization_barrier(jnp.sum((segment_ids[None, :] == request[:, None]).astype(jnp.int32), axis=1))
    starts = lax.optimization_barrier(jnp.sum((segment_ids[None, :] < request[:, None]).astype(jnp.int32), axis=1))
    segment = segment_ids[token_order]
    position = token_order - starts[segment]
    device = jnp.arange(total, dtype=jnp.int32) // tok_rows
    normed = rms_scale(tokens.astype(jnp.float32), attention_gain).astype(jnp.bfloat16)
    query = rotate(jnp.dot(normed, query_weight, preferred_element_type=jnp.float32).reshape(total, H, HD), position).astype(jnp.bfloat16)
    key = rotate(jnp.dot(normed, key_weight, preferred_element_type=jnp.float32).reshape(total, KVH, HD), position).astype(jnp.bfloat16)
    value = jnp.dot(normed, value_weight, preferred_element_type=jnp.float32).astype(jnp.bfloat16)
    cache_rows = (device * tok_rows + cache_slots).astype(jnp.int32)
    stacked = jnp.stack([key.reshape(total, KVH * HD), value], axis=1)
    kv_cache = jnp.zeros((total, 2, KVH * HD), jnp.bfloat16).at[cache_rows].set(stacked)
    key_rep = jnp.repeat(key, group, axis=1).astype(jnp.float32)
    value_rep = jnp.repeat(value.reshape(total, KVH, HD), group, axis=1).astype(jnp.float32)
    width = math.gcd(total, 256)
    scale = HD ** (-0.5)

    def attend(index):
        low = index * width
        query_block = lax.dynamic_slice_in_dim(query, low, width, 0).astype(jnp.float32)
        order_query = lax.dynamic_slice_in_dim(token_order, low, width, 0)
        segment_query = lax.dynamic_slice_in_dim(segment, low, width, 0)
        device_query = lax.dynamic_slice_in_dim(device, low, width, 0)
        live = live_blocks[device_query[:, None], (device_query[:, None] - device[None, :]) % N_SEQ]
        allowed = (segment_query[:, None] == segment[None, :]) & (token_order[None, :] <= order_query[:, None]) & (live > 0)
        scores = jnp.einsum('qhd,khd->hqk', query_block, key_rep) * scale
        scores = jnp.where(allowed[None], scores, neg_fill)
        top = lax.optimization_barrier(jnp.max(scores, axis=-1, keepdims=True))
        probs = jnp.where(allowed[None], jnp.exp(scores - top), 0.0)
        weight_total = lax.optimization_barrier(jnp.sum(probs, axis=-1))
        weights = lax.optimization_barrier(probs.astype(jnp.bfloat16)).astype(jnp.float32)
        summed = jnp.einsum('hqk,khd->qhd', weights, value_rep)
        return (summed / jnp.transpose(weight_total)[:, :, None]).astype(jnp.bfloat16)
    heads_out = lax.map(attend, jnp.arange(total // width, dtype=jnp.int32)).reshape(total, H * HD)
    head_cols = H // N_VOCAB * HD
    attention_sum = jnp.zeros((total, D), jnp.float32)
    for group_index in range(N_VOCAB):
        partial_sum = jnp.dot(heads_out[:, group_index * head_cols:(group_index + 1) * head_cols], out_weight[group_index * head_cols:(group_index + 1) * head_cols], preferred_element_type=jnp.float32)
        attention_sum = attention_sum + lax.optimization_barrier(partial_sum.astype(jnp.bfloat16)).astype(jnp.float32)
    residual = tokens.astype(jnp.float32) + attention_sum
    mid_normed = rms_scale(residual, forward_gain).astype(jnp.bfloat16)
    gate = jnp.dot(mid_normed, gate_weight, preferred_element_type=jnp.float32)
    upward = jnp.dot(mid_normed, up_weight, preferred_element_type=jnp.float32)
    activated = (jax.nn.silu(gate) * upward).astype(jnp.bfloat16)
    unit_cols = FF // N_VOCAB
    forward_sum = jnp.zeros((total, D), jnp.float32)
    for group_index in range(N_VOCAB):
        partial_sum = jnp.dot(activated[:, group_index * unit_cols:(group_index + 1) * unit_cols], down_weight[group_index * unit_cols:(group_index + 1) * unit_cols], preferred_element_type=jnp.float32)
        forward_sum = forward_sum + lax.optimization_barrier(partial_sum.astype(jnp.bfloat16)).astype(jnp.float32)
    hidden_out = (residual + forward_sum).astype(jnp.bfloat16)
    last_index = starts + counts - 1
    slot_index = lax.optimization_barrier(jnp.sum(jnp.where(token_order[None, :] == last_index[:, None], jnp.arange(total, dtype=jnp.int32)[None, :], 0), axis=1)).astype(jnp.int32)
    last_rows = hidden_out[slot_index].astype(jnp.float32)
    mean_square = lax.optimization_barrier(jnp.mean(last_rows * last_rows, axis=-1, keepdims=True))
    final_rms = jnp.sqrt(mean_square[:, 0] + epsilon)
    last_normed = (last_rows * lax.rsqrt(mean_square + epsilon) * final_gain.astype(jnp.float32)).astype(jnp.bfloat16)
    logits = lax.dot_general(last_normed, head_weight, (((1,), (1,)), ((), ())), preferred_element_type=jnp.float32)
    top_logit = lax.optimization_barrier(jnp.max(logits, axis=1))
    return (hidden_out, kv_cache, final_rms, top_logit)
```

```python
import functools

import jax
import jax.numpy as jnp
from jax import lax
from jax.experimental import pallas as pl
from jax.experimental.pallas import tpu as pltpu
from jax.sharding import PartitionSpec as P

MESH = pl.DeviceIdType.MESH
HD = 128
REQS = 4
epsilon = 1e-06
rope_base = 1000000.0
neg_fill = -1e30
VM = pl.BlockSpec(memory_space=pltpu.VMEM)
SM = pl.BlockSpec(memory_space=pltpu.SMEM)
HB = pl.BlockSpec(memory_space=pl.ANY)
F32 = jnp.float32
BF16 = jnp.bfloat16
LIMIT = 62 * 1024 * 1024


def params(cid=None):
    if cid is None:
        return pltpu.CompilerParams(vmem_limit_bytes=LIMIT)
    return pltpu.CompilerParams(
        collective_id=cid, has_side_effects=True, vmem_limit_bytes=LIMIT
    )


def seq_at(s, dz, dy, dc):
    z, y, c = s // 4, (s // 2) % 2, s % 2
    return ((z + dz + 8) % 8) * 4 + ((y + dy) % 2) * 2 + (c + dc) % 2


def vocab_at(v, dx, dy):
    x, y = v // 2, v % 2
    return ((x + dx + 4) % 4) * 2 + (y + dy) % 2


def greet(peers):
    barrier = pltpu.get_barrier_semaphore()
    for peer in peers:
        pl.semaphore_signal(barrier, inc=1, device_id=peer, device_id_type=MESH)
    pl.semaphore_wait(barrier, len(peers))


def project_kernel(
    base_ref, tok_ref, gain_ref, wq_ref, wk_ref, wv_ref, cos_ref, sin_ref, slot_ref,
    q_ref, kv_ref, cache_ref,
):
    gain = gain_ref[...].astype(F32)

    def rows_step(i, carry):
        rows = pl.ds(pl.multiple_of(i * 128, 128), 128)
        x = tok_ref[rows, :].astype(F32)
        scale = lax.rsqrt(jnp.mean(x * x, axis=-1, keepdims=True) + epsilon)
        normed = (x * scale * gain).astype(BF16)
        cos = cos_ref[rows, :]
        sin = sin_ref[rows, :]

        def turn(u):
            return u * cos + pltpu.roll(u, 64, axis=1) * sin

        q = jnp.dot(normed, wq_ref[...], preferred_element_type=F32)
        q_ref[rows, 0:128] = turn(q[:, 0:128]).astype(BF16)
        q_ref[rows, 128:256] = turn(q[:, 128:256]).astype(BF16)
        k = jnp.dot(normed, wk_ref[...], preferred_element_type=F32)
        kv_ref[rows, 0:128] = turn(k).astype(BF16)
        v = jnp.dot(normed, wv_ref[...], preferred_element_type=F32)
        kv_ref[rows, 128:256] = v.astype(BF16)
        return carry

    lax.fori_loop(0, 4, rows_step, 0)
    lane = lax.broadcasted_iota(jnp.int32, (16, 256), 1)
    run = jnp.where(lane < 128, base_ref[0] // 256, base_ref[1] // 256)
    kv_ref[512:528, :] = run.astype(F32).astype(BF16)
    slots = slot_ref[...]

    def cache_step(i, carry):
        row = i * 128 + lax.broadcasted_iota(jnp.int32, (128, 512), 0)
        pick = jnp.where(row == slots, 1.0, 0.0).astype(BF16)
        moved = jnp.dot(pick, kv_ref[0:512, :], preferred_element_type=F32)
        cache_ref[pl.ds(pl.multiple_of(i * 128, 128), 128), :] = moved.astype(BF16)
        return carry

    lax.fori_loop(0, 4, cache_step, 0)


PIECE_ROWS = ((0, 256), (256, 272))


def gather_kernel(kv_ref, w_ref, kv_all, w_all, own_sem, send_sem, kv_sem, w_sem):
    s = lax.axis_index("seq")
    v = lax.axis_index("vocab")
    c = s % 2
    up = (seq_at(s, 1, 0, 0), v)
    down = (seq_at(s, -1, 0, 0), v)
    side = (seq_at(s, 0, 1, 0), v)
    core = (seq_at(s, 0, 0, 1), v)
    right = (s, vocab_at(v, 1, 0))
    left = (s, vocab_at(v, -1, 0))
    near = (s, vocab_at(v, 0, 1))
    greet([up, down, side, core, right, left, near])

    started = []

    def kv_view(block, p):
        low, count = PIECE_ROWS[p]
        return kv_all.at[block, pl.ds(low, count), :]

    def kv_copy(src, block, p, peer):
        return pltpu.make_async_remote_copy(
            src_ref=src, dst_ref=kv_view(block, p), send_sem=send_sem.at[len(started)],
            recv_sem=kv_sem.at[block, p], device_id=peer, device_id_type=MESH,
        )

    def w_copy(src, shard, p, peer):
        return pltpu.make_async_remote_copy(
            src_ref=src, dst_ref=w_all.at[shard, p], send_sem=send_sem.at[len(started)],
            recv_sem=w_sem.at[shard, p], device_id=peer, device_id_type=MESH,
        )

    def go(copy):
        copy.start()
        started.append(copy)

    def kv_take(dz, dy, p, peers):
        block = seq_at(s, dz, dy, 0)
        kv_copy(kv_view(block, p), block, p, core).wait_recv()
        for peer in peers:
            go(kv_copy(kv_view(block, p), block, p, peer))

    def w_take(dx, dy, p, peers):
        shard = vocab_at(v, dx, dy)
        part = 2 * c + p
        w_copy(w_all.at[shard, part], shard, part, core).wait_recv()
        for peer in peers:
            go(w_copy(w_all.at[shard, part], shard, part, peer))

    own = []
    for p in range(2):
        low, count = PIECE_ROWS[p]
        src = kv_ref.at[pl.ds(low, count), :]
        for peer in (up, down, side, core):
            go(kv_copy(src, s, p, peer))
        part = 2 * c + p
        for peer in (right, left, near):
            go(w_copy(w_ref.at[part], v, part, peer))
    own.append(pltpu.make_async_copy(kv_ref, kv_all.at[s], own_sem.at[0]))
    own.append(pltpu.make_async_copy(w_ref, w_all.at[v], own_sem.at[1]))
    for copy in own:
        copy.start()

    for d in (1, 2):
        for p in range(2):
            kv_take(-d, 0, p, (up, core))
            kv_take(d, 0, p, (down, core))
    for p in range(2):
        w_take(-1, 0, p, (right, core) if p == 0 else (core,))
        w_take(1, 0, p, (left, core) if p == 1 else (core,))
    for p in range(2):
        kv_take(0, 1, p, (up, down, core))
    for p in range(2):
        w_take(0, 1, p, (right, left, core))
    for p in range(2):
        kv_take(-3, 0, p, (up, side, core) if p == 0 else (side, core))
        kv_take(3, 0, p, (down, side, core) if p == 1 else (side, core))
    for p in range(2):
        kv_take(-1, 1, p, (up, core))
        kv_take(1, 1, p, (down, core))
    for p in range(2):
        w_take(2, 0, p, (core,))
    for p in range(2):
        kv_take(4, 0, p, (side, core))
    for p in range(2):
        w_take(-1, 1, p, (right, core) if p == 0 else (core,))
        w_take(1, 1, p, (left, core) if p == 1 else (core,))
    for p in range(2):
        kv_take(-2, 1, p, (core,))
        kv_take(2, 1, p, (core,))
    for p in range(2):
        kv_take(-3, 1, p, (core,))
        kv_take(3, 1, p, (core,))
    for p in range(2):
        w_take(2, 1, p, (core,))
    for p in range(2):
        kv_take(4, 1, p, (core,))

    for dz in range(8):
        for dy in range(2):
            for p in range(2):
                block = seq_at(s, dz, dy, 1)
                kv_copy(kv_view(block, p), block, p, core).wait_recv()
    for dx in range(4):
        for dy in range(2):
            if (dx, dy) != (0, 0):
                for p in range(2):
                    shard = vocab_at(v, dx, dy)
                    part = 2 * (1 - c) + p
                    w_copy(w_all.at[shard, part], shard, part, core).wait_recv()
    for copy in own:
        copy.wait()
    for copy in started:
        copy.wait_send()


SLOTS = 8


def attend_kernel(
    where_ref, base_ref, starts_ref, live_ref, me_ref, q_ref, kv_ref, o_ref,
    buf, sem, q_rows, top, total, acc,
):
    me = me_ref[0]
    scale = HD ** (-0.5) * 1.4426950408889634
    for r in range(2):
        for h in range(2):
            q_rows[r, pl.ds(h * 256, 256), :] = q_ref[
                pl.ds(r * 256, 256), pl.ds(h * 128, 128)
            ]
    top[...] = jnp.full_like(top, neg_fill)
    total[...] = jnp.zeros_like(total)
    acc[...] = jnp.zeros_like(acc)

    def low_of(position):
        low = starts_ref[0]
        for r in range(1, REQS):
            low = jnp.where(starts_ref[r] <= position, starts_ref[r], low)
        return low

    base0, base1 = base_ref[0], base_ref[1]
    first0, first1 = low_of(base0) // 256, low_of(base1) // 256
    last0, last1 = low_of(base0 + 255), low_of(base1 + 255)
    count0 = base0 // 256 - first0 + 1
    count1 = base1 // 256 - first1 + 1
    n = count0 + count1

    def key_run(i):
        return jnp.where(i < count0, first0 + i, first1 + i - count0)

    def fetch(i):
        entry = where_ref[key_run(i)]
        slot = i % SLOTS
        return pltpu.make_async_copy(
            kv_ref.at[entry // 2, pl.ds((entry % 2) * 256, 256), :], buf.at[slot], sem.at[slot]
        )

    for i in range(SLOTS - 1):

        @pl.when(i < n)
        def _():
            fetch(i).start()

    def update(i, r, masked, run, base):
        slot = i % SLOTS
        keys = buf[slot, :, 0:128]
        values = buf[slot, :, 128:256]
        scores = lax.dot_general(
            keys, q_rows[r], (((1,), (1,)), ((), ())), preferred_element_type=F32
        )
        if masked:
            lane = lax.broadcasted_iota(jnp.int32, (1, 512), 1)
            q_pos = base + (lane % 256)
            low = jnp.full((1, 512), starts_ref[0], jnp.int32)
            for req in range(1, REQS):
                low = jnp.where(starts_ref[req] <= q_pos, starts_ref[req], low)
            k_pos = run * 256 + lax.broadcasted_iota(jnp.int32, (256, 512), 0)
            allowed = (k_pos <= q_pos) & (k_pos >= low)
            scores = jnp.where(allowed, scores, neg_fill)
        old = top[r]
        new = jnp.maximum(old, jnp.max(scores, axis=0, keepdims=True))
        probs = jnp.exp2((scores - new) * scale)
        if masked:
            probs = jnp.where(allowed, probs, 0.0)
        keep = jnp.exp2((old - new) * scale)
        top[r] = new
        total[r] = total[r] * keep + jnp.sum(probs, axis=0, keepdims=True)
        added = lax.dot_general(
            values, probs.astype(BF16), (((0,), (0,)), ((), ())), preferred_element_type=F32
        )
        acc[r] = acc[r] * keep + added

    def step(i, carry):
        @pl.when(i + SLOTS - 1 < n)
        def _():
            fetch(i + SLOTS - 1).start()

        fetch(i).wait()
        r = jnp.where(i < count0, 0, 1)
        run = key_run(i)
        base = jnp.where(r == 0, base0, base1)
        last_low = jnp.where(r == 0, last0, last1)
        entry = where_ref[run]
        live = live_ref[(me - entry // 2 + 32) % 32] > 0
        whole = (run * 256 < base) & (run * 256 >= last_low)

        @pl.when(live & whole)
        def _():
            update(i, r, False, run, base)

        @pl.when(live & jnp.logical_not(whole))
        def _():
            update(i, r, True, run, base)

        return carry

    lax.fori_loop(0, n, step, 0)
    for r in range(2):
        done = acc[r] / total[r]
        for h in range(2):
            o_ref[pl.ds(r * 256, 256), pl.ds(h * 128, 128)] = jnp.transpose(
                done[:, h * 256 : (h + 1) * 256]
            ).astype(BF16)


def middle_kernel(
    heads_ref, w_ref, tok_ref, gain_ref, wg_ref, wu_ref, wd_ref, out_ref,
    heads, w, tok_rows, tok_cols, wg, wu, wd, att, att_send, att_cols, normed, act, part, got,
    load_sem, head_send, head_recv, norm_send, norm_recv, att_sent, att_recv, part_send, part_recv,
):
    s = lax.axis_index("seq")
    v = lax.axis_index("vocab")
    others = [(v + r) % 8 for r in range(1, 8)]
    cols = pl.ds(pl.multiple_of(v * 256, 256), 256)
    rows = pl.ds(pl.multiple_of(v * 64, 64), 64)
    loads = [
        pltpu.make_async_copy(w_ref, w, load_sem.at[0]),
        pltpu.make_async_copy(tok_ref.at[rows, :], tok_rows, load_sem.at[1]),
        pltpu.make_async_copy(tok_ref.at[:, cols], tok_cols, load_sem.at[2]),
        pltpu.make_async_copy(wg_ref, wg, load_sem.at[3]),
        pltpu.make_async_copy(wu_ref, wu, load_sem.at[4]),
        pltpu.make_async_copy(wd_ref, wd, load_sem.at[5]),
        pltpu.make_async_copy(heads_ref.at[rows, :], heads.at[v], load_sem.at[6]),
    ]
    for copy in loads:
        copy.start()
    greet([(s, other) for other in others])

    def to(src, dst, sends, recvs, i, slot, other):
        return pltpu.make_async_remote_copy(
            src_ref=src, dst_ref=dst, send_sem=sends.at[i], recv_sem=recvs.at[slot],
            device_id=(s, other), device_id_type=MESH,
        )

    sent = []

    def go(copy):
        copy.start()
        sent.append(copy)

    for i, other in enumerate(others):
        src = heads_ref.at[pl.ds(pl.multiple_of(other * 64, 64), 64), :]
        go(to(src, heads.at[v], head_send, head_recv, i, v, other))
    for i, other in enumerate(others):
        to(heads.at[other], heads.at[other], head_send, head_recv, i, other, other).wait_recv()
    for i in (0, 1, 6):
        loads[i].wait()

    def project(j, square):
        wide = pl.ds(pl.multiple_of(j * 512, 512), 512)
        total = jnp.dot(heads[0], w[0:256, wide], preferred_element_type=F32)
        for k in range(1, 8):
            total += jnp.dot(
                heads[k], w[k * 256 : (k + 1) * 256, wide], preferred_element_type=F32
            )
        att_send[2 * j] = total[:, 0:256].astype(BF16)
        att_send[2 * j + 1] = total[:, 256:512].astype(BF16)
        residual = tok_rows[:, wide].astype(F32) + total
        att[:, wide] = residual
        return square + jnp.sum(residual * residual, axis=-1, keepdims=True)

    square = lax.fori_loop(0, 4, project, jnp.zeros((64, 1), F32))
    inverse = lax.rsqrt(square / 2048 + epsilon)
    mine = (att[...] * inverse * gain_ref[...].astype(F32)).astype(BF16)
    normed[v, 0] = mine[0:32]
    normed[v, 1] = mine[32:64]

    right, left, near = vocab_at(v, 1, 0), vocab_at(v, -1, 0), vocab_at(v, 0, 1)
    count = [0]

    def pass_on(owner, p, other):
        view = normed.at[owner, p]
        copy = pltpu.make_async_remote_copy(
            src_ref=view, dst_ref=view, send_sem=norm_send.at[count[0]],
            recv_sem=norm_recv.at[owner, p], device_id=(s, other), device_id_type=MESH,
        )
        count[0] += 1
        go(copy)

    def arrive(dx, dy, p, peers):
        owner = vocab_at(v, dx, dy)
        view = normed.at[owner, p]
        pltpu.make_async_remote_copy(
            src_ref=view, dst_ref=view, send_sem=norm_send.at[0],
            recv_sem=norm_recv.at[owner, p], device_id=(s, near), device_id_type=MESH,
        ).wait_recv()
        for peer in peers:
            pass_on(owner, p, peer)

    for p in range(2):
        for peer in (right, left, near):
            pass_on(v, p, peer)
    for i, other in enumerate(others):
        go(to(att_send.at[other], att_cols.at[v], att_sent, att_recv, i, v, other))
    own_cols = pltpu.make_async_copy(att_send.at[v], att_cols.at[v], load_sem.at[7])
    own_cols.start()
    for p in range(2):
        arrive(-1, 0, p, (right,) if p == 0 else ())
        arrive(1, 0, p, (left,) if p == 1 else ())
        arrive(0, 1, p, (right, left))
    for p in range(2):
        arrive(-1, 1, p, (right,) if p == 0 else ())
        arrive(1, 1, p, (left,) if p == 1 else ())
    for p in range(2):
        arrive(2, 0, p, ())
        arrive(2, 1, p, ())
    for i in (2, 3, 4, 5):
        loads[i].wait()

    def feed(i, carry):
        x = normed[pl.ds(2 * i, 2)].reshape(128, 2048)
        gate = jnp.dot(x, wg[...], preferred_element_type=F32)
        upward = jnp.dot(x, wu[...], preferred_element_type=F32)
        value = gate / (1.0 + jnp.exp(-gate)) * upward
        act[pl.ds(pl.multiple_of(i * 128, 128), 128), :] = value.astype(BF16)
        return carry

    lax.fori_loop(0, 4, feed, 0)

    def lower(other):
        wide = pl.ds(pl.multiple_of(other * 256, 256), 256)
        return jnp.dot(act[...], wd[:, wide], preferred_element_type=F32).astype(BF16)

    for i, other in enumerate(others):
        part[i] = lower(other)
        go(to(part.at[i], got.at[v], part_send, part_recv, i, v, other))
    got[v] = lower(v)
    own_cols.wait()
    for i, other in enumerate(others):
        to(att_cols.at[other], att_cols.at[other], att_sent, att_recv, i, other, other).wait_recv()
    for i, other in enumerate(others):
        to(got.at[other], got.at[other], part_send, part_recv, i, other, other).wait_recv()

    def finish(i, carry):
        chunk = pl.ds(pl.multiple_of(i * 64, 64), 64)
        residual = tok_cols[chunk, :].astype(F32) + att_cols[i].astype(F32)
        total = got[0, chunk, :].astype(F32)
        for k in range(1, 8):
            total += got[k, chunk, :].astype(F32)
        out_ref[chunk, :] = (residual + total).astype(BF16)
        return carry

    lax.fori_loop(0, 8, finish, 0)
    for copy in sent:
        copy.wait_send()


def last_kernel(
    match_ref, hidden_ref, gain_ref, head_ref, rms_ref, top_ref,
    head, row_send, seq_got, wide_got, max_send, seq_max, wide_send, vocab_max,
    load_sem, send_sem, seq_sem, wide_sem, max_sem, last_sem,
):
    s = lax.axis_index("seq")
    v = lax.axis_index("vocab")
    load = pltpu.make_async_copy(head_ref, head, load_sem.at[0])
    load.start()
    seqs = [(s + r) % 32 for r in range(1, 32)]
    vocabs = [(v + r) % 8 for r in range(1, 8)]
    greet([(other, v) for other in seqs] + [(s, other) for other in vocabs])
    sent = []

    def exchange(src, dst, sems, index, peers, slots):
        for peer in peers:
            copy = pltpu.make_async_remote_copy(
                src_ref=src, dst_ref=dst.at[index], send_sem=send_sem.at[len(sent)],
                recv_sem=sems.at[index], device_id=peer, device_id_type=MESH,
            )
            copy.start()
            sent.append(copy)
        for peer, slot in zip(peers, slots):
            pltpu.make_async_remote_copy(
                src_ref=src, dst_ref=dst.at[slot], send_sem=send_sem.at[0],
                recv_sem=sems.at[slot], device_id=peer, device_id_type=MESH,
            ).wait_recv()

    seq_peers = [(other, v) for other in seqs]
    vocab_peers = [(s, other) for other in vocabs]
    picked = jnp.dot(match_ref[...], hidden_ref[...], preferred_element_type=F32)
    row_send[...] = picked
    seq_got[s] = picked
    exchange(row_send, seq_got, seq_sem, s, seq_peers, seqs)
    mine = jnp.sum(seq_got[...], axis=0)
    wide_send[...] = mine
    wide_got[v] = mine
    exchange(wide_send, wide_got, wide_sem, v, vocab_peers, vocabs)
    square = jnp.zeros((8, 1), F32)
    for k in range(8):
        square += jnp.sum(wide_got[k] * wide_got[k], axis=-1, keepdims=True)
    mean_square = square / 2048 + epsilon
    rms_ref[...] = jnp.broadcast_to(jnp.sqrt(mean_square), (8, 128))
    inverse = lax.rsqrt(mean_square)
    load.wait()
    logits = jnp.zeros((8, 360), F32)
    for k in range(8):
        gain = gain_ref[:, k * 256 : (k + 1) * 256].astype(F32)
        normed = (wide_got[k] * inverse * gain).astype(BF16)
        logits += lax.dot_general(
            normed, head[:, k * 256 : (k + 1) * 256], (((1,), (1,)), ((), ())),
            preferred_element_type=F32,
        )
    best = jnp.broadcast_to(jnp.max(logits, axis=-1, keepdims=True), (8, 128))
    max_send[0] = best
    seq_max[s] = best
    exchange(max_send.at[0], seq_max, max_sem, s, seq_peers, seqs)
    best = jnp.max(seq_max[...], axis=0)
    max_send[1] = best
    vocab_max[v] = best
    exchange(max_send.at[1], vocab_max, last_sem, v, vocab_peers, vocabs)
    top_ref[...] = jnp.max(vocab_max[...], axis=0)
    for copy in sent:
        copy.wait_send()


def per_device(
    tokens,
    attention_gain,
    query_weight,
    key_weight,
    value_weight,
    out_weight,
    forward_gain,
    gate_weight,
    up_weight,
    down_weight,
    final_gain,
    head_weight,
    segment_ids,
    token_order,
    live_blocks,
    cache_slots,
):
    shape = jax.ShapeDtypeStruct
    me = lax.axis_index("seq").astype(jnp.int32)
    request = jnp.arange(8, dtype=jnp.int32)
    starts = jnp.sum((segment_ids[None, :] < request[:, None]).astype(jnp.int32), axis=1)
    begins = jnp.where(starts[None, :REQS] <= token_order[:, None], starts[None, :REQS], 0)
    position = token_order - jnp.max(begins, axis=1)
    inverse = rope_base ** (-jnp.arange(64, dtype=F32) * 2.0 / 128)
    angle = position.astype(F32)[:, None] * inverse[None, :]
    cos, sin = jnp.cos(angle), jnp.sin(angle)
    cos = jnp.concatenate([cos, cos], axis=1)
    sin = jnp.concatenate([-sin, sin], axis=1)
    base = jnp.stack([token_order[0], token_order[256]])

    query, kv, cache = pl.pallas_call(
        project_kernel,
        out_shape=(shape((512, 256), BF16), shape((528, 256), BF16), shape((512, 256), BF16)),
        in_specs=[SM] + [VM] * 8,
        out_specs=(VM, VM, VM),
        compiler_params=params(),
        name="project",
    )(
        base, tokens, attention_gain[None], query_weight, key_weight, value_weight, cos, sin,
        cache_slots[None],
    )

    kv_all, w_all = pl.pallas_call(
        gather_kernel,
        out_shape=(shape((32, 528, 256), BF16), shape((8, 4, 64, 2048), BF16)),
        in_specs=[VM, HB],
        out_specs=(HB, HB),
        scratch_shapes=[
            pltpu.SemaphoreType.DMA((2,)),
            pltpu.SemaphoreType.DMA((128,)),
            pltpu.SemaphoreType.DMA((32, 2)),
            pltpu.SemaphoreType.DMA((8, 4)),
        ],
        compiler_params=params(0),
        name="gather",
    )(kv, out_weight.reshape(4, 64, 2048))

    runs = jnp.stack([kv_all[:, 512, 0], kv_all[:, 512, 128]], axis=1).astype(jnp.int32).reshape(64)
    entry = jnp.arange(64, dtype=jnp.int32)
    where = jnp.sum(jnp.where(runs[None, :] == entry[:, None], entry[None, :], 0), axis=1)
    heads = pl.pallas_call(
        attend_kernel,
        out_shape=shape((512, 256), BF16),
        in_specs=[SM, SM, SM, SM, SM, VM, HB],
        out_specs=VM,
        scratch_shapes=[
            pltpu.VMEM((SLOTS, 256, 256), BF16),
            pltpu.SemaphoreType.DMA((SLOTS,)),
            pltpu.VMEM((2, 512, 128), BF16),
            pltpu.VMEM((2, 1, 512), F32),
            pltpu.VMEM((2, 1, 512), F32),
            pltpu.VMEM((2, 128, 512), F32),
        ],
        compiler_params=params(),
        name="attend",
    )(where, base, starts, live_blocks[0], me[None], query, kv_all)

    dma = pltpu.SemaphoreType.DMA
    hidden = pl.pallas_call(
        middle_kernel,
        out_shape=shape((512, 256), BF16),
        in_specs=[VM, HB, HB, VM, HB, HB, HB],
        out_specs=VM,
        scratch_shapes=[
            pltpu.VMEM((8, 64, 256), BF16),
            pltpu.VMEM((2048, 2048), BF16),
            pltpu.VMEM((64, 2048), BF16),
            pltpu.VMEM((512, 256), BF16),
            pltpu.VMEM((2048, 512), BF16),
            pltpu.VMEM((2048, 512), BF16),
            pltpu.VMEM((512, 2048), BF16),
            pltpu.VMEM((64, 2048), F32),
            pltpu.VMEM((8, 64, 256), BF16),
            pltpu.VMEM((8, 64, 256), BF16),
            pltpu.VMEM((8, 2, 32, 2048), BF16),
            pltpu.VMEM((512, 512), BF16),
            pltpu.VMEM((7, 512, 256), BF16),
            pltpu.VMEM((8, 512, 256), BF16),
            dma((8,)), dma((7,)), dma((8,)), dma((16,)), dma((8, 2)), dma((7,)), dma((8,)),
            dma((7,)), dma((8,)),
        ],
        compiler_params=params(1),
        name="middle",
    )(
        heads, w_all.reshape(2048, 2048), tokens, forward_gain[None], gate_weight, up_weight,
        down_weight,
    )

    ends = jnp.concatenate([starts[1:REQS], jnp.full((1,), segment_ids.shape[0], jnp.int32)])
    last_index = jnp.concatenate([ends - 1, jnp.full((8 - REQS,), -1, jnp.int32)])
    match = (token_order[None, :] == last_index[:, None]).astype(BF16)
    rms, top = pl.pallas_call(
        last_kernel,
        out_shape=(shape((8, 128), F32), shape((8, 128), F32)),
        in_specs=[VM, VM, VM, HB],
        out_specs=(VM, VM),
        scratch_shapes=[
            pltpu.VMEM((360, 2048), BF16),
            pltpu.VMEM((8, 256), F32),
            pltpu.VMEM((32, 8, 256), F32),
            pltpu.VMEM((8, 8, 256), F32),
            pltpu.VMEM((2, 8, 128), F32),
            pltpu.VMEM((32, 8, 128), F32),
            pltpu.VMEM((8, 256), F32),
            pltpu.VMEM((8, 8, 128), F32),
            dma((1,)), dma((80,)), dma((32,)), dma((8,)), dma((32,)), dma((8,)),
        ],
        compiler_params=params(2),
        name="last",
    )(match, hidden, final_gain[None], head_weight)
    return (hidden, cache.reshape(512, 2, 128), rms[:REQS, 0], top[:REQS, 0])


def solution(mesh):
    return jax.shard_map(
        per_device,
        mesh=mesh,
        in_specs=(
            P("seq", None),
            P(),
            P(None, "vocab"),
            P(None, "vocab"),
            P(None, "vocab"),
            P("vocab", None),
            P(),
            P(None, "vocab"),
            P(None, "vocab"),
            P("vocab", None),
            P(),
            P(("seq", "vocab"), None),
            P(),
            P("seq"),
            P("seq", None),
            P("seq"),
        ),
        out_specs=(P("seq", "vocab"), P("seq", None, "vocab"), P(), P()),
        check_vma=False,
    )
```

```python
import functools

import jax
import jax.numpy as jnp
from jax import lax
from jax.experimental import pallas as pl
from jax.experimental.pallas import tpu as pltpu
from jax.sharding import PartitionSpec as P

MESH = pl.DeviceIdType.MESH
HD = 128
REQS = 4
epsilon = 1e-06
rope_base = 1000000.0
neg_fill = -1e30
VM = pl.BlockSpec(memory_space=pltpu.VMEM)
SM = pl.BlockSpec(memory_space=pltpu.SMEM)
HB = pl.BlockSpec(memory_space=pl.ANY)
F32 = jnp.float32
BF16 = jnp.bfloat16
LIMIT = 62 * 1024 * 1024
SCALE = HD ** (-0.5) * 1.4426950408889634


def params(cid=None):
    if cid is None:
        return pltpu.CompilerParams(vmem_limit_bytes=LIMIT)
    return pltpu.CompilerParams(
        collective_id=cid, has_side_effects=True, vmem_limit_bytes=LIMIT
    )


def seq_at(s, dz, dy, dc):
    z, y, c = s // 4, (s // 2) % 2, s % 2
    return ((z + dz + 8) % 8) * 4 + ((y + dy) % 2) * 2 + (c + dc) % 2


def vocab_at(v, dx, dy):
    x, y = v // 2, v % 2
    return ((x + dx + 4) % 4) * 2 + (y + dy) % 2


def greet(peers):
    barrier = pltpu.get_barrier_semaphore()
    for peer in peers:
        pl.semaphore_signal(barrier, inc=1, device_id=peer, device_id_type=MESH)
    pl.semaphore_wait(barrier, len(peers))


def project_kernel(
    base_ref, tok_ref, gain_ref, wq_ref, wk_ref, wv_ref, cos_ref, sin_ref, slot_ref,
    q_ref, kv_ref, cache_ref,
):
    gain = gain_ref[...].astype(F32)

    def rows_step(i, carry):
        rows = pl.ds(pl.multiple_of(i * 128, 128), 128)
        x = tok_ref[rows, :].astype(F32)
        scale = lax.rsqrt(jnp.mean(x * x, axis=-1, keepdims=True) + epsilon)
        normed = (x * scale * gain).astype(BF16)
        cos = cos_ref[rows, :]
        sin = sin_ref[rows, :]

        def turn(u):
            return u * cos + pltpu.roll(u, 64, axis=1) * sin

        q = jnp.dot(normed, wq_ref[...], preferred_element_type=F32)
        q_ref[rows, 0:128] = (turn(q[:, 0:128]) * SCALE).astype(BF16)
        q_ref[rows, 128:256] = (turn(q[:, 128:256]) * SCALE).astype(BF16)
        k = jnp.dot(normed, wk_ref[...], preferred_element_type=F32)
        kv_ref[rows, 0:128] = turn(k).astype(BF16)
        v = jnp.dot(normed, wv_ref[...], preferred_element_type=F32)
        kv_ref[rows, 128:256] = v.astype(BF16)
        return carry

    lax.fori_loop(0, 4, rows_step, 0)
    lane = lax.broadcasted_iota(jnp.int32, (16, 256), 1)
    run = jnp.where(lane < 128, base_ref[0] // 256, base_ref[256] // 256)
    kv_ref[512:528, :] = run.astype(F32).astype(BF16)
    slots = slot_ref[...]

    def cache_step(i, carry):
        row = i * 128 + lax.broadcasted_iota(jnp.int32, (128, 512), 0)
        pick = jnp.where(row == slots, 1.0, 0.0).astype(BF16)
        moved = jnp.dot(pick, kv_ref[0:512, :], preferred_element_type=F32)
        cache_ref[pl.ds(pl.multiple_of(i * 128, 128), 128), :] = moved.astype(BF16)
        return carry

    lax.fori_loop(0, 4, cache_step, 0)


PIECE_ROWS = ((0, 256), (256, 272))


def gather_kernel(kv_ref, w_ref, kv_all, w_all, own_sem, send_sem, kv_sem, w_sem):
    s = lax.axis_index("seq")
    v = lax.axis_index("vocab")
    c = s % 2
    up = (seq_at(s, 1, 0, 0), v)
    down = (seq_at(s, -1, 0, 0), v)
    side = (seq_at(s, 0, 1, 0), v)
    core = (seq_at(s, 0, 0, 1), v)
    right = (s, vocab_at(v, 1, 0))
    left = (s, vocab_at(v, -1, 0))
    near = (s, vocab_at(v, 0, 1))
    greet([up, down, side, core, right, left, near])

    started = []

    def kv_view(block, p):
        low, count = PIECE_ROWS[p]
        return kv_all.at[block, pl.ds(low, count), :]

    def kv_copy(src, block, p, peer):
        return pltpu.make_async_remote_copy(
            src_ref=src, dst_ref=kv_view(block, p), send_sem=send_sem.at[len(started)],
            recv_sem=kv_sem.at[block, p], device_id=peer, device_id_type=MESH,
        )

    def w_copy(src, shard, p, peer):
        return pltpu.make_async_remote_copy(
            src_ref=src, dst_ref=w_all.at[shard, p], send_sem=send_sem.at[len(started)],
            recv_sem=w_sem.at[shard, p], device_id=peer, device_id_type=MESH,
        )

    def go(copy):
        copy.start()
        started.append(copy)

    def kv_take(dz, dy, p, peers):
        block = seq_at(s, dz, dy, 0)
        kv_copy(kv_view(block, p), block, p, core).wait_recv()
        for peer in peers:
            go(kv_copy(kv_view(block, p), block, p, peer))

    def w_take(dx, dy, p, peers):
        shard = vocab_at(v, dx, dy)
        part = 2 * c + p
        w_copy(w_all.at[shard, part], shard, part, core).wait_recv()
        for peer in peers:
            go(w_copy(w_all.at[shard, part], shard, part, peer))

    own = []
    for p in range(2):
        low, count = PIECE_ROWS[p]
        src = kv_ref.at[pl.ds(low, count), :]
        for peer in (up, down, side, core):
            go(kv_copy(src, s, p, peer))
        part = 2 * c + p
        for peer in (right, left, near):
            go(w_copy(w_ref.at[part], v, part, peer))
    own.append(pltpu.make_async_copy(kv_ref, kv_all.at[s], own_sem.at[0]))
    own.append(pltpu.make_async_copy(w_ref, w_all.at[v], own_sem.at[1]))
    for copy in own:
        copy.start()

    for d in (1, 2):
        for p in range(2):
            kv_take(-d, 0, p, (up, core))
            kv_take(d, 0, p, (down, core))
    for p in range(2):
        w_take(-1, 0, p, (right, core) if p == 0 else (core,))
        w_take(1, 0, p, (left, core) if p == 1 else (core,))
    for p in range(2):
        kv_take(0, 1, p, (up, down, core))
    for p in range(2):
        w_take(0, 1, p, (right, left, core))
    for p in range(2):
        kv_take(-3, 0, p, (up, side, core) if p == 0 else (side, core))
        kv_take(3, 0, p, (down, side, core) if p == 1 else (side, core))
    for p in range(2):
        kv_take(-1, 1, p, (up, core))
        kv_take(1, 1, p, (down, core))
    for p in range(2):
        w_take(2, 0, p, (core,))
    for p in range(2):
        kv_take(4, 0, p, (side, core))
    for p in range(2):
        w_take(-1, 1, p, (right, core) if p == 0 else (core,))
        w_take(1, 1, p, (left, core) if p == 1 else (core,))
    for p in range(2):
        kv_take(-2, 1, p, (core,))
        kv_take(2, 1, p, (core,))
    for p in range(2):
        kv_take(-3, 1, p, (core,))
        kv_take(3, 1, p, (core,))
    for p in range(2):
        w_take(2, 1, p, (core,))
    for p in range(2):
        kv_take(4, 1, p, (core,))

    for dz in range(8):
        for dy in range(2):
            for p in range(2):
                block = seq_at(s, dz, dy, 1)
                kv_copy(kv_view(block, p), block, p, core).wait_recv()
    for dx in range(4):
        for dy in range(2):
            if (dx, dy) != (0, 0):
                for p in range(2):
                    shard = vocab_at(v, dx, dy)
                    part = 2 * (1 - c) + p
                    w_copy(w_all.at[shard, part], shard, part, core).wait_recv()
    for copy in own:
        copy.wait()
    for copy in started:
        copy.wait_send()


SLOTS = 8


def attend_kernel(
    where_ref, base_ref, starts_ref, live_ref, me_ref, q_ref, kv_ref, o_ref,
    buf, sem, q_rows, top, total, acc, scores0, scores1, probs0, probs1, keep0, keep1,
):
    me = me_ref[0]
    all_scores, all_probs, all_keep = (scores0, scores1), (probs0, probs1), (keep0, keep1)
    base0, base1 = base_ref[0], base_ref[256]

    def low_of(position):
        low = starts_ref[0]
        for r in range(1, REQS):
            low = jnp.where(starts_ref[r] <= position, starts_ref[r], low)
        return low

    first0, first1 = low_of(base0) // 256, low_of(base1) // 256
    last0, last1 = low_of(base0 + 255), low_of(base1 + 255)
    count0 = base0 // 256 - first0 + 1
    count1 = base1 // 256 - first1 + 1
    n = count0 + count1

    def key_run(i):
        return jnp.where(i < count0, first0 + i, first1 + i - count0)

    def fetch(i):
        entry = where_ref[key_run(i)]
        slot = i % SLOTS
        return pltpu.make_async_copy(
            kv_ref.at[entry // 2, pl.ds((entry % 2) * 256, 256), :], buf.at[slot], sem.at[slot]
        )

    for i in range(SLOTS - 2):

        @pl.when(i < n)
        def _():
            fetch(i).start()

    for r in range(2):
        for h in range(2):
            q_rows[r, pl.ds(h * 256, 256), :] = q_ref[
                pl.ds(r * 256, 256), pl.ds(h * 128, 128)
            ]
    top[...] = jnp.full_like(top, neg_fill)
    total[...] = jnp.zeros_like(total)
    acc[...] = jnp.zeros_like(acc)
    buf[SLOTS - 1] = jnp.zeros((256, 256), BF16)
    probs1[...] = jnp.zeros_like(probs1)
    keep1[...] = jnp.ones_like(keep1)

    def half(i):
        return jnp.where(i < count0, 0, 1)

    def score(i, into):
        into[...] = lax.dot_general(
            buf[i % SLOTS, :, 0:128], q_rows[half(i)],
            (((1,), (1,)), ((), ())), preferred_element_type=F32,
        )

    def collect(i, parity):
        r = half(i)
        added = lax.dot_general(
            buf[(i + SLOTS) % SLOTS, :, 128:256], all_probs[parity][...],
            (((0,), (0,)), ((), ())), preferred_element_type=F32,
        )
        acc[r] = acc[r] * all_keep[parity][...] + added

    def weigh(i, parity, masked, base):
        r = half(i)
        scores = all_scores[parity][...]
        if masked:
            lane = lax.broadcasted_iota(jnp.int32, (1, 512), 1)
            q_pos = base + (lane % 256)
            low = jnp.full((1, 512), starts_ref[0], jnp.int32)
            for req in range(1, REQS):
                low = jnp.where(starts_ref[req] <= q_pos, starts_ref[req], low)
            k_pos = key_run(i) * 256 + lax.broadcasted_iota(jnp.int32, (256, 512), 0)
            allowed = (k_pos <= q_pos) & (k_pos >= low)
            scores = jnp.where(allowed, scores, neg_fill)
        old = top[r]
        new = jnp.maximum(old, jnp.max(scores, axis=0, keepdims=True))
        probs = jnp.exp2(scores - new)
        if masked:
            probs = jnp.where(allowed, probs, 0.0)
        keep = jnp.exp2(old - new)
        top[r] = new
        total[r] = total[r] * keep + jnp.sum(probs, axis=0, keepdims=True)
        all_keep[parity][...] = keep
        all_probs[parity][...] = probs.astype(BF16)

    def stage(i, parity):
        @pl.when(i + SLOTS - 2 < n)
        def _():
            fetch(i + SLOTS - 2).start()

        @pl.when(i + 1 < n)
        def _():
            fetch(i + 1).wait()

        run = key_run(i)
        base = jnp.where(i < count0, base0, base1)
        last_low = jnp.where(i < count0, last0, last1)
        live = live_ref[(me - where_ref[run] // 2 + 32) % 32] > 0
        whole = (run * 256 < base) & (run * 256 >= last_low)

        @pl.when(live & whole)
        def _():
            score(i + 1, all_scores[1 - parity])
            collect(i - 1, 1 - parity)
            weigh(i, parity, False, base)

        @pl.when(live & jnp.logical_not(whole))
        def _():
            score(i + 1, all_scores[1 - parity])
            collect(i - 1, 1 - parity)
            weigh(i, parity, True, base)

        @pl.when(jnp.logical_not(live))
        def _():
            score(i + 1, all_scores[1 - parity])
            collect(i - 1, 1 - parity)
            all_keep[parity][...] = jnp.ones((1, 512), F32)
            all_probs[parity][...] = jnp.zeros((256, 512), BF16)

    def pair(k, carry):
        stage(2 * k, 0)

        @pl.when(2 * k + 1 < n)
        def _():
            stage(2 * k + 1, 1)

        return carry

    fetch(0).wait()
    score(0, scores0)
    lax.fori_loop(0, (n + 1) // 2, pair, 0)

    @pl.when(n % 2 == 1)
    def _():
        collect(n - 1, 0)

    @pl.when(n % 2 == 0)
    def _():
        collect(n - 1, 1)

    for r in range(2):
        done = acc[r] / total[r]
        for h in range(2):
            o_ref[pl.ds(r * 256, 256), pl.ds(h * 128, 128)] = jnp.transpose(
                done[:, h * 256 : (h + 1) * 256]
            ).astype(BF16)


def middle_kernel(
    heads_ref, w_ref, tok_ref, gain_ref, wg_ref, wu_ref, wd_ref, match_ref, final_ref, head_ref,
    out_ref, rms_ref, top_ref,
    heads, w, tok_rows, tok_cols, wg, wu, wd, att, att_send, att_cols, normed, act, part, got,
    head, row_send, seq_got, wide_send, wide_got, last_send, last_got, max_send, seq_max, vocab_max,
    load_sem, send_sem, head_recv, norm_recv, att_recv, part_recv,
    row_recv, wide_recv, last_recv, max_recv, top_recv,
):
    s = lax.axis_index("seq")
    v = lax.axis_index("vocab")
    others = [(v + r) % 8 for r in range(1, 8)]
    seqs = [(s + r) % 32 for r in range(1, 32)]
    cols = pl.ds(pl.multiple_of(v * 256, 256), 256)
    rows = pl.ds(pl.multiple_of(v * 64, 64), 64)
    loads = [
        pltpu.make_async_copy(w_ref, w, load_sem.at[0]),
        pltpu.make_async_copy(tok_ref.at[rows, :], tok_rows, load_sem.at[1]),
        pltpu.make_async_copy(tok_ref.at[:, cols], tok_cols, load_sem.at[2]),
        pltpu.make_async_copy(wg_ref, wg, load_sem.at[3]),
        pltpu.make_async_copy(wu_ref, wu, load_sem.at[4]),
        pltpu.make_async_copy(wd_ref, wd, load_sem.at[5]),
        pltpu.make_async_copy(heads_ref.at[rows, :], heads.at[v], load_sem.at[6]),
        pltpu.make_async_copy(head_ref, head, load_sem.at[8]),
    ]
    for copy in loads:
        copy.start()
    greet([(s, other) for other in others] + [(other, v) for other in seqs])
    sent = []

    def go(src, dst, recv, peer):
        copy = pltpu.make_async_remote_copy(
            src_ref=src, dst_ref=dst, send_sem=send_sem.at[len(sent)], recv_sem=recv,
            device_id=peer, device_id_type=MESH,
        )
        copy.start()
        sent.append(copy)

    def take(dst, recv):
        pltpu.make_async_remote_copy(
            src_ref=dst, dst_ref=dst, send_sem=send_sem.at[0], recv_sem=recv,
            device_id=(s, others[0]), device_id_type=MESH,
        ).wait_recv()

    for other in others:
        src = heads_ref.at[pl.ds(pl.multiple_of(other * 64, 64), 64), :]
        go(src, heads.at[v], head_recv.at[v], (s, other))
    for other in others:
        take(heads.at[other], head_recv.at[other])
    for i in (0, 1, 6):
        loads[i].wait()

    def project(j, square):
        wide = pl.ds(pl.multiple_of(j * 512, 512), 512)
        total = jnp.dot(heads[0], w[0:256, wide], preferred_element_type=F32)
        for k in range(1, 8):
            total += jnp.dot(
                heads[k], w[k * 256 : (k + 1) * 256, wide], preferred_element_type=F32
            )
        att_send[2 * j] = total[:, 0:256].astype(BF16)
        att_send[2 * j + 1] = total[:, 256:512].astype(BF16)
        residual = tok_rows[:, wide].astype(F32) + total
        att[:, wide] = residual
        return square + jnp.sum(residual * residual, axis=-1, keepdims=True)

    square = lax.fori_loop(0, 4, project, jnp.zeros((64, 1), F32))
    gain = gain_ref[...].astype(F32)
    mine = (att[...] * lax.rsqrt(square / 2048 + epsilon) * gain).astype(BF16)
    normed[2 * v] = mine[0:32]
    normed[2 * v + 1] = mine[32:64]

    right, left, near = vocab_at(v, 1, 0), vocab_at(v, -1, 0), vocab_at(v, 0, 1)

    def pass_on(owner, p, other):
        view = normed.at[2 * owner + p]
        go(view, view, norm_recv.at[owner, p], (s, other))

    def arrive(dx, dy, p, peers):
        owner = vocab_at(v, dx, dy)
        take(normed.at[2 * owner + p], norm_recv.at[owner, p])
        for peer in peers:
            pass_on(owner, p, peer)

    for other in others:
        go(att_send.at[other], att_cols.at[v], att_recv.at[v], (s, other))
    for p in range(2):
        for peer in (right, left, near):
            pass_on(v, p, peer)
    own_cols = pltpu.make_async_copy(att_send.at[v], att_cols.at[v], load_sem.at[7])
    own_cols.start()

    loads[2].wait()
    own_cols.wait()
    for other in others:
        take(att_cols.at[other], att_recv.at[other])
    picked = jnp.zeros((8, 256), F32)
    for i in range(8):
        residual = tok_cols[i * 64 : (i + 1) * 64, :].astype(F32) + att_cols[i].astype(F32)
        high = residual.astype(BF16)
        low = (residual - high.astype(F32)).astype(BF16)
        picked += jnp.dot(match_ref[i], high, preferred_element_type=F32)
        picked += jnp.dot(match_ref[i], low, preferred_element_type=F32)
    row_send[...] = picked
    seq_got[s] = picked
    for other in seqs:
        go(row_send, seq_got.at[s], row_recv.at[s], (other, v))

    for p in range(2):
        arrive(-1, 0, p, (right,) if p == 0 else ())
        arrive(1, 0, p, (left,) if p == 1 else ())
        arrive(0, 1, p, (right, left))

    for other in seqs:
        take(seq_got.at[other], row_recv.at[other])
    picked = jnp.sum(seq_got[...], axis=0)
    wide_send[...] = picked
    wide_got[v] = picked
    for other in others:
        go(wide_send, wide_got.at[v], wide_recv.at[v], (s, other))

    for p in range(2):
        arrive(-1, 1, p, (right,) if p == 0 else ())
        arrive(1, 1, p, (left,) if p == 1 else ())
    for p in range(2):
        arrive(2, 0, p, ())
        arrive(2, 1, p, ())

    for other in others:
        take(wide_got.at[other], wide_recv.at[other])
    square = jnp.zeros((8, 1), F32)
    for k in range(8):
        square += jnp.sum(wide_got[k] * wide_got[k], axis=-1, keepdims=True)
    inverse = lax.rsqrt(square / 2048 + epsilon)
    normed[16, 16:32, :] = jnp.zeros((16, 2048), BF16)
    for k in range(8):
        one = wide_got[k] * inverse * gain[:, k * 256 : (k + 1) * 256]
        normed[16, 0:16, k * 256 : (k + 1) * 256] = jnp.concatenate([one, one], axis=0).astype(BF16)
    for i in (3, 4, 5):
        loads[i].wait()

    def feed(x):
        gate = jnp.dot(x, wg[...], preferred_element_type=F32)
        upward = jnp.dot(x, wu[...], preferred_element_type=F32)
        return (gate / (1.0 + jnp.exp(-gate)) * upward).astype(BF16)

    act[384:544, :] = feed(normed[12:17].reshape(160, 2048))

    group = lax.broadcasted_iota(jnp.int32, (16, 512), 0) // 4

    def packed(quarter):
        out = quarter(0)
        for q in range(1, 4):
            out = jnp.where(group == q, quarter(q), out)
        return out

    last = act[512:528, :]
    mine = packed(
        lambda q: jnp.dot(
            last, wd[:, q * 512 : (q + 1) * 512], preferred_element_type=F32
        )
    ).astype(BF16)
    last_send[...] = mine
    last_got[v] = mine
    for other in others:
        go(last_send, last_got.at[v], last_recv.at[v], (s, other))

    def feed_step(i, carry):
        act[pl.ds(pl.multiple_of(i * 128, 128), 128), :] = feed(
            normed[pl.ds(4 * i, 4)].reshape(128, 2048)
        )
        return carry

    lax.fori_loop(0, 3, feed_step, 0)

    def lower(other):
        wide = pl.ds(pl.multiple_of(other * 256, 256), 256)
        return jnp.dot(act[0:512, :], wd[:, wide], preferred_element_type=F32).astype(BF16)

    for i, other in enumerate(others):
        part[i] = lower(other)
        go(part.at[i], got.at[v], part_recv.at[v], (s, other))
    got[v] = lower(v)

    for other in others:
        take(last_got.at[other], last_recv.at[other])

    def quarter_rows(q):
        one = jnp.concatenate([wide_got[2 * q], wide_got[2 * q + 1]], axis=1)
        return jnp.concatenate([one, one], axis=0)

    total = last_got[0].astype(F32)
    for k in range(1, 8):
        total += last_got[k].astype(F32)
    final = (packed(quarter_rows) + total).astype(BF16).astype(F32)
    square = jnp.broadcast_to(jnp.sum(final * final, axis=-1, keepdims=True), (16, 128))
    square = square + pltpu.roll(square, 8, axis=0)
    square = square + pltpu.roll(square, 4, axis=0)
    mean_square = square / 2048 + epsilon
    diagonal = lax.broadcasted_iota(jnp.int32, (16, 128), 0) == lax.broadcasted_iota(
        jnp.int32, (16, 128), 1
    )

    def along_lanes(value):
        return jnp.sum(jnp.where(diagonal, value, 0.0), axis=0, keepdims=True)

    rms_ref[...] = along_lanes(jnp.sqrt(mean_square))[:, :REQS]
    inverse = lax.rsqrt(mean_square)[:, 0:1]
    spread = packed(
        lambda q: jnp.broadcast_to(
            final_ref[:, q * 512 : (q + 1) * 512].astype(F32), (16, 512)
        )
    )
    final = final * inverse * spread
    loads[7].wait()
    logits = jnp.zeros((16, 360), F32)
    for q in range(4):
        turned = final if q == 0 else pltpu.roll(final, 16 - 4 * q, axis=0)
        logits += lax.dot_general(
            turned.astype(BF16), head[:, q * 512 : (q + 1) * 512], (((1,), (1,)), ((), ())),
            preferred_element_type=F32,
        )
    best = along_lanes(jnp.broadcast_to(jnp.max(logits, axis=-1, keepdims=True), (16, 128)))
    best = jnp.broadcast_to(best, (8, 128))
    max_send[0] = best
    seq_max[s] = best
    for other in seqs:
        go(max_send.at[0], seq_max.at[s], max_recv.at[s], (other, v))
    for other in seqs:
        take(seq_max.at[other], max_recv.at[other])
    best = jnp.max(seq_max[...], axis=0)
    max_send[1] = best
    vocab_max[v] = best
    for other in others:
        go(max_send.at[1], vocab_max.at[v], top_recv.at[v], (s, other))

    for other in others:
        take(got.at[other], part_recv.at[other])

    def finish(i, carry):
        chunk = pl.ds(pl.multiple_of(i * 64, 64), 64)
        residual = tok_cols[chunk, :].astype(F32) + att_cols[i].astype(F32)
        total = got[0, chunk, :].astype(F32)
        for k in range(1, 8):
            total += got[k, chunk, :].astype(F32)
        out_ref[chunk, :] = (residual + total).astype(BF16)
        return carry

    lax.fori_loop(0, 8, finish, 0)
    for other in others:
        take(vocab_max.at[other], top_recv.at[other])
    top_ref[...] = jnp.max(vocab_max[...], axis=0)[0:1, :REQS]
    for copy in sent:
        copy.wait_send()


def per_device(
    tokens,
    attention_gain,
    query_weight,
    key_weight,
    value_weight,
    out_weight,
    forward_gain,
    gate_weight,
    up_weight,
    down_weight,
    final_gain,
    head_weight,
    segment_ids,
    token_order,
    live_blocks,
    cache_slots,
):
    shape = jax.ShapeDtypeStruct
    me = lax.axis_index("seq").astype(jnp.int32)
    request = jnp.arange(8, dtype=jnp.int32)
    starts = jnp.sum((segment_ids[None, :] < request[:, None]).astype(jnp.int32), axis=1)
    begins = jnp.where(starts[None, :REQS] <= token_order[:, None], starts[None, :REQS], 0)
    position = token_order - jnp.max(begins, axis=1)
    lane = jnp.arange(128, dtype=jnp.int32)
    inverse = rope_base ** (-(lane % 64).astype(F32) * 2.0 / 128)
    angle = position.astype(F32)[:, None] * inverse[None, :]
    cos = jnp.cos(angle)
    sin = jnp.where(lane < 64, -1.0, 1.0)[None, :] * jnp.sin(angle)

    query, kv, cache = pl.pallas_call(
        project_kernel,
        out_shape=(shape((512, 256), BF16), shape((528, 256), BF16), shape((512, 256), BF16)),
        in_specs=[SM] + [VM] * 8,
        out_specs=(VM, VM, VM),
        compiler_params=params(),
        name="project",
    )(
        token_order, tokens, attention_gain[None], query_weight, key_weight, value_weight, cos, sin,
        cache_slots[None],
    )

    kv_all, w_all = pl.pallas_call(
        gather_kernel,
        out_shape=(shape((32, 528, 256), BF16), shape((8, 4, 64, 2048), BF16)),
        in_specs=[VM, HB],
        out_specs=(HB, HB),
        scratch_shapes=[
            pltpu.SemaphoreType.DMA((2,)),
            pltpu.SemaphoreType.DMA((128,)),
            pltpu.SemaphoreType.DMA((32, 2)),
            pltpu.SemaphoreType.DMA((8, 4)),
        ],
        compiler_params=params(0),
        name="gather",
    )(kv, out_weight.reshape(4, 64, 2048))

    runs = jnp.stack([kv_all[:, 512, 0], kv_all[:, 512, 128]], axis=1).astype(jnp.int32).reshape(64)
    entry = jnp.arange(64, dtype=jnp.int32)
    where = jnp.sum(jnp.where(runs[None, :] == entry[:, None], entry[None, :], 0), axis=1)
    heads = pl.pallas_call(
        attend_kernel,
        out_shape=shape((512, 256), BF16),
        in_specs=[SM, SM, SM, SM, SM, VM, HB],
        out_specs=VM,
        scratch_shapes=[
            pltpu.VMEM((SLOTS, 256, 256), BF16),
            pltpu.SemaphoreType.DMA((SLOTS,)),
            pltpu.VMEM((2, 512, 128), BF16),
            pltpu.VMEM((2, 1, 512), F32),
            pltpu.VMEM((2, 1, 512), F32),
            pltpu.VMEM((2, 128, 512), F32),
            pltpu.VMEM((256, 512), F32),
            pltpu.VMEM((256, 512), F32),
            pltpu.VMEM((256, 512), BF16),
            pltpu.VMEM((256, 512), BF16),
            pltpu.VMEM((1, 512), F32),
            pltpu.VMEM((1, 512), F32),
        ],
        compiler_params=params(),
        name="attend",
    )(where, token_order, starts, live_blocks[0], me[None], query, kv_all)

    ends = jnp.concatenate([starts[1:REQS], jnp.full((1,), segment_ids.shape[0], jnp.int32)])
    last_index = jnp.concatenate([ends - 1, ends - 1])
    match = (token_order.reshape(8, 1, 64) == last_index[None, :, None]).astype(BF16)
    dma = pltpu.SemaphoreType.DMA
    hidden, rms, top = pl.pallas_call(
        middle_kernel,
        out_shape=(shape((512, 256), BF16), shape((1, REQS), F32), shape((1, REQS), F32)),
        in_specs=[VM, HB, HB, VM, HB, HB, HB, VM, VM, HB],
        out_specs=(VM, VM, VM),
        scratch_shapes=[
            pltpu.VMEM((8, 64, 256), BF16),
            pltpu.VMEM((2048, 2048), BF16),
            pltpu.VMEM((64, 2048), BF16),
            pltpu.VMEM((512, 256), BF16),
            pltpu.VMEM((2048, 512), BF16),
            pltpu.VMEM((2048, 512), BF16),
            pltpu.VMEM((512, 2048), BF16),
            pltpu.VMEM((64, 2048), F32),
            pltpu.VMEM((8, 64, 256), BF16),
            pltpu.VMEM((8, 64, 256), BF16),
            pltpu.VMEM((17, 32, 2048), BF16),
            pltpu.VMEM((544, 512), BF16),
            pltpu.VMEM((7, 512, 256), BF16),
            pltpu.VMEM((8, 512, 256), BF16),
            pltpu.VMEM((360, 2048), BF16),
            pltpu.VMEM((8, 256), F32),
            pltpu.VMEM((32, 8, 256), F32),
            pltpu.VMEM((8, 256), F32),
            pltpu.VMEM((8, 8, 256), F32),
            pltpu.VMEM((16, 512), BF16),
            pltpu.VMEM((8, 16, 512), BF16),
            pltpu.VMEM((2, 8, 128), F32),
            pltpu.VMEM((32, 8, 128), F32),
            pltpu.VMEM((8, 8, 128), F32),
            dma((9,)), dma((128,)), dma((8,)), dma((8, 2)), dma((8,)), dma((8,)),
            dma((32,)), dma((8,)), dma((8,)), dma((32,)), dma((8,)),
        ],
        compiler_params=params(1),
        name="middle",
    )(
        heads, w_all.reshape(2048, 2048), tokens, forward_gain[None], gate_weight, up_weight,
        down_weight, match, final_gain[None], head_weight,
    )
    return (hidden, cache.reshape(512, 2, 128), rms.reshape(REQS), top.reshape(REQS))


def solution(mesh):
    return jax.shard_map(
        per_device,
        mesh=mesh,
        in_specs=(
            P("seq", None),
            P(),
            P(None, "vocab"),
            P(None, "vocab"),
            P(None, "vocab"),
            P("vocab", None),
            P(),
            P(None, "vocab"),
            P(None, "vocab"),
            P("vocab", None),
            P(),
            P(("seq", "vocab"), None),
            P(),
            P("seq"),
            P("seq", None),
            P("seq"),
        ),
        out_specs=(P("seq", "vocab"), P("seq", None, "vocab"), P(), P()),
        check_vma=False,
    )
```

```python
import functools

import jax
import jax.numpy as jnp
from jax import lax
from jax.experimental import pallas as pl
from jax.experimental.pallas import tpu as pltpu
from jax.sharding import PartitionSpec as P

MESH = pl.DeviceIdType.MESH
HD = 128
REQS = 4
epsilon = 1e-06
rope_base = 1000000.0
neg_fill = -1e30
VM = pl.BlockSpec(memory_space=pltpu.VMEM)
SM = pl.BlockSpec(memory_space=pltpu.SMEM)
HB = pl.BlockSpec(memory_space=pl.ANY)
F32 = jnp.float32
BF16 = jnp.bfloat16
LIMIT = 62 * 1024 * 1024
SCALE = HD ** (-0.5) * 1.4426950408889634


def params(cid=None):
    if cid is None:
        return pltpu.CompilerParams(vmem_limit_bytes=LIMIT)
    return pltpu.CompilerParams(
        collective_id=cid, has_side_effects=True, vmem_limit_bytes=LIMIT
    )


def seq_at(s, dz, dy, dc):
    z, y, c = s // 4, (s // 2) % 2, s % 2
    return ((z + dz + 8) % 8) * 4 + ((y + dy) % 2) * 2 + (c + dc) % 2


def vocab_at(v, dx, dy):
    x, y = v // 2, v % 2
    return ((x + dx + 4) % 4) * 2 + (y + dy) % 2


def greet(peers):
    barrier = pltpu.get_barrier_semaphore()
    for peer in peers:
        pl.semaphore_signal(barrier, inc=1, device_id=peer, device_id_type=MESH)
    pl.semaphore_wait(barrier, len(peers))


def project_kernel(
    base_ref, tok_ref, gain_ref, wq_ref, wk_ref, wv_ref, cos_ref, sin_ref, slot_ref,
    q_ref, kv_ref, cache_ref,
):
    gain = gain_ref[...].astype(F32)

    def rows_step(i, carry):
        rows = pl.ds(pl.multiple_of(i * 128, 128), 128)
        x = tok_ref[rows, :].astype(F32)
        scale = lax.rsqrt(jnp.mean(x * x, axis=-1, keepdims=True) + epsilon)
        normed = (x * scale * gain).astype(BF16)
        cos = cos_ref[rows, :]
        sin = sin_ref[rows, :]

        def turn(u):
            return u * cos + pltpu.roll(u, 64, axis=1) * sin

        q = jnp.dot(normed, wq_ref[...], preferred_element_type=F32)
        q_ref[rows, 0:128] = (turn(q[:, 0:128]) * SCALE).astype(BF16)
        q_ref[rows, 128:256] = (turn(q[:, 128:256]) * SCALE).astype(BF16)
        k = jnp.dot(normed, wk_ref[...], preferred_element_type=F32)
        kv_ref[rows, 0:128] = turn(k).astype(BF16)
        v = jnp.dot(normed, wv_ref[...], preferred_element_type=F32)
        kv_ref[rows, 128:256] = v.astype(BF16)
        return carry

    lax.fori_loop(0, 4, rows_step, 0)
    lane = lax.broadcasted_iota(jnp.int32, (16, 256), 1)
    run = jnp.where(lane < 128, base_ref[0] // 256, base_ref[256] // 256)
    kv_ref[512:528, :] = run.astype(F32).astype(BF16)
    slots = slot_ref[...]

    def cache_step(i, carry):
        row = i * 128 + lax.broadcasted_iota(jnp.int32, (128, 512), 0)
        pick = jnp.where(row == slots, 1.0, 0.0).astype(BF16)
        moved = jnp.dot(pick, kv_ref[0:512, :], preferred_element_type=F32)
        cache_ref[pl.ds(pl.multiple_of(i * 128, 128), 128), :] = moved.astype(BF16)
        return carry

    lax.fori_loop(0, 4, cache_step, 0)


PIECE_ROWS = ((0, 256), (256, 272))


def gather_kernel(kv_ref, w_ref, kv_all, w_all, own_sem, send_sem, kv_sem, w_sem):
    s = lax.axis_index("seq")
    v = lax.axis_index("vocab")
    c = s % 2
    up = (seq_at(s, 1, 0, 0), v)
    down = (seq_at(s, -1, 0, 0), v)
    side = (seq_at(s, 0, 1, 0), v)
    core = (seq_at(s, 0, 0, 1), v)
    right = (s, vocab_at(v, 1, 0))
    left = (s, vocab_at(v, -1, 0))
    near = (s, vocab_at(v, 0, 1))
    greet([up, down, side, core, right, left, near])

    started = []

    def kv_view(block, p):
        low, count = PIECE_ROWS[p]
        return kv_all.at[block, pl.ds(low, count), :]

    def kv_copy(src, block, p, peer):
        return pltpu.make_async_remote_copy(
            src_ref=src, dst_ref=kv_view(block, p), send_sem=send_sem.at[len(started)],
            recv_sem=kv_sem.at[block, p], device_id=peer, device_id_type=MESH,
        )

    def w_copy(src, shard, p, peer):
        return pltpu.make_async_remote_copy(
            src_ref=src, dst_ref=w_all.at[shard, p], send_sem=send_sem.at[len(started)],
            recv_sem=w_sem.at[shard, p], device_id=peer, device_id_type=MESH,
        )

    def go(copy):
        copy.start()
        started.append(copy)

    def kv_take(dz, dy, p, peers):
        block = seq_at(s, dz, dy, 0)
        kv_copy(kv_view(block, p), block, p, core).wait_recv()
        for peer in peers:
            go(kv_copy(kv_view(block, p), block, p, peer))

    def w_take(dx, dy, p, peers):
        shard = vocab_at(v, dx, dy)
        part = 2 * c + p
        w_copy(w_all.at[shard, part], shard, part, core).wait_recv()
        for peer in peers:
            go(w_copy(w_all.at[shard, part], shard, part, peer))

    own = []
    for p in range(2):
        low, count = PIECE_ROWS[p]
        src = kv_ref.at[pl.ds(low, count), :]
        for peer in (up, down, side, core):
            go(kv_copy(src, s, p, peer))
        part = 2 * c + p
        for peer in (right, left, near):
            go(w_copy(w_ref.at[part], v, part, peer))
    own.append(pltpu.make_async_copy(kv_ref, kv_all.at[s], own_sem.at[0]))
    own.append(pltpu.make_async_copy(w_ref, w_all.at[v], own_sem.at[1]))
    for copy in own:
        copy.start()

    for d in (1, 2):
        for p in range(2):
            kv_take(-d, 0, p, (up, core))
            kv_take(d, 0, p, (down, core))
    for p in range(2):
        w_take(-1, 0, p, (right, core) if p == 0 else (core,))
        w_take(1, 0, p, (left, core) if p == 1 else (core,))
    for p in range(2):
        kv_take(0, 1, p, (up, down, core))
    for p in range(2):
        w_take(0, 1, p, (right, left, core))
    for p in range(2):
        kv_take(-3, 0, p, (up, side, core) if p == 0 else (side, core))
        kv_take(3, 0, p, (down, side, core) if p == 1 else (side, core))
    for p in range(2):
        kv_take(-1, 1, p, (up, core))
        kv_take(1, 1, p, (down, core))
    for p in range(2):
        w_take(2, 0, p, (core,))
    for p in range(2):
        kv_take(4, 0, p, (side, core))
    for p in range(2):
        w_take(-1, 1, p, (right, core) if p == 0 else (core,))
        w_take(1, 1, p, (left, core) if p == 1 else (core,))
    for p in range(2):
        kv_take(-2, 1, p, (core,))
        kv_take(2, 1, p, (core,))
    for p in range(2):
        kv_take(-3, 1, p, (core,))
        kv_take(3, 1, p, (core,))
    for p in range(2):
        w_take(2, 1, p, (core,))
    for p in range(2):
        kv_take(4, 1, p, (core,))

    for dz in range(8):
        for dy in range(2):
            for p in range(2):
                block = seq_at(s, dz, dy, 1)
                kv_copy(kv_view(block, p), block, p, core).wait_recv()
    for dx in range(4):
        for dy in range(2):
            if (dx, dy) != (0, 0):
                for p in range(2):
                    shard = vocab_at(v, dx, dy)
                    part = 2 * (1 - c) + p
                    w_copy(w_all.at[shard, part], shard, part, core).wait_recv()
    for copy in own:
        copy.wait()
    for copy in started:
        copy.wait_send()


SLOTS = 8


def attend_kernel(
    where_ref, base_ref, starts_ref, live_ref, me_ref, q_ref, kv_ref, o_ref,
    buf, sem, q_rows, top, total, acc, scores0, scores1, probs0, probs1, keep0, keep1,
):
    me = me_ref[0]
    all_scores, all_probs, all_keep = (scores0, scores1), (probs0, probs1), (keep0, keep1)
    base0, base1 = base_ref[0], base_ref[256]

    def low_of(position):
        low = starts_ref[0]
        for r in range(1, REQS):
            low = jnp.where(starts_ref[r] <= position, starts_ref[r], low)
        return low

    first0, first1 = low_of(base0) // 256, low_of(base1) // 256
    last0, last1 = low_of(base0 + 255), low_of(base1 + 255)
    count0 = base0 // 256 - first0 + 1
    count1 = base1 // 256 - first1 + 1
    n = count0 + count1

    def key_run(i):
        return jnp.where(i < count0, first0 + i, first1 + i - count0)

    def fetch(i):
        entry = where_ref[key_run(i)]
        slot = i % SLOTS
        return pltpu.make_async_copy(
            kv_ref.at[entry // 2, pl.ds((entry % 2) * 256, 256), :], buf.at[slot], sem.at[slot]
        )

    for i in range(SLOTS - 2):

        @pl.when(i < n)
        def _():
            fetch(i).start()

    for r in range(2):
        for h in range(2):
            q_rows[r, pl.ds(h * 256, 256), :] = q_ref[
                pl.ds(r * 256, 256), pl.ds(h * 128, 128)
            ]
    top[...] = jnp.full_like(top, neg_fill)
    total[...] = jnp.zeros_like(total)
    acc[...] = jnp.zeros_like(acc)
    buf[SLOTS - 1] = jnp.zeros((256, 256), BF16)
    probs1[...] = jnp.zeros_like(probs1)
    keep1[...] = jnp.ones_like(keep1)

    def half(i):
        return jnp.where(i < count0, 0, 1)

    def score(i, into):
        into[...] = lax.dot_general(
            buf[i % SLOTS, :, 0:128], q_rows[half(i)],
            (((1,), (1,)), ((), ())), preferred_element_type=F32,
        )

    def collect(i, parity):
        r = half(i)
        added = lax.dot_general(
            buf[(i + SLOTS) % SLOTS, :, 128:256], all_probs[parity][...],
            (((0,), (0,)), ((), ())), preferred_element_type=F32,
        )
        acc[r] = acc[r] * all_keep[parity][...] + added

    def weigh(i, parity, masked, base):
        r = half(i)
        scores = all_scores[parity][...]
        if masked:
            lane = lax.broadcasted_iota(jnp.int32, (1, 512), 1)
            q_pos = base + (lane % 256)
            low = jnp.full((1, 512), starts_ref[0], jnp.int32)
            for req in range(1, REQS):
                low = jnp.where(starts_ref[req] <= q_pos, starts_ref[req], low)
            k_pos = key_run(i) * 256 + lax.broadcasted_iota(jnp.int32, (256, 512), 0)
            allowed = (k_pos <= q_pos) & (k_pos >= low)
            scores = jnp.where(allowed, scores, neg_fill)
        old = top[r]
        new = jnp.maximum(old, jnp.max(scores, axis=0, keepdims=True))
        probs = jnp.exp2(scores - new)
        if masked:
            probs = jnp.where(allowed, probs, 0.0)
        keep = jnp.exp2(old - new)
        top[r] = new
        total[r] = total[r] * keep + jnp.sum(probs, axis=0, keepdims=True)
        all_keep[parity][...] = keep
        all_probs[parity][...] = probs.astype(BF16)

    def stage(i, parity):
        @pl.when(i + SLOTS - 2 < n)
        def _():
            fetch(i + SLOTS - 2).start()

        @pl.when(i + 1 < n)
        def _():
            fetch(i + 1).wait()

        run = key_run(i)
        base = jnp.where(i < count0, base0, base1)
        last_low = jnp.where(i < count0, last0, last1)
        live = live_ref[(me - where_ref[run] // 2 + 32) % 32] > 0
        whole = (run * 256 < base) & (run * 256 >= last_low)

        @pl.when(live & whole)
        def _():
            score(i + 1, all_scores[1 - parity])
            collect(i - 1, 1 - parity)
            weigh(i, parity, False, base)

        @pl.when(live & jnp.logical_not(whole))
        def _():
            score(i + 1, all_scores[1 - parity])
            collect(i - 1, 1 - parity)
            weigh(i, parity, True, base)

        @pl.when(jnp.logical_not(live))
        def _():
            score(i + 1, all_scores[1 - parity])
            collect(i - 1, 1 - parity)
            all_keep[parity][...] = jnp.ones((1, 512), F32)
            all_probs[parity][...] = jnp.zeros((256, 512), BF16)

    def pair(k, carry):
        stage(2 * k, 0)

        @pl.when(2 * k + 1 < n)
        def _():
            stage(2 * k + 1, 1)

        return carry

    fetch(0).wait()
    score(0, scores0)
    lax.fori_loop(0, (n + 1) // 2, pair, 0)

    @pl.when(n % 2 == 1)
    def _():
        collect(n - 1, 0)

    @pl.when(n % 2 == 0)
    def _():
        collect(n - 1, 1)

    for r in range(2):
        done = acc[r] / total[r]
        for h in range(2):
            o_ref[pl.ds(r * 256, 256), pl.ds(h * 128, 128)] = jnp.transpose(
                done[:, h * 256 : (h + 1) * 256]
            ).astype(BF16)


def middle_kernel(
    heads_ref, w_ref, tok_ref, gain_ref, wg_ref, wu_ref, wd_ref, match_ref, final_ref, head_ref,
    out_ref, rms_ref, top_ref,
    heads, w, tok_rows, tok_cols, wg, wu, wd, att, att_send, att_cols, normed, act, part, fwd_in,
    x_in, y_in, head, row_send, seq_got, wide_send, wide_got, last_send, last_got, max_send, seq_max, vocab_max,
    load_sem, send_sem, head_recv, norm_recv, att_recv, fwd_recv, x_recv, y_recv,
    row_recv, wide_recv, last_recv, max_recv, top_recv,
):
    s = lax.axis_index("seq")
    v = lax.axis_index("vocab")
    others = [(v + r) % 8 for r in range(1, 8)]
    seqs = [(s + r) % 32 for r in range(1, 32)]
    cols = pl.ds(pl.multiple_of(v * 256, 256), 256)
    rows = pl.ds(pl.multiple_of(v * 64, 64), 64)
    loads = [
        pltpu.make_async_copy(w_ref, w, load_sem.at[0]),
        pltpu.make_async_copy(tok_ref.at[rows, :], tok_rows, load_sem.at[1]),
        pltpu.make_async_copy(tok_ref.at[:, cols], tok_cols, load_sem.at[2]),
        pltpu.make_async_copy(wg_ref, wg, load_sem.at[3]),
        pltpu.make_async_copy(wu_ref, wu, load_sem.at[4]),
        pltpu.make_async_copy(wd_ref, wd, load_sem.at[5]),
        pltpu.make_async_copy(heads_ref.at[rows, :], heads.at[v], load_sem.at[6]),
        pltpu.make_async_copy(head_ref, head, load_sem.at[8]),
    ]
    for copy in loads:
        copy.start()
    greet([(s, other) for other in others] + [(other, v) for other in seqs])
    sent = []

    def go(src, dst, recv, peer):
        copy = pltpu.make_async_remote_copy(
            src_ref=src, dst_ref=dst, send_sem=send_sem.at[len(sent)], recv_sem=recv,
            device_id=peer, device_id_type=MESH,
        )
        copy.start()
        sent.append(copy)

    def take(dst, recv):
        pltpu.make_async_remote_copy(
            src_ref=dst, dst_ref=dst, send_sem=send_sem.at[0], recv_sem=recv,
            device_id=(s, others[0]), device_id_type=MESH,
        ).wait_recv()

    for other in others:
        src = heads_ref.at[pl.ds(pl.multiple_of(other * 64, 64), 64), :]
        go(src, heads.at[v], head_recv.at[v], (s, other))
    for other in others:
        take(heads.at[other], head_recv.at[other])
    for i in (0, 1, 6):
        loads[i].wait()

    def project(j, square):
        wide = pl.ds(pl.multiple_of(j * 512, 512), 512)
        total = jnp.dot(heads[0], w[0:256, wide], preferred_element_type=F32)
        for k in range(1, 8):
            total += jnp.dot(
                heads[k], w[k * 256 : (k + 1) * 256, wide], preferred_element_type=F32
            )
        att_send[2 * j] = total[:, 0:256].astype(BF16)
        att_send[2 * j + 1] = total[:, 256:512].astype(BF16)
        residual = tok_rows[:, wide].astype(F32) + total
        att[:, wide] = residual
        return square + jnp.sum(residual * residual, axis=-1, keepdims=True)

    square = lax.fori_loop(0, 4, project, jnp.zeros((64, 1), F32))
    gain = gain_ref[...].astype(F32)
    mine = (att[...] * lax.rsqrt(square / 2048 + epsilon) * gain).astype(BF16)
    normed[2 * v] = mine[0:32]
    normed[2 * v + 1] = mine[32:64]

    right, left, near = vocab_at(v, 1, 0), vocab_at(v, -1, 0), vocab_at(v, 0, 1)

    def pass_on(owner, p, other):
        view = normed.at[2 * owner + p]
        go(view, view, norm_recv.at[owner, p], (s, other))

    def arrive(dx, dy, p, peers):
        owner = vocab_at(v, dx, dy)
        take(normed.at[2 * owner + p], norm_recv.at[owner, p])
        for peer in peers:
            pass_on(owner, p, peer)

    for other in others:
        go(att_send.at[other], att_cols.at[v], att_recv.at[v], (s, other))
    for p in range(2):
        for peer in (right, left, near):
            pass_on(v, p, peer)
    own_cols = pltpu.make_async_copy(att_send.at[v], att_cols.at[v], load_sem.at[7])
    own_cols.start()

    loads[2].wait()
    own_cols.wait()
    for other in others:
        take(att_cols.at[other], att_recv.at[other])
    picked = jnp.zeros((8, 256), F32)
    for i in range(8):
        residual = tok_cols[i * 64 : (i + 1) * 64, :].astype(F32) + att_cols[i].astype(F32)
        high = residual.astype(BF16)
        low = (residual - high.astype(F32)).astype(BF16)
        picked += jnp.dot(match_ref[i], high, preferred_element_type=F32)
        picked += jnp.dot(match_ref[i], low, preferred_element_type=F32)
    row_send[...] = picked
    seq_got[s] = picked
    for other in seqs:
        go(row_send, seq_got.at[s], row_recv.at[s], (other, v))

    for p in range(2):
        arrive(-1, 0, p, (right,) if p == 0 else ())
        arrive(1, 0, p, (left,) if p == 1 else ())
        arrive(0, 1, p, (right, left))

    for i in (3, 4, 5):
        loads[i].wait()
    x = v // 2
    y = v % 2

    def feed(values):
        gate = jnp.dot(values, wg[...], preferred_element_type=F32)
        upward = jnp.dot(values, wu[...], preferred_element_type=F32)
        return (gate / (1.0 + jnp.exp(-gate)) * upward).astype(BF16)

    def part_of(chunk, dx, dy):
        return part.at[chunk, vocab_at(v, dx, dy)]

    def at_y(chunk, dx, lane):
        return part.at[chunk, ((x + dx + 4) % 4) * 2 + lane]

    def rows_of(dx, extra):
        chunk = (x + dx + 4) % 4
        values = normed[pl.ds(4 * chunk, 4)].reshape(128, 2048)
        if extra:
            values = jnp.concatenate([values, normed[16]], axis=0)
        active = feed(values)
        if extra:
            act[...] = active[128:144]
            active = active[0:128]
        for t in range(8):
            part[chunk, t] = jnp.dot(
                active, wd[:, t * 256 : (t + 1) * 256], preferred_element_type=F32
            ).astype(BF16)
        go(at_y(chunk, 2, 0), fwd_in.at[chunk, 0], fwd_recv.at[chunk, 0], (s, right))
        go(at_y(chunk, 2, 1), fwd_in.at[chunk, 1], fwd_recv.at[chunk, 1], (s, left))
        go(at_y(chunk, 1, 1), x_in.at[chunk, 0, 1], x_recv.at[chunk, 0, 1], (s, right))
        go(at_y(chunk, -1, 0), x_in.at[chunk, 1, 0], x_recv.at[chunk, 1, 0], (s, left))

    rows_of(0, False)
    for other in seqs:
        take(seq_got.at[other], row_recv.at[other])
    picked = jnp.sum(seq_got[...], axis=0)
    wide_send[...] = picked
    wide_got[v] = picked
    for other in others:
        go(wide_send, wide_got.at[v], wide_recv.at[v], (s, other))

    for p in range(2):
        arrive(-1, 1, p, (right,) if p == 0 else ())
        arrive(1, 1, p, (left,) if p == 1 else ())
    rows_of(-1, False)
    for other in others:
        take(wide_got.at[other], wide_recv.at[other])
    square = jnp.zeros((8, 1), F32)
    for k in range(8):
        square += jnp.sum(wide_got[k] * wide_got[k], axis=-1, keepdims=True)
    inverse = lax.rsqrt(square / 2048 + epsilon)
    normed[16, 16:32, :] = jnp.zeros((16, 2048), BF16)
    for k in range(8):
        one = wide_got[k] * inverse * gain[:, k * 256 : (k + 1) * 256]
        normed[16, 0:16, k * 256 : (k + 1) * 256] = jnp.concatenate([one, one], axis=0).astype(BF16)
    rows_of(1, True)

    group = lax.broadcasted_iota(jnp.int32, (16, 512), 0) // 4

    def packed(quarter):
        out = quarter(0)
        for q in range(1, 4):
            out = jnp.where(group == q, quarter(q), out)
        return out

    last = act[...]
    mine = packed(
        lambda q: jnp.dot(
            last, wd[:, q * 512 : (q + 1) * 512], preferred_element_type=F32
        )
    ).astype(BF16)
    last_send[...] = mine
    last_got[v] = mine
    for other in others:
        go(last_send, last_got.at[v], last_recv.at[v], (s, other))
    for p in range(2):
        arrive(2, 0, p, ())
        arrive(2, 1, p, ())
    rows_of(2, False)

    def add_to(ref, *incoming):
        value = ref[...].astype(F32)
        for one in incoming:
            value += one[...].astype(F32)
        ref[...] = value.astype(BF16)

    def onward(dx, way):
        chunk = (x + dx + 4) % 4
        take(fwd_in.at[chunk, way], fwd_recv.at[chunk, way])
        ref = at_y(chunk, 1 if way == 0 else -1, way)
        add_to(ref, fwd_in.at[chunk, way])
        go(ref, x_in.at[chunk, way, way], x_recv.at[chunk, way, way], (s, right if way == 0 else left))

    for to_right, to_left in ((-1, 1), (2, 0), (0, 2), (1, -1)):
        onward(to_right, 0)
        onward(to_left, 1)

    for other in others:
        take(last_got.at[other], last_recv.at[other])

    def quarter_rows(q):
        one = jnp.concatenate([wide_got[2 * q], wide_got[2 * q + 1]], axis=1)
        return jnp.concatenate([one, one], axis=0)

    total = last_got[0].astype(F32)
    for k in range(1, 8):
        total += last_got[k].astype(F32)
    final = (packed(quarter_rows) + total).astype(BF16).astype(F32)
    square = jnp.broadcast_to(jnp.sum(final * final, axis=-1, keepdims=True), (16, 128))
    square = square + pltpu.roll(square, 8, axis=0)
    square = square + pltpu.roll(square, 4, axis=0)
    mean_square = square / 2048 + epsilon
    diagonal = lax.broadcasted_iota(jnp.int32, (16, 128), 0) == lax.broadcasted_iota(
        jnp.int32, (16, 128), 1
    )

    def along_lanes(value):
        return jnp.sum(jnp.where(diagonal, value, 0.0), axis=0, keepdims=True)

    rms_ref[...] = along_lanes(jnp.sqrt(mean_square))[:, :REQS]
    inverse = lax.rsqrt(mean_square)[:, 0:1]
    spread = packed(
        lambda q: jnp.broadcast_to(
            final_ref[:, q * 512 : (q + 1) * 512].astype(F32), (16, 512)
        )
    )
    final = final * inverse * spread
    loads[7].wait()
    logits = jnp.zeros((16, 360), F32)
    for q in range(4):
        turned = final if q == 0 else pltpu.roll(final, 16 - 4 * q, axis=0)
        logits += lax.dot_general(
            turned.astype(BF16), head[:, q * 512 : (q + 1) * 512], (((1,), (1,)), ((), ())),
            preferred_element_type=F32,
        )
    best = along_lanes(jnp.broadcast_to(jnp.max(logits, axis=-1, keepdims=True), (16, 128)))
    best = jnp.broadcast_to(best, (8, 128))
    max_send[0] = best
    seq_max[s] = best
    for other in seqs:
        go(max_send.at[0], seq_max.at[s], max_recv.at[s], (other, v))
    for dx in (0, -1, 1, 2):
        chunk = (x + dx + 4) % 4
        for way in range(2):
            take(x_in.at[chunk, way, 1 - y], x_recv.at[chunk, way, 1 - y])
        ref = part_of(chunk, 0, 1)
        add_to(ref, x_in.at[chunk, 0, 1 - y], x_in.at[chunk, 1, 1 - y])
        go(ref, y_in.at[chunk], y_recv.at[chunk], (s, near))

    for other in seqs:
        take(seq_max.at[other], max_recv.at[other])
    best = jnp.max(seq_max[...], axis=0)
    max_send[1] = best
    vocab_max[v] = best
    for other in others:
        go(max_send.at[1], vocab_max.at[v], top_recv.at[v], (s, other))

    for dx in (0, -1, 1, 2):
        chunk = (x + dx + 4) % 4
        for way in range(2):
            take(x_in.at[chunk, way, y], x_recv.at[chunk, way, y])
        take(y_in.at[chunk], y_recv.at[chunk])
        rows = pl.ds(pl.multiple_of(chunk * 128, 128), 128)
        total = tok_cols[rows, :].astype(F32)
        total += att_cols[pl.ds(2 * chunk, 2)].reshape(128, 256).astype(F32)
        total += part[chunk, v].astype(F32)
        total += x_in[chunk, 0, y].astype(F32)
        total += x_in[chunk, 1, y].astype(F32)
        total += y_in[chunk].astype(F32)
        out_ref[rows, :] = total.astype(BF16)
    for other in others:
        take(vocab_max.at[other], top_recv.at[other])
    top_ref[...] = jnp.max(vocab_max[...], axis=0)[0:1, :REQS]
    for copy in sent:
        copy.wait_send()


def per_device(
    tokens,
    attention_gain,
    query_weight,
    key_weight,
    value_weight,
    out_weight,
    forward_gain,
    gate_weight,
    up_weight,
    down_weight,
    final_gain,
    head_weight,
    segment_ids,
    token_order,
    live_blocks,
    cache_slots,
):
    shape = jax.ShapeDtypeStruct
    me = lax.axis_index("seq").astype(jnp.int32)
    request = jnp.arange(8, dtype=jnp.int32)
    starts = jnp.sum((segment_ids[None, :] < request[:, None]).astype(jnp.int32), axis=1)
    begins = jnp.where(starts[None, :REQS] <= token_order[:, None], starts[None, :REQS], 0)
    position = token_order - jnp.max(begins, axis=1)
    lane = jnp.arange(128, dtype=jnp.int32)
    inverse = rope_base ** (-(lane % 64).astype(F32) * 2.0 / 128)
    angle = position.astype(F32)[:, None] * inverse[None, :]
    cos = jnp.cos(angle)
    sin = jnp.where(lane < 64, -1.0, 1.0)[None, :] * jnp.sin(angle)

    query, kv, cache = pl.pallas_call(
        project_kernel,
        out_shape=(shape((512, 256), BF16), shape((528, 256), BF16), shape((512, 256), BF16)),
        in_specs=[SM] + [VM] * 8,
        out_specs=(VM, VM, VM),
        compiler_params=params(),
        name="project",
    )(
        token_order, tokens, attention_gain[None], query_weight, key_weight, value_weight, cos, sin,
        cache_slots[None],
    )

    kv_all, w_all = pl.pallas_call(
        gather_kernel,
        out_shape=(shape((32, 528, 256), BF16), shape((8, 4, 64, 2048), BF16)),
        in_specs=[VM, HB],
        out_specs=(HB, HB),
        scratch_shapes=[
            pltpu.SemaphoreType.DMA((2,)),
            pltpu.SemaphoreType.DMA((128,)),
            pltpu.SemaphoreType.DMA((32, 2)),
            pltpu.SemaphoreType.DMA((8, 4)),
        ],
        compiler_params=params(0),
        name="gather",
    )(kv, out_weight.reshape(4, 64, 2048))

    runs = jnp.stack([kv_all[:, 512, 0], kv_all[:, 512, 128]], axis=1).astype(jnp.int32).reshape(64)
    entry = jnp.arange(64, dtype=jnp.int32)
    where = jnp.sum(jnp.where(runs[None, :] == entry[:, None], entry[None, :], 0), axis=1)
    heads = pl.pallas_call(
        attend_kernel,
        out_shape=shape((512, 256), BF16),
        in_specs=[SM, SM, SM, SM, SM, VM, HB],
        out_specs=VM,
        scratch_shapes=[
            pltpu.VMEM((SLOTS, 256, 256), BF16),
            pltpu.SemaphoreType.DMA((SLOTS,)),
            pltpu.VMEM((2, 512, 128), BF16),
            pltpu.VMEM((2, 1, 512), F32),
            pltpu.VMEM((2, 1, 512), F32),
            pltpu.VMEM((2, 128, 512), F32),
            pltpu.VMEM((256, 512), F32),
            pltpu.VMEM((256, 512), F32),
            pltpu.VMEM((256, 512), BF16),
            pltpu.VMEM((256, 512), BF16),
            pltpu.VMEM((1, 512), F32),
            pltpu.VMEM((1, 512), F32),
        ],
        compiler_params=params(),
        name="attend",
    )(where, token_order, starts, live_blocks[0], me[None], query, kv_all)

    ends = jnp.concatenate([starts[1:REQS], jnp.full((1,), segment_ids.shape[0], jnp.int32)])
    last_index = jnp.concatenate([ends - 1, ends - 1])
    match = (token_order.reshape(8, 1, 64) == last_index[None, :, None]).astype(BF16)
    dma = pltpu.SemaphoreType.DMA
    hidden, rms, top = pl.pallas_call(
        middle_kernel,
        out_shape=(shape((512, 256), BF16), shape((1, REQS), F32), shape((1, REQS), F32)),
        in_specs=[VM, HB, HB, VM, HB, HB, HB, VM, VM, HB],
        out_specs=(VM, VM, VM),
        scratch_shapes=[
            pltpu.VMEM((8, 64, 256), BF16),
            pltpu.VMEM((2048, 2048), BF16),
            pltpu.VMEM((64, 2048), BF16),
            pltpu.VMEM((512, 256), BF16),
            pltpu.VMEM((2048, 512), BF16),
            pltpu.VMEM((2048, 512), BF16),
            pltpu.VMEM((512, 2048), BF16),
            pltpu.VMEM((64, 2048), F32),
            pltpu.VMEM((8, 64, 256), BF16),
            pltpu.VMEM((8, 64, 256), BF16),
            pltpu.VMEM((17, 32, 2048), BF16),
            pltpu.VMEM((16, 512), BF16),
            pltpu.VMEM((4, 8, 128, 256), BF16),
            pltpu.VMEM((4, 2, 128, 256), BF16),
            pltpu.VMEM((4, 2, 2, 128, 256), BF16),
            pltpu.VMEM((4, 128, 256), BF16),
            pltpu.VMEM((360, 2048), BF16),
            pltpu.VMEM((8, 256), F32),
            pltpu.VMEM((32, 8, 256), F32),
            pltpu.VMEM((8, 256), F32),
            pltpu.VMEM((8, 8, 256), F32),
            pltpu.VMEM((16, 512), BF16),
            pltpu.VMEM((8, 16, 512), BF16),
            pltpu.VMEM((2, 8, 128), F32),
            pltpu.VMEM((32, 8, 128), F32),
            pltpu.VMEM((8, 8, 128), F32),
            dma((9,)), dma((176,)), dma((8,)), dma((8, 2)), dma((8,)), dma((4, 2)), dma((4, 2, 2)), dma((4,)),
            dma((32,)), dma((8,)), dma((8,)), dma((32,)), dma((8,)),
        ],
        compiler_params=params(1),
        name="middle",
    )(
        heads, w_all.reshape(2048, 2048), tokens, forward_gain[None], gate_weight, up_weight,
        down_weight, match, final_gain[None], head_weight,
    )
    return (hidden, cache.reshape(512, 2, 128), rms.reshape(REQS), top.reshape(REQS))


def solution(mesh):
    return jax.shard_map(
        per_device,
        mesh=mesh,
        in_specs=(
            P("seq", None),
            P(),
            P(None, "vocab"),
            P(None, "vocab"),
            P(None, "vocab"),
            P("vocab", None),
            P(),
            P(None, "vocab"),
            P(None, "vocab"),
            P("vocab", None),
            P(),
            P(("seq", "vocab"), None),
            P(),
            P("seq"),
            P("seq", None),
            P("seq"),
        ),
        out_specs=(P("seq", "vocab"), P("seq", None, "vocab"), P(), P()),
        check_vma=False,
    )
```

```python
import functools

import jax
import jax.numpy as jnp
from jax import lax
from jax.experimental import pallas as pl
from jax.experimental.pallas import tpu as pltpu
from jax.sharding import PartitionSpec as P

MESH = pl.DeviceIdType.MESH
HD = 128
REQS = 4
epsilon = 1e-06
rope_base = 1000000.0
neg_fill = -1e30
VM = pl.BlockSpec(memory_space=pltpu.VMEM)
SM = pl.BlockSpec(memory_space=pltpu.SMEM)
HB = pl.BlockSpec(memory_space=pl.ANY)
F32 = jnp.float32
BF16 = jnp.bfloat16
LIMIT = 62 * 1024 * 1024
SCALE = HD ** (-0.5) * 1.4426950408889634


def params(cid=None):
    if cid is None:
        return pltpu.CompilerParams(vmem_limit_bytes=LIMIT)
    return pltpu.CompilerParams(
        collective_id=cid, has_side_effects=True, vmem_limit_bytes=LIMIT
    )


def seq_at(s, dz, dy, dc):
    z, y, c = s // 4, (s // 2) % 2, s % 2
    return ((z + dz + 8) % 8) * 4 + ((y + dy) % 2) * 2 + (c + dc) % 2


def vocab_at(v, dx, dy):
    x, y = v // 2, v % 2
    return ((x + dx + 4) % 4) * 2 + (y + dy) % 2


def greet(peers):
    barrier = pltpu.get_barrier_semaphore()
    for peer in peers:
        pl.semaphore_signal(barrier, inc=1, device_id=peer, device_id_type=MESH)
    pl.semaphore_wait(barrier, len(peers))


def project_kernel(
    base_ref, tok_ref, gain_ref, wq_ref, wk_ref, wv_ref, cos_ref, sin_ref, slot_ref, live_ref,
    q_ref, kv_ref, cache_ref,
):
    gain = gain_ref[...].astype(F32)

    def rows_step(i, carry):
        rows = pl.ds(pl.multiple_of(i * 128, 128), 128)
        x = tok_ref[rows, :].astype(F32)
        scale = lax.rsqrt(jnp.mean(x * x, axis=-1, keepdims=True) + epsilon)
        normed = (x * scale * gain).astype(BF16)
        cos = cos_ref[rows, :]
        sin = sin_ref[rows, :]

        def turn(u):
            return u * cos + pltpu.roll(u, 64, axis=1) * sin

        q = jnp.dot(normed, wq_ref[...], preferred_element_type=F32)
        q_ref[rows, 0:128] = (turn(q[:, 0:128]) * SCALE).astype(BF16)
        q_ref[rows, 128:256] = (turn(q[:, 128:256]) * SCALE).astype(BF16)
        k = jnp.dot(normed, wk_ref[...], preferred_element_type=F32)
        kv_ref[rows, 0:128] = turn(k).astype(BF16)
        v = jnp.dot(normed, wv_ref[...], preferred_element_type=F32)
        kv_ref[rows, 128:256] = v.astype(BF16)
        return carry

    lax.fori_loop(0, 4, rows_step, 0)
    lane = lax.broadcasted_iota(jnp.int32, (16, 256), 1)
    run = jnp.where(lane < 128, base_ref[0] // 256, base_ref[256] // 256)
    run = run.astype(F32)
    kv_ref[512:528, :] = run.astype(BF16)
    row = lax.broadcasted_iota(jnp.int32, (16, 256), 0)
    q_ref[512:528, :] = jnp.where(row == 1, live_ref[...], run).astype(BF16)
    slots = slot_ref[...]

    def cache_step(i, carry):
        row = i * 128 + lax.broadcasted_iota(jnp.int32, (128, 512), 0)
        pick = jnp.where(row == slots, 1.0, 0.0).astype(BF16)
        moved = jnp.dot(pick, kv_ref[0:512, :], preferred_element_type=F32)
        cache_ref[pl.ds(pl.multiple_of(i * 128, 128), 128), :] = moved.astype(BF16)
        return carry

    lax.fori_loop(0, 4, cache_step, 0)


PIECE_ROWS = ((0, 256), (256, 272))


def gather_kernel(kv_ref, q_ref, w_ref, kv_all, q_all, w_all, own_sem, send_sem, kv_sem, q_sem, w_sem):
    s = lax.axis_index("seq")
    v = lax.axis_index("vocab")
    z, c, x = s // 4, s % 2, v // 2
    up = (seq_at(s, 1, 0, 0), v)
    down = (seq_at(s, -1, 0, 0), v)
    side = (seq_at(s, 0, 1, 0), v)
    core = (seq_at(s, 0, 0, 1), v)
    right = (s, vocab_at(v, 1, 0))
    left = (s, vocab_at(v, -1, 0))
    greet([up, down, side, core, right, left])
    started = []

    def go(src, dst, recv, peer):
        copy = pltpu.make_async_remote_copy(
            src_ref=src, dst_ref=dst, send_sem=send_sem.at[len(started)], recv_sem=recv,
            device_id=peer, device_id_type=MESH,
        )
        copy.start()
        started.append(copy)

    def take(dst, recv):
        pltpu.make_async_remote_copy(
            src_ref=dst, dst_ref=dst, send_sem=send_sem.at[0], recv_sem=recv,
            device_id=core, device_id_type=MESH,
        ).wait_recv()

    def kv_view(block, p):
        low, count = PIECE_ROWS[p]
        return kv_all.at[block, pl.ds(low, count), :]

    def kv_take(dz, p, peers):
        block = ((z + dz + 8) % 8) * 2 + c
        take(kv_view(block, p), kv_sem.at[block, p])
        for peer in peers:
            go(kv_view(block, p), kv_view(block, p), kv_sem.at[block, p], peer)

    def w_take(dx, p, peers):
        shard, piece = (x + dx + 4) % 4, 2 * c + p
        take(w_all.at[shard, piece], w_sem.at[shard, piece])
        for peer in peers:
            go(w_all.at[shard, piece], w_all.at[shard, piece], w_sem.at[shard, piece], peer)

    mine = z * 2 + c
    for p in range(2):
        low, count = PIECE_ROWS[p]
        for peer in (up, down, core):
            go(kv_ref.at[pl.ds(low, count), :], kv_view(mine, p), kv_sem.at[mine, p], peer)
        piece = 2 * c + p
        for peer in (right, left):
            go(w_ref.at[piece], w_all.at[x, piece], w_sem.at[x, piece], peer)
    go(q_ref, q_all, q_sem.at[0], side)
    own = [
        pltpu.make_async_copy(kv_ref, kv_all.at[mine], own_sem.at[0]),
        pltpu.make_async_copy(w_ref, w_all.at[x], own_sem.at[1]),
    ]
    for copy in own:
        copy.start()

    for d in (1, 2):
        for p in range(2):
            kv_take(-d, p, (up, core))
            kv_take(d, p, (down, core))
        if d == 1:
            w_take(-1, 0, (right, core))
            w_take(1, 0, (core,))
    w_take(-1, 1, (core,))
    w_take(1, 1, (left, core))
    for p in range(2):
        kv_take(-3, p, (up, core) if p == 0 else (core,))
        kv_take(3, p, (down, core) if p == 1 else (core,))
    for p in range(2):
        w_take(2, p, (core,))
    for p in range(2):
        kv_take(4, p, (core,))

    for dz in range(8):
        for p in range(2):
            block = ((z + dz) % 8) * 2 + 1 - c
            take(kv_view(block, p), kv_sem.at[block, p])
    for dx in range(1, 4):
        for p in range(2):
            shard, piece = (x + dx) % 4, 2 * (1 - c) + p
            take(w_all.at[shard, piece], w_sem.at[shard, piece])
    take(q_all, q_sem.at[0])
    for copy in own:
        copy.wait()
    for copy in started:
        copy.wait_send()


SLOTS = 8


def attend_kernel(
    runs_ref, tail_ref, base_ref, starts_ref, live_ref, me_ref, q_ref, other_ref, kv_ref, o_ref, st_ref,
    buf, sem, q_rows, top, total, acc, scores0, scores1, probs0, probs1, keep0, keep1,
    table, sorted_run, sorted_entry, before,
):
    me = me_ref[0]
    my_y = (me // 2) % 2
    other = me + 2 - 4 * my_y
    all_scores, all_probs, all_keep = (scores0, scores1), (probs0, probs1), (keep0, keep1)
    q_run = [base_ref[0] // 256, base_ref[256] // 256, tail_ref[0], tail_ref[1]]

    def clear(i, carry):
        table[i] = -1
        return carry

    def enter(i, carry):
        table[runs_ref[i]] = i
        return carry

    def gather_up(i, count):
        before[i] = count
        entry = table[i]

        @pl.when(entry >= 0)
        def _():
            sorted_run[count] = i
            sorted_entry[count] = entry

        return jnp.where(entry >= 0, count + 1, count)

    lax.fori_loop(0, 64, clear, 0)
    lax.fori_loop(0, 32, enter, 0)
    before[64] = lax.fori_loop(0, 64, gather_up, 0)

    def low_of(position):
        low = starts_ref[0]
        for r in range(1, REQS):
            low = jnp.where(starts_ref[r] <= position, starts_ref[r], low)
        return low

    lasts, shifts, offsets = [], [], [0]
    for r in range(4):
        first = before[low_of(q_run[r] * 256) // 256]
        lasts.append(low_of(q_run[r] * 256 + 255))
        shifts.append(first - offsets[-1])
        offsets.append(offsets[-1] + before[q_run[r] + 1] - first)
    n = offsets[4]

    def choose(i, values):
        out = values[0]
        for r in range(1, 4):
            out = jnp.where(i >= offsets[r], values[r], out)
        return out

    def half(i):
        return choose(i, [0, 1, 2, 3])

    def place(i):
        return jnp.clip(i + choose(i, shifts), 0, 31)

    def key_run(i):
        return sorted_run[place(i)]

    def fetch(i):
        entry = sorted_entry[place(i)]
        slot = i % SLOTS
        return pltpu.make_async_copy(
            kv_ref.at[entry // 2, pl.ds((entry % 2) * 256, 256), :], buf.at[slot], sem.at[slot]
        )

    for i in range(SLOTS - 2):

        @pl.when(i < n)
        def _():
            fetch(i).start()

    for r in range(4):
        source = q_ref if r < 2 else other_ref
        for h in range(2):
            q_rows[r, pl.ds(h * 256, 256), :] = source[
                pl.ds((r % 2) * 256, 256), pl.ds(h * 128, 128)
            ]
    top[...] = jnp.full_like(top, neg_fill)
    total[...] = jnp.zeros_like(total)
    acc[...] = jnp.zeros_like(acc)
    buf[SLOTS - 1] = jnp.zeros((256, 256), BF16)
    probs1[...] = jnp.zeros_like(probs1)
    keep1[...] = jnp.ones_like(keep1)

    def score(i, into):
        into[...] = lax.dot_general(
            buf[i % SLOTS, :, 0:128], q_rows[half(i)],
            (((1,), (1,)), ((), ())), preferred_element_type=F32,
        )

    def collect(i, parity):
        r = half(i)
        added = lax.dot_general(
            buf[(i + SLOTS) % SLOTS, :, 128:256], all_probs[parity][...],
            (((0,), (0,)), ((), ())), preferred_element_type=F32,
        )
        acc[r] = acc[r] * all_keep[parity][...] + added

    def weigh(i, parity, masked, base):
        r = half(i)
        scores = all_scores[parity][...]
        if masked:
            lane = lax.broadcasted_iota(jnp.int32, (1, 512), 1)
            q_pos = base + (lane % 256)
            low = jnp.full((1, 512), starts_ref[0], jnp.int32)
            for req in range(1, REQS):
                low = jnp.where(starts_ref[req] <= q_pos, starts_ref[req], low)
            k_pos = key_run(i) * 256 + lax.broadcasted_iota(jnp.int32, (256, 512), 0)
            allowed = (k_pos <= q_pos) & (k_pos >= low)
            scores = jnp.where(allowed, scores, neg_fill)
        old = top[r]
        new = jnp.maximum(old, jnp.max(scores, axis=0, keepdims=True))
        probs = jnp.exp2(scores - new)
        if masked:
            probs = jnp.where(allowed, probs, 0.0)
        keep = jnp.exp2(old - new)
        top[r] = new
        total[r] = total[r] * keep + jnp.sum(probs, axis=0, keepdims=True)
        all_keep[parity][...] = keep
        all_probs[parity][...] = probs.astype(BF16)

    def stage(i, parity):
        @pl.when(i + SLOTS - 2 < n)
        def _():
            fetch(i + SLOTS - 2).start()

        @pl.when(i + 1 < n)
        def _():
            fetch(i + 1).wait()

        run = key_run(i)
        base = choose(i, q_run) * 256
        last_low = choose(i, lasts)
        slot = sorted_entry[place(i)] // 2
        block = (slot // 2) * 4 + my_y * 2 + slot % 2
        live = jnp.where(
            i < offsets[2], live_ref[(me - block + 32) % 32], tail_ref[2 + (other - block + 32) % 32]
        ) > 0
        whole = (run * 256 < base) & (run * 256 >= last_low)

        @pl.when(live & whole)
        def _():
            score(i + 1, all_scores[1 - parity])
            collect(i - 1, 1 - parity)
            weigh(i, parity, False, base)

        @pl.when(live & jnp.logical_not(whole))
        def _():
            score(i + 1, all_scores[1 - parity])
            collect(i - 1, 1 - parity)
            weigh(i, parity, True, base)

        @pl.when(jnp.logical_not(live))
        def _():
            score(i + 1, all_scores[1 - parity])
            collect(i - 1, 1 - parity)
            all_keep[parity][...] = jnp.ones((1, 512), F32)
            all_probs[parity][...] = jnp.zeros((256, 512), BF16)

    def pair(k, carry):
        stage(2 * k, 0)

        @pl.when(2 * k + 1 < n)
        def _():
            stage(2 * k + 1, 1)

        return carry

    fetch(0).wait()
    score(0, scores0)
    lax.fori_loop(0, (n + 1) // 2, pair, 0)

    @pl.when(n % 2 == 1)
    def _():
        collect(n - 1, 0)

    @pl.when(n % 2 == 0)
    def _():
        collect(n - 1, 1)

    for r in range(4):
        weight = total[r]
        done = (acc[r] * jnp.where(weight > 0, 1.0 / weight, 0.0)).astype(BF16)
        for part in range(2):
            k = 2 * (r % 2) + part
            for h in range(2):
                low = h * 256 + part * 128
                o_ref[r // 2, k, h * 128 : (h + 1) * 128, :] = done[:, low : low + 128]
                st_ref[r // 2, k, h : h + 1, :] = top[r, :, low : low + 128]
                st_ref[r // 2, k, 2 + h : 3 + h, :] = weight[:, low : low + 128]


def middle_kernel(
    heads_ref, stats_ref, w_ref, tok_ref, gain_ref, wg_ref, wu_ref, wd_ref, match_ref, final_ref, head_ref,
    out_ref, rms_ref, top_ref,
    heads, stats, joined, near_send, near_got, w, tok_rows, tok_cols, wg, wu, wd, att, att_send, att_cols, normed, act, part, fwd_in,
    x_in, y_in, head, row_send, seq_got, wide_send, wide_got, last_send, last_got, max_send, seq_max, vocab_max,
    load_sem, send_sem, head_recv, stat_recv, near_recv, norm_recv, att_recv, fwd_recv, x_recv, y_recv,
    row_recv, wide_recv, last_recv, max_recv, top_recv,
):
    s = lax.axis_index("seq")
    v = lax.axis_index("vocab")
    others = [(v + r) % 8 for r in range(1, 8)]
    seqs = [(s + r) % 32 for r in range(1, 32)]
    cols = pl.ds(pl.multiple_of(v * 256, 256), 256)
    rows = pl.ds(pl.multiple_of(v * 64, 64), 64)
    loads = [
        pltpu.make_async_copy(w_ref, w, load_sem.at[0]),
        pltpu.make_async_copy(tok_ref.at[rows, :], tok_rows, load_sem.at[1]),
        pltpu.make_async_copy(tok_ref.at[:, cols], tok_cols, load_sem.at[2]),
        pltpu.make_async_copy(wg_ref, wg, load_sem.at[3]),
        pltpu.make_async_copy(wu_ref, wu, load_sem.at[4]),
        pltpu.make_async_copy(wd_ref, wd, load_sem.at[5]),
        pltpu.make_async_copy(heads_ref.at[0, v // 2], heads.at[v // 2, (s // 2) % 2], load_sem.at[6]),
        pltpu.make_async_copy(stats_ref.at[0, v // 2], stats.at[v // 2, (s // 2) % 2], load_sem.at[9]),
        pltpu.make_async_copy(head_ref, head, load_sem.at[8]),
    ]
    for copy in loads:
        copy.start()
    x = v // 2
    y = v % 2
    my_y = (s // 2) % 2
    across = seq_at(s, 0, 1, 0)
    greet(
        [(s, other) for other in others]
        + [(other, v) for other in seqs]
        + [(across, vocab_at(v, dx, 0)) for dx in range(1, 4)]
    )
    sent = []

    def go(src, dst, recv, peer):
        copy = pltpu.make_async_remote_copy(
            src_ref=src, dst_ref=dst, send_sem=send_sem.at[len(sent)], recv_sem=recv,
            device_id=peer, device_id_type=MESH,
        )
        copy.start()
        sent.append(copy)

    def take(dst, recv):
        pltpu.make_async_remote_copy(
            src_ref=dst, dst_ref=dst, send_sem=send_sem.at[0], recv_sem=recv,
            device_id=(s, others[0]), device_id_type=MESH,
        ).wait_recv()

    for dx in (2, 1, 3, 0):
        target = (x + dx) % 4
        for which in (1, 0):
            if (dx, which) != (0, 0):
                peer = (across if which else s, vocab_at(v, dx, 0))
                go(heads_ref.at[which, target], heads.at[x, my_y], head_recv.at[x, my_y], peer)
                go(stats_ref.at[which, target], stats.at[x, my_y], stat_recv.at[x, my_y], peer)
    for i in (0, 1, 6, 7):
        loads[i].wait()
    for dx in range(4):
        source = (x + dx) % 4
        for which in range(2):
            if (dx, which) != (0, 0):
                held = (my_y + which) % 2
                take(heads.at[source, held], head_recv.at[source, held])
                take(stats.at[source, held], stat_recv.at[source, held])
    for k in range(4):
        for h in range(2):
            tops = [stats[k, i, h : h + 1, :] for i in range(2)]
            best = jnp.maximum(tops[0], tops[1])
            weights = [stats[k, i, 2 + h : 3 + h, :] * jnp.exp2(tops[i] - best) for i in range(2)]
            scale = 1.0 / (weights[0] + weights[1])
            span = pl.ds(h * 128, 128)
            joined[k, span, :] = (
                heads[k, 0, span, :].astype(F32) * (weights[0] * scale)
                + heads[k, 1, span, :].astype(F32) * (weights[1] * scale)
            ).astype(BF16)

    near = vocab_at(v, 0, 1)
    for j in range(4):
        total = jnp.zeros((128, 512), F32)
        for k in range(4):
            total += lax.dot_general(
                joined[k], w[k * 256 : (k + 1) * 256, j * 512 : (j + 1) * 512],
                (((0,), (0,)), ((), ())), preferred_element_type=F32,
            )
        att[:, j * 512 : (j + 1) * 512] = jnp.where(y == 0, total[0:64], total[64:128])
        near_send[j] = jnp.where(y == 0, total[64:128], total[0:64]).astype(BF16)
        go(near_send.at[j], near_got.at[j], near_recv.at[j], (s, near))
    for j in range(4):
        take(near_got.at[j], near_recv.at[j])

    def project(j, square):
        wide = pl.ds(pl.multiple_of(j * 512, 512), 512)
        total = att[:, wide] + near_got[j].astype(F32)
        att_send[2 * j] = total[:, 0:256].astype(BF16)
        att_send[2 * j + 1] = total[:, 256:512].astype(BF16)
        residual = tok_rows[:, wide].astype(F32) + total
        att[:, wide] = residual
        return square + jnp.sum(residual * residual, axis=-1, keepdims=True)

    square = lax.fori_loop(0, 4, project, jnp.zeros((64, 1), F32))
    gain = gain_ref[...].astype(F32)
    mine = (att[...] * lax.rsqrt(square / 2048 + epsilon) * gain).astype(BF16)
    normed[2 * v] = mine[0:32]
    normed[2 * v + 1] = mine[32:64]

    right, left = vocab_at(v, 1, 0), vocab_at(v, -1, 0)

    def pass_on(owner, p, other):
        view = normed.at[2 * owner + p]
        go(view, view, norm_recv.at[owner, p], (s, other))

    def arrive(dx, dy, p, peers):
        owner = vocab_at(v, dx, dy)
        take(normed.at[2 * owner + p], norm_recv.at[owner, p])
        for peer in peers:
            pass_on(owner, p, peer)

    for other in others:
        go(att_send.at[other], att_cols.at[v], att_recv.at[v], (s, other))
    for p in range(2):
        for peer in (right, left, near):
            pass_on(v, p, peer)
    own_cols = pltpu.make_async_copy(att_send.at[v], att_cols.at[v], load_sem.at[7])
    own_cols.start()

    loads[2].wait()
    own_cols.wait()
    for other in others:
        take(att_cols.at[other], att_recv.at[other])
    picked = jnp.zeros((8, 256), F32)
    for i in range(8):
        residual = tok_cols[i * 64 : (i + 1) * 64, :].astype(F32) + att_cols[i].astype(F32)
        high = residual.astype(BF16)
        low = (residual - high.astype(F32)).astype(BF16)
        picked += jnp.dot(match_ref[i], high, preferred_element_type=F32)
        picked += jnp.dot(match_ref[i], low, preferred_element_type=F32)
    row_send[...] = picked
    seq_got[s] = picked
    for other in seqs:
        go(row_send, seq_got.at[s], row_recv.at[s], (other, v))

    for p in range(2):
        arrive(-1, 0, p, (right,) if p == 0 else ())
        arrive(1, 0, p, (left,) if p == 1 else ())
        arrive(0, 1, p, (right, left))

    for i in (3, 4, 5):
        loads[i].wait()
    def feed(values):
        gate = jnp.dot(values, wg[...], preferred_element_type=F32)
        upward = jnp.dot(values, wu[...], preferred_element_type=F32)
        return (gate / (1.0 + jnp.exp(-gate)) * upward).astype(BF16)

    def part_of(chunk, dx, dy):
        return part.at[chunk, vocab_at(v, dx, dy)]

    def at_y(chunk, dx, lane):
        return part.at[chunk, ((x + dx + 4) % 4) * 2 + lane]

    def rows_of(dx, extra):
        chunk = (x + dx + 4) % 4
        values = normed[pl.ds(4 * chunk, 4)].reshape(128, 2048)
        if extra:
            values = jnp.concatenate([values, normed[16]], axis=0)
        active = feed(values)
        if extra:
            act[...] = active[128:144]
            active = active[0:128]
        for t in range(8):
            part[chunk, t] = jnp.dot(
                active, wd[:, t * 256 : (t + 1) * 256], preferred_element_type=F32
            ).astype(BF16)
        go(at_y(chunk, 2, 0), fwd_in.at[chunk, 0], fwd_recv.at[chunk, 0], (s, right))
        go(at_y(chunk, 2, 1), fwd_in.at[chunk, 1], fwd_recv.at[chunk, 1], (s, left))
        go(at_y(chunk, 1, 1), x_in.at[chunk, 0, 1], x_recv.at[chunk, 0, 1], (s, right))
        go(at_y(chunk, -1, 0), x_in.at[chunk, 1, 0], x_recv.at[chunk, 1, 0], (s, left))

    rows_of(0, False)
    for other in seqs:
        take(seq_got.at[other], row_recv.at[other])
    picked = jnp.sum(seq_got[...], axis=0)
    wide_send[...] = picked
    wide_got[v] = picked
    for other in others:
        go(wide_send, wide_got.at[v], wide_recv.at[v], (s, other))

    for p in range(2):
        arrive(-1, 1, p, (right,) if p == 0 else ())
        arrive(1, 1, p, (left,) if p == 1 else ())
    rows_of(-1, False)
    for other in others:
        take(wide_got.at[other], wide_recv.at[other])
    square = jnp.zeros((8, 1), F32)
    for k in range(8):
        square += jnp.sum(wide_got[k] * wide_got[k], axis=-1, keepdims=True)
    inverse = lax.rsqrt(square / 2048 + epsilon)
    normed[16, 16:32, :] = jnp.zeros((16, 2048), BF16)
    for k in range(8):
        one = wide_got[k] * inverse * gain[:, k * 256 : (k + 1) * 256]
        normed[16, 0:16, k * 256 : (k + 1) * 256] = jnp.concatenate([one, one], axis=0).astype(BF16)
    rows_of(1, True)

    group = lax.broadcasted_iota(jnp.int32, (16, 512), 0) // 4

    def packed(quarter):
        out = quarter(0)
        for q in range(1, 4):
            out = jnp.where(group == q, quarter(q), out)
        return out

    last = act[...]
    mine = packed(
        lambda q: jnp.dot(
            last, wd[:, q * 512 : (q + 1) * 512], preferred_element_type=F32
        )
    ).astype(BF16)
    last_send[...] = mine
    last_got[v] = mine
    for other in others:
        go(last_send, last_got.at[v], last_recv.at[v], (s, other))
    for p in range(2):
        arrive(2, 0, p, ())
        arrive(2, 1, p, ())
    rows_of(2, False)

    def add_to(ref, *incoming):
        value = ref[...].astype(F32)
        for one in incoming:
            value += one[...].astype(F32)
        ref[...] = value.astype(BF16)

    def onward(dx, way):
        chunk = (x + dx + 4) % 4
        take(fwd_in.at[chunk, way], fwd_recv.at[chunk, way])
        ref = at_y(chunk, 1 if way == 0 else -1, way)
        add_to(ref, fwd_in.at[chunk, way])
        go(ref, x_in.at[chunk, way, way], x_recv.at[chunk, way, way], (s, right if way == 0 else left))

    for to_right, to_left in ((-1, 1), (2, 0), (0, 2), (1, -1)):
        onward(to_right, 0)
        onward(to_left, 1)

    for other in others:
        take(last_got.at[other], last_recv.at[other])

    def quarter_rows(q):
        one = jnp.concatenate([wide_got[2 * q], wide_got[2 * q + 1]], axis=1)
        return jnp.concatenate([one, one], axis=0)

    total = last_got[0].astype(F32)
    for k in range(1, 8):
        total += last_got[k].astype(F32)
    final = (packed(quarter_rows) + total).astype(BF16).astype(F32)
    square = jnp.broadcast_to(jnp.sum(final * final, axis=-1, keepdims=True), (16, 128))
    square = square + pltpu.roll(square, 8, axis=0)
    square = square + pltpu.roll(square, 4, axis=0)
    mean_square = square / 2048 + epsilon
    diagonal = lax.broadcasted_iota(jnp.int32, (16, 128), 0) == lax.broadcasted_iota(
        jnp.int32, (16, 128), 1
    )

    def along_lanes(value):
        return jnp.sum(jnp.where(diagonal, value, 0.0), axis=0, keepdims=True)

    rms_ref[...] = along_lanes(jnp.sqrt(mean_square))[:, :REQS]
    inverse = lax.rsqrt(mean_square)[:, 0:1]
    spread = packed(
        lambda q: jnp.broadcast_to(
            final_ref[:, q * 512 : (q + 1) * 512].astype(F32), (16, 512)
        )
    )
    final = final * inverse * spread
    loads[8].wait()
    logits = jnp.zeros((16, 360), F32)
    for q in range(4):
        turned = final if q == 0 else pltpu.roll(final, 16 - 4 * q, axis=0)
        logits += lax.dot_general(
            turned.astype(BF16), head[:, q * 512 : (q + 1) * 512], (((1,), (1,)), ((), ())),
            preferred_element_type=F32,
        )
    best = along_lanes(jnp.broadcast_to(jnp.max(logits, axis=-1, keepdims=True), (16, 128)))
    best = jnp.broadcast_to(best, (8, 128))
    max_send[0] = best
    seq_max[s] = best
    for other in seqs:
        go(max_send.at[0], seq_max.at[s], max_recv.at[s], (other, v))
    for dx in (0, -1, 1, 2):
        chunk = (x + dx + 4) % 4
        for way in range(2):
            take(x_in.at[chunk, way, 1 - y], x_recv.at[chunk, way, 1 - y])
        ref = part_of(chunk, 0, 1)
        add_to(ref, x_in.at[chunk, 0, 1 - y], x_in.at[chunk, 1, 1 - y])
        go(ref, y_in.at[chunk], y_recv.at[chunk], (s, near))

    for other in seqs:
        take(seq_max.at[other], max_recv.at[other])
    best = jnp.max(seq_max[...], axis=0)
    max_send[1] = best
    vocab_max[v] = best
    for other in others:
        go(max_send.at[1], vocab_max.at[v], top_recv.at[v], (s, other))

    for dx in (0, -1, 1, 2):
        chunk = (x + dx + 4) % 4
        for way in range(2):
            take(x_in.at[chunk, way, y], x_recv.at[chunk, way, y])
        take(y_in.at[chunk], y_recv.at[chunk])
        rows = pl.ds(pl.multiple_of(chunk * 128, 128), 128)
        total = tok_cols[rows, :].astype(F32)
        total += att_cols[pl.ds(2 * chunk, 2)].reshape(128, 256).astype(F32)
        total += part[chunk, v].astype(F32)
        total += x_in[chunk, 0, y].astype(F32)
        total += x_in[chunk, 1, y].astype(F32)
        total += y_in[chunk].astype(F32)
        out_ref[rows, :] = total.astype(BF16)
    for other in others:
        take(vocab_max.at[other], top_recv.at[other])
    top_ref[...] = jnp.max(vocab_max[...], axis=0)[0:1, :REQS]
    for copy in sent:
        copy.wait_send()


def per_device(
    tokens,
    attention_gain,
    query_weight,
    key_weight,
    value_weight,
    out_weight,
    forward_gain,
    gate_weight,
    up_weight,
    down_weight,
    final_gain,
    head_weight,
    segment_ids,
    token_order,
    live_blocks,
    cache_slots,
):
    shape = jax.ShapeDtypeStruct
    me = lax.axis_index("seq").astype(jnp.int32)
    request = jnp.arange(8, dtype=jnp.int32)
    starts = jnp.sum((segment_ids[None, :] < request[:, None]).astype(jnp.int32), axis=1)
    begins = jnp.where(starts[None, :REQS] <= token_order[:, None], starts[None, :REQS], 0)
    position = token_order - jnp.max(begins, axis=1)
    lane = jnp.arange(128, dtype=jnp.int32)
    inverse = rope_base ** (-(lane % 64).astype(F32) * 2.0 / 128)
    angle = position.astype(F32)[:, None] * inverse[None, :]
    cos = jnp.cos(angle)
    sin = jnp.where(lane < 64, -1.0, 1.0)[None, :] * jnp.sin(angle)

    query, kv, cache = pl.pallas_call(
        project_kernel,
        out_shape=(shape((528, 256), BF16), shape((528, 256), BF16), shape((512, 256), BF16)),
        in_specs=[SM] + [VM] * 9,
        out_specs=(VM, VM, VM),
        compiler_params=params(),
        name="project",
    )(
        token_order, tokens, attention_gain[None], query_weight, key_weight, value_weight, cos, sin,
        cache_slots[None], jnp.pad(live_blocks.astype(F32), ((0, 0), (0, 224))),
    )

    kv_all, q_other, w_all = pl.pallas_call(
        gather_kernel,
        out_shape=(
            shape((16, 528, 256), BF16), shape((528, 256), BF16), shape((4, 4, 64, 2048), BF16),
        ),
        in_specs=[VM, VM, HB],
        out_specs=(HB, HB, HB),
        scratch_shapes=[
            pltpu.SemaphoreType.DMA((2,)),
            pltpu.SemaphoreType.DMA((96,)),
            pltpu.SemaphoreType.DMA((16, 2)),
            pltpu.SemaphoreType.DMA((1,)),
            pltpu.SemaphoreType.DMA((4, 4)),
        ],
        compiler_params=params(0),
        name="gather",
    )(kv, query, out_weight.reshape(4, 64, 2048))

    runs = jnp.stack([kv_all[:, 512, 0], kv_all[:, 512, 128]], axis=1).astype(jnp.int32).reshape(32)
    tail = jnp.concatenate([q_other[512, 0:256:128], q_other[513, 0:32]]).astype(jnp.int32)
    heads, stats = pl.pallas_call(
        attend_kernel,
        out_shape=(shape((2, 4, 256, 128), BF16), shape((2, 4, 8, 128), F32)),
        in_specs=[SM] * 6 + [VM, VM, HB],
        out_specs=(VM, VM),
        scratch_shapes=[
            pltpu.VMEM((SLOTS, 256, 256), BF16),
            pltpu.SemaphoreType.DMA((SLOTS,)),
            pltpu.VMEM((4, 512, 128), BF16),
            pltpu.VMEM((4, 1, 512), F32),
            pltpu.VMEM((4, 1, 512), F32),
            pltpu.VMEM((4, 128, 512), F32),
            pltpu.VMEM((256, 512), F32),
            pltpu.VMEM((256, 512), F32),
            pltpu.VMEM((256, 512), BF16),
            pltpu.VMEM((256, 512), BF16),
            pltpu.VMEM((1, 512), F32),
            pltpu.VMEM((1, 512), F32),
            pltpu.SMEM((64,), jnp.int32),
            pltpu.SMEM((32,), jnp.int32),
            pltpu.SMEM((32,), jnp.int32),
            pltpu.SMEM((65,), jnp.int32),
        ],
        compiler_params=params(),
        name="attend",
    )(runs, tail, token_order, starts, live_blocks[0], me[None], query, q_other, kv_all)

    ends = jnp.concatenate([starts[1:REQS], jnp.full((1,), segment_ids.shape[0], jnp.int32)])
    last_index = jnp.concatenate([ends - 1, ends - 1])
    match = (token_order.reshape(8, 1, 64) == last_index[None, :, None]).astype(BF16)
    dma = pltpu.SemaphoreType.DMA
    hidden, rms, top = pl.pallas_call(
        middle_kernel,
        out_shape=(shape((512, 256), BF16), shape((1, REQS), F32), shape((1, REQS), F32)),
        in_specs=[VM, VM, HB, HB, VM, HB, HB, HB, VM, VM, HB],
        out_specs=(VM, VM, VM),
        scratch_shapes=[
            pltpu.VMEM((4, 2, 256, 128), BF16),
            pltpu.VMEM((4, 2, 8, 128), F32),
            pltpu.VMEM((4, 256, 128), BF16),
            pltpu.VMEM((4, 64, 512), BF16),
            pltpu.VMEM((4, 64, 512), BF16),
            pltpu.VMEM((1024, 2048), BF16),
            pltpu.VMEM((64, 2048), BF16),
            pltpu.VMEM((512, 256), BF16),
            pltpu.VMEM((2048, 512), BF16),
            pltpu.VMEM((2048, 512), BF16),
            pltpu.VMEM((512, 2048), BF16),
            pltpu.VMEM((64, 2048), F32),
            pltpu.VMEM((8, 64, 256), BF16),
            pltpu.VMEM((8, 64, 256), BF16),
            pltpu.VMEM((17, 32, 2048), BF16),
            pltpu.VMEM((16, 512), BF16),
            pltpu.VMEM((4, 8, 128, 256), BF16),
            pltpu.VMEM((4, 2, 128, 256), BF16),
            pltpu.VMEM((4, 2, 2, 128, 256), BF16),
            pltpu.VMEM((4, 128, 256), BF16),
            pltpu.VMEM((360, 2048), BF16),
            pltpu.VMEM((8, 256), F32),
            pltpu.VMEM((32, 8, 256), F32),
            pltpu.VMEM((8, 256), F32),
            pltpu.VMEM((8, 8, 256), F32),
            pltpu.VMEM((16, 512), BF16),
            pltpu.VMEM((8, 16, 512), BF16),
            pltpu.VMEM((2, 8, 128), F32),
            pltpu.VMEM((32, 8, 128), F32),
            pltpu.VMEM((8, 8, 128), F32),
            dma((10,)), dma((192,)), dma((4, 2)), dma((4, 2)), dma((4,)), dma((8, 2)), dma((8,)), dma((4, 2)), dma((4, 2, 2)), dma((4,)),
            dma((32,)), dma((8,)), dma((8,)), dma((32,)), dma((8,)),
        ],
        compiler_params=params(1),
        name="middle",
    )(
        heads, stats, w_all.reshape(1024, 2048), tokens, forward_gain[None], gate_weight, up_weight,
        down_weight, match, final_gain[None], head_weight,
    )
    return (hidden, cache.reshape(512, 2, 128), rms.reshape(REQS), top.reshape(REQS))


def solution(mesh):
    return jax.shard_map(
        per_device,
        mesh=mesh,
        in_specs=(
            P("seq", None),
            P(),
            P(None, "vocab"),
            P(None, "vocab"),
            P(None, "vocab"),
            P("vocab", None),
            P(),
            P(None, "vocab"),
            P(None, "vocab"),
            P("vocab", None),
            P(),
            P(("seq", "vocab"), None),
            P(),
            P("seq"),
            P("seq", None),
            P("seq"),
        ),
        out_specs=(P("seq", "vocab"), P("seq", None, "vocab"), P(), P()),
        check_vma=False,
    )
```

```python
import functools

import jax
import jax.numpy as jnp
from jax import lax
from jax.experimental import pallas as pl
from jax.experimental.pallas import tpu as pltpu
from jax.sharding import PartitionSpec as P

MESH = pl.DeviceIdType.MESH
HD = 128
REQS = 4
epsilon = 1e-06
rope_base = 1000000.0
neg_fill = -1e30
VM = pl.BlockSpec(memory_space=pltpu.VMEM)
SM = pl.BlockSpec(memory_space=pltpu.SMEM)
HB = pl.BlockSpec(memory_space=pl.ANY)
F32 = jnp.float32
BF16 = jnp.bfloat16
LIMIT = 62 * 1024 * 1024
SCALE = HD ** (-0.5) * 1.4426950408889634


def params(cid=None):
    if cid is None:
        return pltpu.CompilerParams(vmem_limit_bytes=LIMIT)
    return pltpu.CompilerParams(
        collective_id=cid, has_side_effects=True, vmem_limit_bytes=LIMIT
    )


def seq_at(s, dz, dy, dc):
    z, y, c = s // 4, (s // 2) % 2, s % 2
    return ((z + dz + 8) % 8) * 4 + ((y + dy) % 2) * 2 + (c + dc) % 2


def vocab_at(v, dx, dy):
    x, y = v // 2, v % 2
    return ((x + dx + 4) % 4) * 2 + (y + dy) % 2


def greet(peers):
    barrier = pltpu.get_barrier_semaphore()
    for peer in peers:
        pl.semaphore_signal(barrier, inc=1, device_id=peer, device_id_type=MESH)
    pl.semaphore_wait(barrier, len(peers))


def project_kernel(
    base_ref, tok_ref, gain_ref, wq_ref, wk_ref, wv_ref, cos_ref, sin_ref, slot_ref, live_ref,
    q_ref, kv_ref, cache_ref,
):
    gain = gain_ref[...].astype(F32)

    def rows_step(i, carry):
        rows = pl.ds(pl.multiple_of(i * 128, 128), 128)
        x = tok_ref[rows, :].astype(F32)
        scale = lax.rsqrt(jnp.mean(x * x, axis=-1, keepdims=True) + epsilon)
        normed = (x * scale * gain).astype(BF16)
        cos = cos_ref[rows, :]
        sin = sin_ref[rows, :]

        def turn(u):
            return u * cos + pltpu.roll(u, 64, axis=1) * sin

        q = jnp.dot(normed, wq_ref[...], preferred_element_type=F32)
        q_ref[rows, 0:128] = (turn(q[:, 0:128]) * SCALE).astype(BF16)
        q_ref[rows, 128:256] = (turn(q[:, 128:256]) * SCALE).astype(BF16)
        k = jnp.dot(normed, wk_ref[...], preferred_element_type=F32)
        kv_ref[rows, 0:128] = turn(k).astype(BF16)
        v = jnp.dot(normed, wv_ref[...], preferred_element_type=F32)
        kv_ref[rows, 128:256] = v.astype(BF16)
        return carry

    lax.fori_loop(0, 4, rows_step, 0)
    lane = lax.broadcasted_iota(jnp.int32, (16, 256), 1)
    run = jnp.where(lane < 128, base_ref[0] // 256, base_ref[256] // 256)
    run = run.astype(F32)
    kv_ref[512:528, :] = run.astype(BF16)
    row = lax.broadcasted_iota(jnp.int32, (16, 256), 0)
    q_ref[512:528, :] = jnp.where(row == 1, live_ref[...], run).astype(BF16)
    slots = slot_ref[...]

    def cache_step(i, carry):
        row = i * 128 + lax.broadcasted_iota(jnp.int32, (128, 512), 0)
        pick = jnp.where(row == slots, 1.0, 0.0).astype(BF16)
        moved = jnp.dot(pick, kv_ref[0:512, :], preferred_element_type=F32)
        cache_ref[pl.ds(pl.multiple_of(i * 128, 128), 128), :] = moved.astype(BF16)
        return carry

    lax.fori_loop(0, 4, cache_step, 0)


PIECE_ROWS = ((0, 128), (128, 128), (256, 128), (384, 144))


def gather_kernel(
    kv_ref, q_ref, w_ref, kv_all, q_all, w_all, tail_ref, tails, own_sem, send_sem, kv_sem, q_sem, w_sem
):
    s = lax.axis_index("seq")
    v = lax.axis_index("vocab")
    z, c, x = s // 4, s % 2, v // 2
    up = (seq_at(s, 1, 0, 0), v)
    down = (seq_at(s, -1, 0, 0), v)
    side = (seq_at(s, 0, 1, 0), v)
    core = (seq_at(s, 0, 0, 1), v)
    right = (s, vocab_at(v, 1, 0))
    left = (s, vocab_at(v, -1, 0))
    greet([up, down, side, core, right, left])
    started = []

    def go(src, dst, recv, peer):
        copy = pltpu.make_async_remote_copy(
            src_ref=src, dst_ref=dst, send_sem=send_sem.at[len(started)], recv_sem=recv,
            device_id=peer, device_id_type=MESH,
        )
        copy.start()
        started.append(copy)

    def take(dst, recv):
        pltpu.make_async_remote_copy(
            src_ref=dst, dst_ref=dst, send_sem=send_sem.at[0], recv_sem=recv,
            device_id=core, device_id_type=MESH,
        ).wait_recv()

    def kv_view(block, p):
        low, count = PIECE_ROWS[p]
        return kv_all.at[block, pl.ds(low, count), :]

    def kv_take(dz, p, peers):
        block = ((z + dz + 8) % 8) * 2 + c
        take(kv_view(block, p), kv_sem.at[block, p])
        for peer in peers:
            go(kv_view(block, p), kv_view(block, p), kv_sem.at[block, p], peer)

    def w_take(dx, p, peers):
        shard, piece = (x + dx + 4) % 4, 2 * c + p
        take(w_all.at[shard, piece], w_sem.at[shard, piece])
        for peer in peers:
            go(w_all.at[shard, piece], w_all.at[shard, piece], w_sem.at[shard, piece], peer)

    mine = z * 2 + c
    for p in range(4):
        low, count = PIECE_ROWS[p]
        for peer in (up, down, core):
            go(kv_ref.at[pl.ds(low, count), :], kv_view(mine, p), kv_sem.at[mine, p], peer)
    for p in range(2):
        piece = 2 * c + p
        for peer in (right, left):
            go(w_ref.at[piece], w_all.at[x, piece], w_sem.at[x, piece], peer)
    go(q_ref, q_all, q_sem.at[0], side)
    own = pltpu.make_async_copy(kv_ref, kv_all.at[mine], own_sem.at[0])
    own.start()

    for d in (1, 2):
        for p in range(4):
            kv_take(-d, p, (up, core))
            kv_take(d, p, (down, core))
        if d == 1:
            w_take(-1, 0, (right, core))
            w_take(1, 0, (core,))
    w_take(-1, 1, (core,))
    w_take(1, 1, (left, core))
    for p in range(4):
        kv_take(-3, p, (up, core) if p < 2 else (core,))
        kv_take(3, p, (down, core) if p >= 2 else (core,))
    for p in range(2):
        w_take(2, p, (core,))
    for p in range(4):
        kv_take(4, p, (core,))

    for dz in range(8):
        for p in range(4):
            block = ((z + dz) % 8) * 2 + 1 - c
            take(kv_view(block, p), kv_sem.at[block, p])
    take(q_all, q_sem.at[0])
    own.wait()
    ends = [
        pltpu.make_async_copy(kv_all.at[:, pl.ds(512, 16), :], tails.at[pl.ds(0, 16)], own_sem.at[0]),
        pltpu.make_async_copy(q_all.at[pl.ds(512, 16), :], tails.at[16], own_sem.at[1]),
    ]
    for copy in ends:
        copy.start()
    for dx in range(1, 4):
        for p in range(2):
            shard, piece = (x + dx) % 4, 2 * (1 - c) + p
            take(w_all.at[shard, piece], w_sem.at[shard, piece])
    for copy in ends:
        copy.wait()
    rows = tails[0:16].astype(F32)[:, 0, :].astype(jnp.int32)
    tail_ref[0:16, :] = rows[:, 0:128]
    tail_ref[16:32, :] = rows[:, 128:256]
    rows = tails[16].astype(F32)[0:8, :].astype(jnp.int32)
    tail_ref[32:33, :] = rows[0:1, 0:128]
    tail_ref[33:34, :] = rows[0:1, 128:256]
    tail_ref[34:35, :] = rows[1:2, 0:128]
    tail_ref[35:40, :] = jnp.zeros((5, 128), jnp.int32)
    for copy in started:
        copy.wait_send()


SLOTS = 8


def attend_kernel(
    tail_ref, base_ref, starts_ref, live_ref, me_ref, q_ref, other_ref, kv_ref, o_ref, st_ref,
    buf, sem, q_rows, top, total, acc, scores0, scores1, probs0, probs1, keep0, keep1,
    table, sorted_run, sorted_entry, before,
):
    me = me_ref[0]
    my_y = (me // 2) % 2
    other = me + 2 - 4 * my_y
    all_scores, all_probs, all_keep = (scores0, scores1), (probs0, probs1), (keep0, keep1)
    q_run = [base_ref[0] // 256, base_ref[256] // 256, tail_ref[32, 0], tail_ref[33, 0]]

    def clear(i, carry):
        table[i] = -1
        return carry

    def enter(i, carry):
        table[tail_ref[i, 0]] = i
        return carry

    def gather_up(i, count):
        before[i] = count
        entry = table[i]

        @pl.when(entry >= 0)
        def _():
            sorted_run[count] = i
            sorted_entry[count] = entry

        return jnp.where(entry >= 0, count + 1, count)

    lax.fori_loop(0, 64, clear, 0)
    lax.fori_loop(0, 32, enter, 0)
    before[64] = lax.fori_loop(0, 64, gather_up, 0)

    def low_of(position):
        low = starts_ref[0]
        for r in range(1, REQS):
            low = jnp.where(starts_ref[r] <= position, starts_ref[r], low)
        return low

    lasts, shifts, offsets = [], [], [0]
    for r in range(4):
        first = before[low_of(q_run[r] * 256) // 256]
        lasts.append(low_of(q_run[r] * 256 + 255))
        shifts.append(first - offsets[-1])
        offsets.append(offsets[-1] + before[q_run[r] + 1] - first)
    n = offsets[4]

    def choose(i, values):
        out = values[0]
        for r in range(1, 4):
            out = jnp.where(i >= offsets[r], values[r], out)
        return out

    def half(i):
        return choose(i, [0, 1, 2, 3])

    def place(i):
        return jnp.clip(i + choose(i, shifts), 0, 31)

    def key_run(i):
        return sorted_run[place(i)]

    def fetch(i):
        entry = sorted_entry[place(i)]
        slot = i % SLOTS
        return pltpu.make_async_copy(
            kv_ref.at[entry % 16, pl.ds((entry // 16) * 256, 256), :], buf.at[slot], sem.at[slot]
        )

    for i in range(SLOTS - 2):

        @pl.when(i < n)
        def _():
            fetch(i).start()

    for r in range(4):
        source = q_ref if r < 2 else other_ref
        for h in range(2):
            q_rows[r, pl.ds(h * 256, 256), :] = source[
                pl.ds((r % 2) * 256, 256), pl.ds(h * 128, 128)
            ]
    top[...] = jnp.full_like(top, neg_fill)
    total[...] = jnp.zeros_like(total)
    acc[...] = jnp.zeros_like(acc)
    buf[SLOTS - 1] = jnp.zeros((256, 256), BF16)
    probs1[...] = jnp.zeros_like(probs1)
    keep1[...] = jnp.ones_like(keep1)

    def score(i, into):
        into[...] = lax.dot_general(
            buf[i % SLOTS, :, 0:128], q_rows[half(i)],
            (((1,), (1,)), ((), ())), preferred_element_type=F32,
        )

    def collect(i, parity):
        r = half(i)
        added = lax.dot_general(
            buf[(i + SLOTS) % SLOTS, :, 128:256], all_probs[parity][...],
            (((0,), (0,)), ((), ())), preferred_element_type=F32,
        )
        acc[r] = acc[r] * all_keep[parity][...] + added

    def weigh(i, parity, masked, base):
        r = half(i)
        scores = all_scores[parity][...]
        if masked:
            lane = lax.broadcasted_iota(jnp.int32, (1, 512), 1)
            q_pos = base + (lane % 256)
            low = jnp.full((1, 512), starts_ref[0], jnp.int32)
            for req in range(1, REQS):
                low = jnp.where(starts_ref[req] <= q_pos, starts_ref[req], low)
            k_pos = key_run(i) * 256 + lax.broadcasted_iota(jnp.int32, (256, 512), 0)
            allowed = (k_pos <= q_pos) & (k_pos >= low)
            scores = jnp.where(allowed, scores, neg_fill)
        old = top[r]
        new = jnp.maximum(old, jnp.max(scores, axis=0, keepdims=True))
        probs = jnp.exp2(scores - new)
        if masked:
            probs = jnp.where(allowed, probs, 0.0)
        keep = jnp.exp2(old - new)
        top[r] = new
        total[r] = total[r] * keep + jnp.sum(probs, axis=0, keepdims=True)
        all_keep[parity][...] = keep
        all_probs[parity][...] = probs.astype(BF16)

    def stage(i, parity):
        @pl.when(i + SLOTS - 2 < n)
        def _():
            fetch(i + SLOTS - 2).start()

        @pl.when(i + 1 < n)
        def _():
            fetch(i + 1).wait()

        run = key_run(i)
        base = choose(i, q_run) * 256
        last_low = choose(i, lasts)
        slot = sorted_entry[place(i)] % 16
        block = (slot // 2) * 4 + my_y * 2 + slot % 2
        live = jnp.where(
            i < offsets[2], live_ref[(me - block + 32) % 32], tail_ref[34, (other - block + 32) % 32]
        ) > 0
        whole = (run * 256 < base) & (run * 256 >= last_low)

        @pl.when(live & whole)
        def _():
            weigh(i, parity, False, base)
            score(i + 1, all_scores[1 - parity])
            collect(i - 1, 1 - parity)

        @pl.when(live & jnp.logical_not(whole))
        def _():
            weigh(i, parity, True, base)
            score(i + 1, all_scores[1 - parity])
            collect(i - 1, 1 - parity)

        @pl.when(jnp.logical_not(live))
        def _():
            score(i + 1, all_scores[1 - parity])
            collect(i - 1, 1 - parity)
            all_keep[parity][...] = jnp.ones((1, 512), F32)
            all_probs[parity][...] = jnp.zeros((256, 512), BF16)

    def pair(k, carry):
        stage(2 * k, 0)

        @pl.when(2 * k + 1 < n)
        def _():
            stage(2 * k + 1, 1)

        return carry

    fetch(0).wait()
    score(0, scores0)
    lax.fori_loop(0, (n + 1) // 2, pair, 0)

    @pl.when(n % 2 == 1)
    def _():
        collect(n - 1, 0)

    @pl.when(n % 2 == 0)
    def _():
        collect(n - 1, 1)

    for r in range(4):
        weight = total[r]
        done = (acc[r] * jnp.where(weight > 0, 1.0 / weight, 0.0)).astype(BF16)
        for part in range(2):
            k = 2 * (r % 2) + part
            for h in range(2):
                low = h * 256 + part * 128
                o_ref[r // 2, k, h * 128 : (h + 1) * 128, :] = done[:, low : low + 128]
                st_ref[r // 2, k, h : h + 1, :] = top[r, :, low : low + 128]
                st_ref[r // 2, k, 2 + h : 3 + h, :] = weight[:, low : low + 128]


def middle_kernel(
    heads_ref, stats_ref, w_ref, w_own, tok_ref, gain_ref, wg_ref, wu_ref, wd_ref, match_ref, final_ref, head_ref,
    out_ref, rms_ref, top_ref,
    heads, stats, joined, near_send, near_got, w, tok_rows, tok_cols, wg, wu, wd, att, att_send, att_cols, normed, act, part, fwd_in,
    x_in, y_in, head, row_send, seq_got, wide_send, wide_got, last_send, last_got, max_send, seq_max, vocab_max,
    load_sem, send_sem, head_recv, stat_recv, near_recv, norm_recv, att_recv, fwd_recv, x_recv, y_recv,
    row_recv, wide_recv, last_recv, max_recv, top_recv,
):
    s = lax.axis_index("seq")
    v = lax.axis_index("vocab")
    others = [(v + r) % 8 for r in range(1, 8)]
    seqs = [(s + r) % 32 for r in range(1, 32)]
    cols = pl.ds(pl.multiple_of(v * 256, 256), 256)
    rows = pl.ds(pl.multiple_of(v * 64, 64), 64)
    loads = [
        pltpu.make_async_copy(w_own, w.at[v // 2], load_sem.at[0]),
        pltpu.make_async_copy(tok_ref.at[rows, :], tok_rows, load_sem.at[1]),
        pltpu.make_async_copy(tok_ref.at[:, cols], tok_cols, load_sem.at[2]),
        pltpu.make_async_copy(wg_ref, wg, load_sem.at[3]),
        pltpu.make_async_copy(wu_ref, wu, load_sem.at[4]),
        pltpu.make_async_copy(wd_ref, wd, load_sem.at[5]),
        pltpu.make_async_copy(heads_ref.at[0, v // 2], heads.at[v // 2, (s // 2) % 2], load_sem.at[6]),
        pltpu.make_async_copy(stats_ref.at[0, v // 2], stats.at[v // 2, (s // 2) % 2], load_sem.at[9]),
        pltpu.make_async_copy(head_ref, head, load_sem.at[8]),
    ] + [
        pltpu.make_async_copy(
            w_ref.at[(v // 2 + d) % 4], w.at[(v // 2 + d) % 4], load_sem.at[9 + d]
        )
        for d in range(1, 4)
    ]
    for copy in loads:
        copy.start()
    x = v // 2
    y = v % 2
    my_y = (s // 2) % 2
    across = seq_at(s, 0, 1, 0)
    greet(
        [(s, other) for other in others]
        + [(other, v) for other in seqs]
        + [(across, vocab_at(v, dx, 0)) for dx in range(1, 4)]
    )
    sent = []

    def go(src, dst, recv, peer):
        copy = pltpu.make_async_remote_copy(
            src_ref=src, dst_ref=dst, send_sem=send_sem.at[len(sent)], recv_sem=recv,
            device_id=peer, device_id_type=MESH,
        )
        copy.start()
        sent.append(copy)

    def take(dst, recv):
        pltpu.make_async_remote_copy(
            src_ref=dst, dst_ref=dst, send_sem=send_sem.at[0], recv_sem=recv,
            device_id=(s, others[0]), device_id_type=MESH,
        ).wait_recv()

    for dx in (2, 1, 3, 0):
        target = (x + dx) % 4
        for which in (1, 0):
            if (dx, which) != (0, 0):
                peer = (across if which else s, vocab_at(v, dx, 0))
                go(heads_ref.at[which, target], heads.at[x, my_y], head_recv.at[x, my_y], peer)
                go(stats_ref.at[which, target], stats.at[x, my_y], stat_recv.at[x, my_y], peer)
    for i in (0, 1, 6, 7, 9, 10, 11):
        loads[i].wait()
    for dx in range(4):
        source = (x + dx) % 4
        for which in range(2):
            if (dx, which) != (0, 0):
                held = (my_y + which) % 2
                take(heads.at[source, held], head_recv.at[source, held])
                take(stats.at[source, held], stat_recv.at[source, held])
    for k in range(4):
        for h in range(2):
            tops = [stats[k, i, h : h + 1, :] for i in range(2)]
            best = jnp.maximum(tops[0], tops[1])
            weights = [stats[k, i, 2 + h : 3 + h, :] * jnp.exp2(tops[i] - best) for i in range(2)]
            scale = 1.0 / (weights[0] + weights[1])
            span = pl.ds(h * 128, 128)
            joined[k, span, :] = (
                heads[k, 0, span, :].astype(F32) * (weights[0] * scale)
                + heads[k, 1, span, :].astype(F32) * (weights[1] * scale)
            ).astype(BF16)

    near = vocab_at(v, 0, 1)
    for j in range(4):
        total = jnp.zeros((128, 512), F32)
        for k in range(4):
            total += lax.dot_general(
                joined[k], w[k, :, j * 512 : (j + 1) * 512],
                (((0,), (0,)), ((), ())), preferred_element_type=F32,
            )
        att[:, j * 512 : (j + 1) * 512] = jnp.where(y == 0, total[0:64], total[64:128])
        near_send[j] = jnp.where(y == 0, total[64:128], total[0:64]).astype(BF16)
        go(near_send.at[j], near_got.at[j], near_recv.at[j], (s, near))
    for j in range(4):
        take(near_got.at[j], near_recv.at[j])

    def project(j, square):
        wide = pl.ds(pl.multiple_of(j * 512, 512), 512)
        total = att[:, wide] + near_got[j].astype(F32)
        att_send[2 * j] = total[:, 0:256].astype(BF16)
        att_send[2 * j + 1] = total[:, 256:512].astype(BF16)
        residual = tok_rows[:, wide].astype(F32) + total
        att[:, wide] = residual
        return square + jnp.sum(residual * residual, axis=-1, keepdims=True)

    square = lax.fori_loop(0, 4, project, jnp.zeros((64, 1), F32))
    gain = gain_ref[...].astype(F32)
    mine = (att[...] * lax.rsqrt(square / 2048 + epsilon) * gain).astype(BF16)
    normed[2 * v] = mine[0:32]
    normed[2 * v + 1] = mine[32:64]

    right, left = vocab_at(v, 1, 0), vocab_at(v, -1, 0)

    def pass_on(owner, p, other):
        view = normed.at[2 * owner + p]
        go(view, view, norm_recv.at[owner, p], (s, other))

    def arrive(dx, dy, p, peers):
        owner = vocab_at(v, dx, dy)
        take(normed.at[2 * owner + p], norm_recv.at[owner, p])
        for peer in peers:
            pass_on(owner, p, peer)

    for other in others:
        go(att_send.at[other], att_cols.at[v], att_recv.at[v], (s, other))
    for p in range(2):
        for peer in (right, left, near):
            pass_on(v, p, peer)
    own_cols = pltpu.make_async_copy(att_send.at[v], att_cols.at[v], load_sem.at[7])
    own_cols.start()

    loads[2].wait()
    own_cols.wait()
    for other in others:
        take(att_cols.at[other], att_recv.at[other])
    picked = jnp.zeros((8, 256), F32)
    for i in range(8):
        residual = tok_cols[i * 64 : (i + 1) * 64, :].astype(F32) + att_cols[i].astype(F32)
        high = residual.astype(BF16)
        low = (residual - high.astype(F32)).astype(BF16)
        picked += jnp.dot(match_ref[i], high, preferred_element_type=F32)
        picked += jnp.dot(match_ref[i], low, preferred_element_type=F32)
    row_send[...] = picked
    seq_got[s] = picked
    for other in seqs:
        go(row_send, seq_got.at[s], row_recv.at[s], (other, v))

    for p in range(2):
        arrive(-1, 0, p, (right,) if p == 0 else ())
        arrive(1, 0, p, (left,) if p == 1 else ())
        arrive(0, 1, p, (right, left))

    for i in (3, 4, 5):
        loads[i].wait()
    def feed(values):
        gate = jnp.dot(values, wg[...], preferred_element_type=F32)
        upward = jnp.dot(values, wu[...], preferred_element_type=F32)
        return (gate / (1.0 + jnp.exp(-gate)) * upward).astype(BF16)

    def part_of(chunk, dx, dy):
        return part.at[chunk, vocab_at(v, dx, dy)]

    def at_y(chunk, dx, lane):
        return part.at[chunk, ((x + dx + 4) % 4) * 2 + lane]

    def rows_of(dx, extra):
        chunk = (x + dx + 4) % 4
        values = normed[pl.ds(4 * chunk, 4)].reshape(128, 2048)
        if extra:
            values = jnp.concatenate([values, normed[16]], axis=0)
        active = feed(values)
        if extra:
            act[...] = active[128:144]
            active = active[0:128]
        for t in range(8):
            part[chunk, t] = jnp.dot(
                active, wd[:, t * 256 : (t + 1) * 256], preferred_element_type=F32
            ).astype(BF16)
        go(at_y(chunk, 2, 0), fwd_in.at[chunk, 0], fwd_recv.at[chunk, 0], (s, right))
        go(at_y(chunk, 2, 1), fwd_in.at[chunk, 1], fwd_recv.at[chunk, 1], (s, left))
        go(at_y(chunk, 1, 1), x_in.at[chunk, 0, 1], x_recv.at[chunk, 0, 1], (s, right))
        go(at_y(chunk, -1, 0), x_in.at[chunk, 1, 0], x_recv.at[chunk, 1, 0], (s, left))

    rows_of(0, False)
    for other in seqs:
        take(seq_got.at[other], row_recv.at[other])
    picked = jnp.sum(seq_got[...], axis=0)
    wide_send[...] = picked
    wide_got[v] = picked
    for other in others:
        go(wide_send, wide_got.at[v], wide_recv.at[v], (s, other))

    for p in range(2):
        arrive(2, 0, p, (near,))
    for p in range(2):
        arrive(-1, 1, p, ())
        arrive(1, 1, p, ())
    rows_of(-1, False)
    for other in others:
        take(wide_got.at[other], wide_recv.at[other])
    square = jnp.zeros((8, 1), F32)
    for k in range(8):
        square += jnp.sum(wide_got[k] * wide_got[k], axis=-1, keepdims=True)
    inverse = lax.rsqrt(square / 2048 + epsilon)
    normed[16, 16:32, :] = jnp.zeros((16, 2048), BF16)
    for k in range(8):
        one = wide_got[k] * inverse * gain[:, k * 256 : (k + 1) * 256]
        normed[16, 0:16, k * 256 : (k + 1) * 256] = jnp.concatenate([one, one], axis=0).astype(BF16)
    rows_of(1, True)

    group = lax.broadcasted_iota(jnp.int32, (16, 512), 0) // 4

    def packed(quarter):
        out = quarter(0)
        for q in range(1, 4):
            out = jnp.where(group == q, quarter(q), out)
        return out

    last = act[...]
    mine = packed(
        lambda q: jnp.dot(
            last, wd[:, q * 512 : (q + 1) * 512], preferred_element_type=F32
        )
    ).astype(BF16)
    last_send[...] = mine
    last_got[v] = mine
    for other in others:
        go(last_send, last_got.at[v], last_recv.at[v], (s, other))
    for p in range(2):
        arrive(2, 1, p, ())
    rows_of(2, False)

    def add_to(ref, *incoming):
        value = ref[...].astype(F32)
        for one in incoming:
            value += one[...].astype(F32)
        ref[...] = value.astype(BF16)

    def onward(dx, way):
        chunk = (x + dx + 4) % 4
        take(fwd_in.at[chunk, way], fwd_recv.at[chunk, way])
        ref = at_y(chunk, 1 if way == 0 else -1, way)
        add_to(ref, fwd_in.at[chunk, way])
        go(ref, x_in.at[chunk, way, way], x_recv.at[chunk, way, way], (s, right if way == 0 else left))

    for to_right, to_left in ((-1, 1), (2, 0), (0, 2), (1, -1)):
        onward(to_right, 0)
        onward(to_left, 1)

    for other in others:
        take(last_got.at[other], last_recv.at[other])

    def quarter_rows(q):
        one = jnp.concatenate([wide_got[2 * q], wide_got[2 * q + 1]], axis=1)
        return jnp.concatenate([one, one], axis=0)

    total = last_got[0].astype(F32)
    for k in range(1, 8):
        total += last_got[k].astype(F32)
    final = (packed(quarter_rows) + total).astype(BF16).astype(F32)
    square = jnp.broadcast_to(jnp.sum(final * final, axis=-1, keepdims=True), (16, 128))
    square = square + pltpu.roll(square, 8, axis=0)
    square = square + pltpu.roll(square, 4, axis=0)
    mean_square = square / 2048 + epsilon
    diagonal = lax.broadcasted_iota(jnp.int32, (16, 128), 0) == lax.broadcasted_iota(
        jnp.int32, (16, 128), 1
    )

    def along_lanes(value):
        return jnp.sum(jnp.where(diagonal, value, 0.0), axis=0, keepdims=True)

    rms_ref[...] = along_lanes(jnp.sqrt(mean_square))[:, :REQS]
    inverse = lax.rsqrt(mean_square)[:, 0:1]
    spread = packed(
        lambda q: jnp.broadcast_to(
            final_ref[:, q * 512 : (q + 1) * 512].astype(F32), (16, 512)
        )
    )
    final = final * inverse * spread
    loads[8].wait()
    logits = jnp.zeros((16, 360), F32)
    for q in range(4):
        turned = final if q == 0 else pltpu.roll(final, 16 - 4 * q, axis=0)
        logits += lax.dot_general(
            turned.astype(BF16), head[:, q * 512 : (q + 1) * 512], (((1,), (1,)), ((), ())),
            preferred_element_type=F32,
        )
    best = along_lanes(jnp.broadcast_to(jnp.max(logits, axis=-1, keepdims=True), (16, 128)))
    best = jnp.broadcast_to(best, (8, 128))
    max_send[0] = best
    seq_max[s] = best
    for other in seqs:
        go(max_send.at[0], seq_max.at[s], max_recv.at[s], (other, v))
    for dx in (0, -1, 1, 2):
        chunk = (x + dx + 4) % 4
        for way in range(2):
            take(x_in.at[chunk, way, 1 - y], x_recv.at[chunk, way, 1 - y])
        ref = part_of(chunk, 0, 1)
        add_to(ref, x_in.at[chunk, 0, 1 - y], x_in.at[chunk, 1, 1 - y])
        go(ref, y_in.at[chunk], y_recv.at[chunk], (s, near))

    for other in seqs:
        take(seq_max.at[other], max_recv.at[other])
    best = jnp.max(seq_max[...], axis=0)
    max_send[1] = best
    vocab_max[v] = best
    for other in others:
        go(max_send.at[1], vocab_max.at[v], top_recv.at[v], (s, other))

    for dx in (0, -1, 1, 2):
        chunk = (x + dx + 4) % 4
        for way in range(2):
            take(x_in.at[chunk, way, y], x_recv.at[chunk, way, y])
        take(y_in.at[chunk], y_recv.at[chunk])
        rows = pl.ds(pl.multiple_of(chunk * 128, 128), 128)
        total = tok_cols[rows, :].astype(F32)
        total += att_cols[pl.ds(2 * chunk, 2)].reshape(128, 256).astype(F32)
        total += part[chunk, v].astype(F32)
        total += x_in[chunk, 0, y].astype(F32)
        total += x_in[chunk, 1, y].astype(F32)
        total += y_in[chunk].astype(F32)
        out_ref[rows, :] = total.astype(BF16)
    for other in others:
        take(vocab_max.at[other], top_recv.at[other])
    top_ref[...] = jnp.max(vocab_max[...], axis=0)[0:1, :REQS]
    for copy in sent:
        copy.wait_send()


def hand_over_kernel(hidden_ref, rms_ref, top_ref, hidden_out, rms_out, top_out):
    hidden_out[...] = hidden_ref[...]
    rms_out[...] = rms_ref[...]
    top_out[...] = top_ref[...]


def per_device(
    tokens,
    attention_gain,
    query_weight,
    key_weight,
    value_weight,
    out_weight,
    forward_gain,
    gate_weight,
    up_weight,
    down_weight,
    final_gain,
    head_weight,
    segment_ids,
    token_order,
    live_blocks,
    cache_slots,
):
    shape = jax.ShapeDtypeStruct
    me = lax.axis_index("seq").astype(jnp.int32)
    request = jnp.arange(8, dtype=jnp.int32)
    starts = jnp.sum((segment_ids[None, :] < request[:, None]).astype(jnp.int32), axis=1)
    position = token_order - starts[0]
    for r in range(1, REQS):
        position = jnp.where(starts[r] <= token_order, token_order - starts[r], position)
    lane = jnp.arange(128, dtype=jnp.int32)
    inverse = rope_base ** (-(lane % 64).astype(F32) * 2.0 / 128)
    angle = position.astype(F32)[:, None] * inverse[None, :]
    cos = jnp.cos(angle)
    sin = jnp.where(lane < 64, -1.0, 1.0)[None, :] * jnp.sin(angle)

    query, kv, cache = pl.pallas_call(
        project_kernel,
        out_shape=(shape((528, 256), BF16), shape((528, 256), BF16), shape((512, 256), BF16)),
        in_specs=[SM] + [VM] * 9,
        out_specs=(VM, VM, VM),
        compiler_params=params(),
        name="project",
    )(
        token_order, tokens, attention_gain[None], query_weight, key_weight, value_weight, cos, sin,
        cache_slots[None], jnp.pad(live_blocks.astype(F32), ((0, 0), (0, 224))),
    )

    kv_all, q_other, w_all, tail = pl.pallas_call(
        gather_kernel,
        out_shape=(
            shape((16, 528, 256), BF16), shape((528, 256), BF16), shape((4, 4, 64, 2048), BF16),
            shape((40, 128), jnp.int32),
        ),
        in_specs=[VM, VM, HB],
        out_specs=(HB, HB, HB, VM),
        scratch_shapes=[
            pltpu.VMEM((17, 16, 256), BF16),
            pltpu.SemaphoreType.DMA((2,)),
            pltpu.SemaphoreType.DMA((128,)),
            pltpu.SemaphoreType.DMA((16, 4)),
            pltpu.SemaphoreType.DMA((1,)),
            pltpu.SemaphoreType.DMA((4, 4)),
        ],
        compiler_params=params(0),
        name="gather",
    )(kv, query, out_weight.reshape(4, 64, 2048))

    heads, stats = pl.pallas_call(
        attend_kernel,
        out_shape=(shape((2, 4, 256, 128), BF16), shape((2, 4, 8, 128), F32)),
        in_specs=[SM] * 5 + [VM, VM, HB],
        out_specs=(VM, VM),
        scratch_shapes=[
            pltpu.VMEM((SLOTS, 256, 256), BF16),
            pltpu.SemaphoreType.DMA((SLOTS,)),
            pltpu.VMEM((4, 512, 128), BF16),
            pltpu.VMEM((4, 1, 512), F32),
            pltpu.VMEM((4, 1, 512), F32),
            pltpu.VMEM((4, 128, 512), F32),
            pltpu.VMEM((256, 512), F32),
            pltpu.VMEM((256, 512), F32),
            pltpu.VMEM((256, 512), BF16),
            pltpu.VMEM((256, 512), BF16),
            pltpu.VMEM((1, 512), F32),
            pltpu.VMEM((1, 512), F32),
            pltpu.SMEM((64,), jnp.int32),
            pltpu.SMEM((32,), jnp.int32),
            pltpu.SMEM((32,), jnp.int32),
            pltpu.SMEM((65,), jnp.int32),
        ],
        compiler_params=params(),
        name="attend",
    )(tail, token_order, starts, live_blocks[0], me[None], query, q_other, kv_all)

    ends = jnp.concatenate([starts[1:REQS], jnp.full((1,), segment_ids.shape[0], jnp.int32)])
    last_index = jnp.concatenate([ends - 1, ends - 1])
    match = (token_order.reshape(8, 1, 64) == last_index[None, :, None]).astype(BF16)
    dma = pltpu.SemaphoreType.DMA
    hidden, rms, top = pl.pallas_call(
        middle_kernel,
        out_shape=(shape((512, 256), BF16), shape((1, REQS), F32), shape((1, REQS), F32)),
        in_specs=[VM, VM, HB, HB, HB, VM, HB, HB, HB, VM, VM, HB],
        out_specs=(VM, VM, VM),
        scratch_shapes=[
            pltpu.VMEM((4, 2, 256, 128), BF16),
            pltpu.VMEM((4, 2, 8, 128), F32),
            pltpu.VMEM((4, 256, 128), BF16),
            pltpu.VMEM((4, 64, 512), BF16),
            pltpu.VMEM((4, 64, 512), BF16),
            pltpu.VMEM((4, 256, 2048), BF16),
            pltpu.VMEM((64, 2048), BF16),
            pltpu.VMEM((512, 256), BF16),
            pltpu.VMEM((2048, 512), BF16),
            pltpu.VMEM((2048, 512), BF16),
            pltpu.VMEM((512, 2048), BF16),
            pltpu.VMEM((64, 2048), F32),
            pltpu.VMEM((8, 64, 256), BF16),
            pltpu.VMEM((8, 64, 256), BF16),
            pltpu.VMEM((17, 32, 2048), BF16),
            pltpu.VMEM((16, 512), BF16),
            pltpu.VMEM((4, 8, 128, 256), BF16),
            pltpu.VMEM((4, 2, 128, 256), BF16),
            pltpu.VMEM((4, 2, 2, 128, 256), BF16),
            pltpu.VMEM((4, 128, 256), BF16),
            pltpu.VMEM((360, 2048), BF16),
            pltpu.VMEM((8, 256), F32),
            pltpu.VMEM((32, 8, 256), F32),
            pltpu.VMEM((8, 256), F32),
            pltpu.VMEM((8, 8, 256), F32),
            pltpu.VMEM((16, 512), BF16),
            pltpu.VMEM((8, 16, 512), BF16),
            pltpu.VMEM((2, 8, 128), F32),
            pltpu.VMEM((32, 8, 128), F32),
            pltpu.VMEM((8, 8, 128), F32),
            dma((13,)), dma((192,)), dma((4, 2)), dma((4, 2)), dma((4,)), dma((8, 2)), dma((8,)), dma((4, 2)), dma((4, 2, 2)), dma((4,)),
            dma((32,)), dma((8,)), dma((8,)), dma((32,)), dma((8,)),
        ],
        compiler_params=params(1),
        name="middle",
    )(
        heads, stats, w_all.reshape(4, 256, 2048), out_weight, tokens, forward_gain[None], gate_weight, up_weight,
        down_weight, match, final_gain[None], head_weight,
    )
    hidden, rms, top = pl.pallas_call(
        hand_over_kernel,
        out_shape=(shape((512, 256), BF16), shape((1, REQS), F32), shape((1, REQS), F32)),
        in_specs=[VM, VM, VM],
        out_specs=(VM, VM, VM),
        compiler_params=params(),
        name="hand_over",
    )(hidden, rms, top)
    return (hidden, cache.reshape(512, 2, 128), rms.reshape(REQS), top.reshape(REQS))


def solution(mesh):
    return jax.shard_map(
        per_device,
        mesh=mesh,
        in_specs=(
            P("seq", None),
            P(),
            P(None, "vocab"),
            P(None, "vocab"),
            P(None, "vocab"),
            P("vocab", None),
            P(),
            P(None, "vocab"),
            P(None, "vocab"),
            P("vocab", None),
            P(),
            P(("seq", "vocab"), None),
            P(),
            P("seq"),
            P("seq", None),
            P("seq"),
        ),
        out_specs=(P("seq", "vocab"), P("seq", None, "vocab"), P(), P()),
        check_vma=False,
    )
```

```python
import functools

import jax
import jax.numpy as jnp
import numpy as np
from jax import lax
from jax.experimental import pallas as pl
from jax.experimental.pallas import tpu as pltpu
from jax.sharding import PartitionSpec as P

MESH = pl.DeviceIdType.MESH
HD = 128
REQS = 4
epsilon = 1e-06
rope_base = 1000000.0
neg_fill = -1e30
VM = pl.BlockSpec(memory_space=pltpu.VMEM)
SM = pl.BlockSpec(memory_space=pltpu.SMEM)
HB = pl.BlockSpec(memory_space=pl.ANY)
F32 = jnp.float32
BF16 = jnp.bfloat16
LIMIT = 62 * 1024 * 1024
SCALE = HD ** (-0.5) * 1.4426950408889634


def params(cid=None):
    if cid is None:
        return pltpu.CompilerParams(vmem_limit_bytes=LIMIT)
    return pltpu.CompilerParams(
        collective_id=cid, has_side_effects=True, vmem_limit_bytes=LIMIT
    )


def seq_at(s, dz, dy, dc):
    z, y, c = s // 4, (s // 2) % 2, s % 2
    return ((z + dz + 8) % 8) * 4 + ((y + dy) % 2) * 2 + (c + dc) % 2


def vocab_at(v, dx, dy):
    x, y = v // 2, v % 2
    return ((x + dx + 4) % 4) * 2 + (y + dy) % 2


def wide_row(ref):
    rows = ref[...].astype(F32)
    return jnp.concatenate([rows[i : i + 1] for i in range(16)], axis=1)


def greet(peers):
    barrier = pltpu.get_barrier_semaphore()
    for peer in peers:
        pl.semaphore_signal(barrier, inc=1, device_id=peer, device_id_type=MESH)
    pl.semaphore_wait(barrier, len(peers))


FREQUENCY = rope_base ** (-(np.arange(128) % 64) * 2.0 / 128)
STEP_COS = np.cos(np.arange(256)[:, None] * FREQUENCY[None, :]).astype(np.float32)
STEP_SIN = np.sin(np.arange(256)[:, None] * FREQUENCY[None, :]).astype(np.float32)


PIECE_ROWS = ((0, 128), (128, 128), (256, 128), (384, 144))


def gather_kernel(
    base_ref, starts_ref, live_ref, tok_ref, gain_ref, wq_ref, wk_ref, wv_ref,
    step_cos, step_sin, run_cos, run_sin, slot_ref, w_ref,
    q_ref, cache_ref, match_ref, kv_all, q_all, w_all, tail_ref,
    kv_ref, normed, cosines, sines, tails, own_sem, send_sem, kv_sem, q_sem, w_sem,
):
    s = lax.axis_index("seq")
    v = lax.axis_index("vocab")
    z, c, x = s // 4, s % 2, v // 2
    up = (seq_at(s, 1, 0, 0), v)
    down = (seq_at(s, -1, 0, 0), v)
    side = (seq_at(s, 0, 1, 0), v)
    core = (seq_at(s, 0, 0, 1), v)
    right = (s, vocab_at(v, 1, 0))
    left = (s, vocab_at(v, -1, 0))
    barrier = pltpu.get_barrier_semaphore()
    for peer in (up, down, side, core, right, left):
        pl.semaphore_signal(barrier, inc=1, device_id=peer, device_id_type=MESH)
    gain = wide_row(gain_ref)
    lane = lax.broadcasted_iota(jnp.int32, (128, 128), 1)

    def turn(u, i):
        rows = pl.ds(i * 128, 128)
        return u * cosines[rows, :] + pltpu.roll(u, 64, axis=1) * sines[rows, :]

    def keys_values(i):
        rows = pl.ds(i * 128, 128)
        values = tok_ref[rows, :].astype(F32)
        scale = lax.rsqrt(jnp.mean(values * values, axis=-1, keepdims=True) + epsilon)
        values = (values * scale * gain).astype(BF16)
        normed[rows, :] = values
        r = i // 2
        steps = pl.ds((i % 2) * 128, 128)
        order = base_ref[r * 256] + (i % 2) * 128 + lax.broadcasted_iota(jnp.int32, (128, 128), 0)
        near_cos = jnp.broadcast_to(run_cos[4 * r : 4 * r + 1, :], (128, 128))
        near_sin = jnp.broadcast_to(run_sin[4 * r : 4 * r + 1, :], (128, 128))
        for req in range(1, REQS):
            later = order >= starts_ref[req]
            near_cos = jnp.where(later, run_cos[4 * r + req : 4 * r + req + 1, :], near_cos)
            near_sin = jnp.where(later, run_sin[4 * r + req : 4 * r + req + 1, :], near_sin)
        cosines[rows, :] = step_cos[steps, :] * near_cos - step_sin[steps, :] * near_sin
        sine = step_sin[steps, :] * near_cos + step_cos[steps, :] * near_sin
        sines[rows, :] = jnp.where(lane < 64, -sine, sine)
        key = jnp.dot(values, wk_ref[...], preferred_element_type=F32)
        kv_ref[rows, 0:128] = turn(key, i).astype(BF16)
        value = jnp.dot(values, wv_ref[...], preferred_element_type=F32)
        kv_ref[rows, 128:256] = value.astype(BF16)

    half = lax.broadcasted_iota(jnp.int32, (16, 256), 1)
    run = jnp.where(half < 128, base_ref[0] // 256, base_ref[256] // 256).astype(F32)
    kv_ref[512:528, :] = run.astype(BF16)
    keys_values(0)
    pl.semaphore_wait(barrier, 6)
    started = []

    def go(src, dst, recv, peer):
        copy = pltpu.make_async_remote_copy(
            src_ref=src, dst_ref=dst, send_sem=send_sem.at[len(started)], recv_sem=recv,
            device_id=peer, device_id_type=MESH,
        )
        copy.start()
        started.append(copy)

    def take(dst, recv):
        pltpu.make_async_remote_copy(
            src_ref=dst, dst_ref=dst, send_sem=send_sem.at[0], recv_sem=recv,
            device_id=core, device_id_type=MESH,
        ).wait_recv()

    def kv_view(block, p):
        low, count = PIECE_ROWS[p]
        return kv_all.at[block, pl.ds(low, count), :]

    def kv_take(dz, p, peers):
        block = ((z + dz + 8) % 8) * 2 + c
        take(kv_view(block, p), kv_sem.at[block, p])
        for peer in peers:
            go(kv_view(block, p), kv_view(block, p), kv_sem.at[block, p], peer)

    def w_take(dx, p, peers):
        shard, piece = (x + dx + 4) % 4, 2 * c + p
        take(w_all.at[shard, piece], w_sem.at[shard, piece])
        for peer in peers:
            go(w_all.at[shard, piece], w_all.at[shard, piece], w_sem.at[shard, piece], peer)

    mine = z * 2 + c
    for p in range(4):
        if p:
            keys_values(p)
        low, count = PIECE_ROWS[p]
        for peer in (up, down, core):
            go(kv_ref.at[pl.ds(low, count), :], kv_view(mine, p), kv_sem.at[mine, p], peer)
        if p < 2:
            piece = 2 * c + p
            for peer in (right, left):
                go(w_ref.at[piece], w_all.at[x, piece], w_sem.at[x, piece], peer)
    own = pltpu.make_async_copy(kv_ref, kv_all.at[mine], own_sem.at[0])
    own.start()
    for p in range(4):
        rows = pl.ds(p * 128, 128)
        query = jnp.dot(normed[rows, :], wq_ref[...], preferred_element_type=F32)
        q_ref[rows, 0:128] = (turn(query[:, 0:128], p) * SCALE).astype(BF16)
        q_ref[rows, 128:256] = (turn(query[:, 128:256], p) * SCALE).astype(BF16)
    row = lax.broadcasted_iota(jnp.int32, (16, 256), 0)
    for i in range(32):
        run = jnp.where((row == 1) & (half == i), live_ref[i].astype(F32), run)
    q_ref[512:528, :] = run.astype(BF16)
    go(q_ref, q_all, q_sem.at[0], side)

    for d in (1, 2):
        for p in range(4):
            kv_take(-d, p, (up, core))
            kv_take(d, p, (down, core))
        if d == 1:
            w_take(-1, 0, (right, core))
            w_take(1, 0, (core,))
    w_take(-1, 1, (core,))
    w_take(1, 1, (left, core))
    slots = slot_ref[...]
    for i in range(4):
        row = i * 128 + lax.broadcasted_iota(jnp.int32, (128, 512), 0)
        pick = jnp.where(row == slots, 1.0, 0.0).astype(BF16)
        moved = jnp.dot(pick, kv_ref[0:512, :], preferred_element_type=F32)
        cache_ref[i * 128 : (i + 1) * 128, :] = moved.astype(BF16)
    request = lax.broadcasted_iota(jnp.int32, (8, 64), 0) % REQS
    last = jnp.full((8, 64), starts_ref[1] - 1, jnp.int32)
    for req in range(1, REQS):
        last = jnp.where(request == req, starts_ref[req + 1] - 1, last)
    for i in range(8):
        order = base_ref[256 * (i // 4)] + (i % 4) * 64 + lax.broadcasted_iota(jnp.int32, (8, 64), 1)
        match_ref[i] = jnp.where(order == last, 1.0, 0.0).astype(BF16)
    for p in range(4):
        kv_take(-3, p, (up, core) if p < 2 else (core,))
        kv_take(3, p, (down, core) if p >= 2 else (core,))
    for p in range(2):
        w_take(2, p, (core,))
    for p in range(4):
        kv_take(4, p, (core,))

    for dz in range(8):
        for p in range(4):
            block = ((z + dz) % 8) * 2 + 1 - c
            take(kv_view(block, p), kv_sem.at[block, p])
    take(q_all, q_sem.at[0])
    own.wait()
    ends = [
        pltpu.make_async_copy(kv_all.at[:, pl.ds(512, 16), :], tails.at[pl.ds(0, 16)], own_sem.at[0]),
        pltpu.make_async_copy(q_all.at[pl.ds(512, 16), :], tails.at[16], own_sem.at[1]),
    ]
    for copy in ends:
        copy.start()
    for dx in range(1, 4):
        for p in range(2):
            shard, piece = (x + dx) % 4, 2 * (1 - c) + p
            take(w_all.at[shard, piece], w_sem.at[shard, piece])
    for copy in ends:
        copy.wait()
    rows = tails[0:16].astype(F32)[:, 0, :].astype(jnp.int32)
    tail_ref[0:16, :] = rows[:, 0:128]
    tail_ref[16:32, :] = rows[:, 128:256]
    rows = tails[16].astype(F32)[0:8, :].astype(jnp.int32)
    tail_ref[32:33, :] = rows[0:1, 0:128]
    tail_ref[33:34, :] = rows[0:1, 128:256]
    tail_ref[34:35, :] = rows[1:2, 0:128]
    tail_ref[35:40, :] = jnp.zeros((5, 128), jnp.int32)
    for copy in started:
        copy.wait_send()


SLOTS = 8


def attend_kernel(
    tail_ref, base_ref, starts_ref, live_ref, me_ref, q_ref, other_ref, kv_ref, o_ref, st_ref,
    buf, sem, q_rows, top, total, acc, scores0, scores1, probs0, probs1, keep0, keep1,
    table, sorted_run, sorted_entry, before,
):
    me = me_ref[0]
    my_y = (me // 2) % 2
    other = me + 2 - 4 * my_y
    all_scores, all_probs, all_keep = (scores0, scores1), (probs0, probs1), (keep0, keep1)
    q_run = [base_ref[0] // 256, base_ref[256] // 256, tail_ref[32, 0], tail_ref[33, 0]]

    def clear(i, carry):
        table[i] = -1
        return carry

    def enter(i, carry):
        table[tail_ref[i, 0]] = i
        return carry

    def gather_up(i, count):
        before[i] = count
        entry = table[i]

        @pl.when(entry >= 0)
        def _():
            sorted_run[count] = i
            sorted_entry[count] = entry

        return jnp.where(entry >= 0, count + 1, count)

    lax.fori_loop(0, 64, clear, 0)
    lax.fori_loop(0, 32, enter, 0)
    before[64] = lax.fori_loop(0, 64, gather_up, 0)

    def low_of(position):
        low = starts_ref[0]
        for r in range(1, REQS):
            low = jnp.where(starts_ref[r] <= position, starts_ref[r], low)
        return low

    lasts, shifts, offsets = [], [], [0]
    for r in range(4):
        first = before[low_of(q_run[r] * 256) // 256]
        lasts.append(low_of(q_run[r] * 256 + 255))
        shifts.append(first - offsets[-1])
        offsets.append(offsets[-1] + before[q_run[r] + 1] - first)
    n = offsets[4]

    def choose(i, values):
        out = values[0]
        for r in range(1, 4):
            out = jnp.where(i >= offsets[r], values[r], out)
        return out

    def half(i):
        return choose(i, [0, 1, 2, 3])

    def place(i):
        return jnp.clip(i + choose(i, shifts), 0, 31)

    def key_run(i):
        return sorted_run[place(i)]

    def fetch(i):
        entry = sorted_entry[place(i)]
        slot = i % SLOTS
        return pltpu.make_async_copy(
            kv_ref.at[entry % 16, pl.ds((entry // 16) * 256, 256), :], buf.at[slot], sem.at[slot]
        )

    for i in range(SLOTS - 2):

        @pl.when(i < n)
        def _():
            fetch(i).start()

    for r in range(4):
        source = q_ref if r < 2 else other_ref
        for h in range(2):
            q_rows[r, pl.ds(h * 256, 256), :] = source[
                pl.ds((r % 2) * 256, 256), pl.ds(h * 128, 128)
            ]
    top[...] = jnp.full_like(top, neg_fill)
    total[...] = jnp.zeros_like(total)
    acc[...] = jnp.zeros_like(acc)
    buf[SLOTS - 1] = jnp.zeros((256, 256), BF16)
    probs1[...] = jnp.zeros_like(probs1)
    keep1[...] = jnp.ones_like(keep1)

    def score(i, into):
        into[...] = lax.dot_general(
            buf[i % SLOTS, :, 0:128], q_rows[half(i)],
            (((1,), (1,)), ((), ())), preferred_element_type=F32,
        )

    def collect(i, parity):
        r = half(i)
        added = lax.dot_general(
            buf[(i + SLOTS) % SLOTS, :, 128:256], all_probs[parity][...],
            (((0,), (0,)), ((), ())), preferred_element_type=F32,
        )
        acc[r] = acc[r] * all_keep[parity][...] + added

    def weigh(i, parity, masked, base):
        r = half(i)
        scores = all_scores[parity][...]
        if masked:
            lane = lax.broadcasted_iota(jnp.int32, (1, 512), 1)
            q_pos = base + (lane % 256)
            low = jnp.full((1, 512), starts_ref[0], jnp.int32)
            for req in range(1, REQS):
                low = jnp.where(starts_ref[req] <= q_pos, starts_ref[req], low)
            k_pos = key_run(i) * 256 + lax.broadcasted_iota(jnp.int32, (256, 512), 0)
            allowed = (k_pos <= q_pos) & (k_pos >= low)
            scores = jnp.where(allowed, scores, neg_fill)
        old = top[r]
        new = jnp.maximum(old, jnp.max(scores, axis=0, keepdims=True))
        probs = jnp.exp2(scores - new)
        if masked:
            probs = jnp.where(allowed, probs, 0.0)
        keep = jnp.exp2(old - new)
        top[r] = new
        total[r] = total[r] * keep + jnp.sum(probs, axis=0, keepdims=True)
        all_keep[parity][...] = keep
        all_probs[parity][...] = probs.astype(BF16)

    def stage(i, parity):
        @pl.when(i + SLOTS - 2 < n)
        def _():
            fetch(i + SLOTS - 2).start()

        @pl.when(i + 1 < n)
        def _():
            fetch(i + 1).wait()

        run = key_run(i)
        base = choose(i, q_run) * 256
        last_low = choose(i, lasts)
        slot = sorted_entry[place(i)] % 16
        block = (slot // 2) * 4 + my_y * 2 + slot % 2
        live = jnp.where(
            i < offsets[2], live_ref[(me - block + 32) % 32], tail_ref[34, (other - block + 32) % 32]
        ) > 0
        whole = (run * 256 < base) & (run * 256 >= last_low)

        @pl.when(live & whole)
        def _():
            weigh(i, parity, False, base)
            score(i + 1, all_scores[1 - parity])
            collect(i - 1, 1 - parity)

        @pl.when(live & jnp.logical_not(whole))
        def _():
            weigh(i, parity, True, base)
            score(i + 1, all_scores[1 - parity])
            collect(i - 1, 1 - parity)

        @pl.when(jnp.logical_not(live))
        def _():
            score(i + 1, all_scores[1 - parity])
            collect(i - 1, 1 - parity)
            all_keep[parity][...] = jnp.ones((1, 512), F32)
            all_probs[parity][...] = jnp.zeros((256, 512), BF16)

    def pair(k, carry):
        stage(2 * k, 0)

        @pl.when(2 * k + 1 < n)
        def _():
            stage(2 * k + 1, 1)

        return carry

    fetch(0).wait()
    score(0, scores0)
    lax.fori_loop(0, (n + 1) // 2, pair, 0)

    @pl.when(n % 2 == 1)
    def _():
        collect(n - 1, 0)

    @pl.when(n % 2 == 0)
    def _():
        collect(n - 1, 1)

    for r in range(4):
        weight = total[r]
        done = (acc[r] * jnp.where(weight > 0, 1.0 / weight, 0.0)).astype(BF16)
        for part in range(2):
            k = 2 * (r % 2) + part
            for h in range(2):
                low = h * 256 + part * 128
                o_ref[r // 2, k, h * 128 : (h + 1) * 128, :] = done[:, low : low + 128]
                st_ref[r // 2, k, h : h + 1, :] = top[r, :, low : low + 128]
                st_ref[r // 2, k, 2 + h : 3 + h, :] = weight[:, low : low + 128]


def middle_kernel(
    heads_ref, stats_ref, w_ref, w_own, tok_ref, gain_ref, wg_ref, wu_ref, wd_ref, match_ref, final_ref, head_ref,
    out_ref, rms_ref, top_ref,
    heads, stats, joined, near_send, near_got, w, tok_rows, tok_cols, wg, wu, wd, att, att_send, att_cols, normed, act, part, fwd_in,
    x_in, y_in, head, row_send, seq_got, wide_send, wide_got, last_send, last_got, max_send, seq_max, vocab_max,
    load_sem, send_sem, head_recv, stat_recv, near_recv, norm_recv, att_recv, fwd_recv, x_recv, y_recv,
    row_recv, wide_recv, last_recv, max_recv, top_recv,
):
    s = lax.axis_index("seq")
    v = lax.axis_index("vocab")
    others = [(v + r) % 8 for r in range(1, 8)]
    seqs = [(s + r) % 32 for r in range(1, 32)]
    cols = pl.ds(pl.multiple_of(v * 256, 256), 256)
    rows = pl.ds(pl.multiple_of(v * 64, 64), 64)
    loads = [
        pltpu.make_async_copy(w_own, w.at[v // 2], load_sem.at[0]),
        pltpu.make_async_copy(tok_ref.at[rows, :], tok_rows, load_sem.at[1]),
        pltpu.make_async_copy(tok_ref.at[:, cols], tok_cols, load_sem.at[2]),
        pltpu.make_async_copy(wg_ref, wg, load_sem.at[3]),
        pltpu.make_async_copy(wu_ref, wu, load_sem.at[4]),
        pltpu.make_async_copy(wd_ref, wd, load_sem.at[5]),
        pltpu.make_async_copy(heads_ref.at[0, v // 2], heads.at[v // 2, (s // 2) % 2], load_sem.at[6]),
        pltpu.make_async_copy(stats_ref.at[0, v // 2], stats.at[v // 2, (s // 2) % 2], load_sem.at[9]),
        pltpu.make_async_copy(head_ref, head, load_sem.at[8]),
    ] + [
        pltpu.make_async_copy(
            w_ref.at[(v // 2 + d) % 4], w.at[(v // 2 + d) % 4], load_sem.at[9 + d]
        )
        for d in range(1, 4)
    ]
    for copy in loads:
        copy.start()
    x = v // 2
    y = v % 2
    my_y = (s // 2) % 2
    across = seq_at(s, 0, 1, 0)
    greet(
        [(s, other) for other in others]
        + [(other, v) for other in seqs]
        + [(across, vocab_at(v, dx, 0)) for dx in range(1, 4)]
    )
    sent = []

    def go(src, dst, recv, peer):
        copy = pltpu.make_async_remote_copy(
            src_ref=src, dst_ref=dst, send_sem=send_sem.at[len(sent)], recv_sem=recv,
            device_id=peer, device_id_type=MESH,
        )
        copy.start()
        sent.append(copy)

    def take(dst, recv):
        pltpu.make_async_remote_copy(
            src_ref=dst, dst_ref=dst, send_sem=send_sem.at[0], recv_sem=recv,
            device_id=(s, others[0]), device_id_type=MESH,
        ).wait_recv()

    for dx in (2, 1, 3, 0):
        target = (x + dx) % 4
        for which in (1, 0):
            if (dx, which) != (0, 0):
                peer = (across if which else s, vocab_at(v, dx, 0))
                go(heads_ref.at[which, target], heads.at[x, my_y], head_recv.at[x, my_y], peer)
                go(stats_ref.at[which, target], stats.at[x, my_y], stat_recv.at[x, my_y], peer)
    for i in (0, 1, 6, 7, 9, 10, 11):
        loads[i].wait()
    for dx in range(4):
        source = (x + dx) % 4
        for which in range(2):
            if (dx, which) != (0, 0):
                held = (my_y + which) % 2
                take(heads.at[source, held], head_recv.at[source, held])
                take(stats.at[source, held], stat_recv.at[source, held])
    for k in range(4):
        for h in range(2):
            tops = [stats[k, i, h : h + 1, :] for i in range(2)]
            best = jnp.maximum(tops[0], tops[1])
            weights = [stats[k, i, 2 + h : 3 + h, :] * jnp.exp2(tops[i] - best) for i in range(2)]
            scale = 1.0 / (weights[0] + weights[1])
            span = pl.ds(h * 128, 128)
            joined[k, span, :] = (
                heads[k, 0, span, :].astype(F32) * (weights[0] * scale)
                + heads[k, 1, span, :].astype(F32) * (weights[1] * scale)
            ).astype(BF16)

    near = vocab_at(v, 0, 1)
    for j in range(4):
        total = jnp.zeros((128, 512), F32)
        for k in range(4):
            total += lax.dot_general(
                joined[k], w[k, :, j * 512 : (j + 1) * 512],
                (((0,), (0,)), ((), ())), preferred_element_type=F32,
            )
        att[:, j * 512 : (j + 1) * 512] = jnp.where(y == 0, total[0:64], total[64:128])
        near_send[j] = jnp.where(y == 0, total[64:128], total[0:64]).astype(BF16)
        go(near_send.at[j], near_got.at[j], near_recv.at[j], (s, near))
    for j in range(4):
        take(near_got.at[j], near_recv.at[j])

    def project(j, square):
        wide = pl.ds(pl.multiple_of(j * 512, 512), 512)
        total = att[:, wide] + near_got[j].astype(F32)
        att_send[2 * j] = total[:, 0:256].astype(BF16)
        att_send[2 * j + 1] = total[:, 256:512].astype(BF16)
        residual = tok_rows[:, wide].astype(F32) + total
        att[:, wide] = residual
        return square + jnp.sum(residual * residual, axis=-1, keepdims=True)

    square = lax.fori_loop(0, 4, project, jnp.zeros((64, 1), F32))
    gain = wide_row(gain_ref)
    mine = (att[...] * lax.rsqrt(square / 2048 + epsilon) * gain).astype(BF16)
    normed[2 * v] = mine[0:32]
    normed[2 * v + 1] = mine[32:64]

    right, left = vocab_at(v, 1, 0), vocab_at(v, -1, 0)

    def pass_on(owner, p, other):
        view = normed.at[2 * owner + p]
        go(view, view, norm_recv.at[owner, p], (s, other))

    def arrive(dx, dy, p, peers):
        owner = vocab_at(v, dx, dy)
        take(normed.at[2 * owner + p], norm_recv.at[owner, p])
        for peer in peers:
            pass_on(owner, p, peer)

    for other in others:
        go(att_send.at[other], att_cols.at[v], att_recv.at[v], (s, other))
    for p in range(2):
        for peer in (right, left, near):
            pass_on(v, p, peer)
    own_cols = pltpu.make_async_copy(att_send.at[v], att_cols.at[v], load_sem.at[7])
    own_cols.start()

    loads[2].wait()
    own_cols.wait()
    for other in others:
        take(att_cols.at[other], att_recv.at[other])
    picked = jnp.zeros((8, 256), F32)
    for i in range(8):
        residual = tok_cols[i * 64 : (i + 1) * 64, :].astype(F32) + att_cols[i].astype(F32)
        high = residual.astype(BF16)
        low = (residual - high.astype(F32)).astype(BF16)
        picked += jnp.dot(match_ref[i], high, preferred_element_type=F32)
        picked += jnp.dot(match_ref[i], low, preferred_element_type=F32)
    row_send[...] = picked
    seq_got[s] = picked
    for other in seqs:
        go(row_send, seq_got.at[s], row_recv.at[s], (other, v))

    for p in range(2):
        arrive(-1, 0, p, (right,) if p == 0 else ())
        arrive(1, 0, p, (left,) if p == 1 else ())
        arrive(0, 1, p, (right, left))

    for i in (3, 4, 5):
        loads[i].wait()
    def feed(values):
        gate = jnp.dot(values, wg[...], preferred_element_type=F32)
        upward = jnp.dot(values, wu[...], preferred_element_type=F32)
        return (gate / (1.0 + jnp.exp(-gate)) * upward).astype(BF16)

    def part_of(chunk, dx, dy):
        return part.at[chunk, vocab_at(v, dx, dy)]

    def at_y(chunk, dx, lane):
        return part.at[chunk, ((x + dx + 4) % 4) * 2 + lane]

    def rows_of(dx, extra):
        chunk = (x + dx + 4) % 4
        values = normed[pl.ds(4 * chunk, 4)].reshape(128, 2048)
        if extra:
            values = jnp.concatenate([values, normed[16]], axis=0)
        active = feed(values)
        if extra:
            act[...] = active[128:144]
            active = active[0:128]
        for t in range(8):
            part[chunk, t] = jnp.dot(
                active, wd[:, t * 256 : (t + 1) * 256], preferred_element_type=F32
            ).astype(BF16)
        go(at_y(chunk, 2, 0), fwd_in.at[chunk, 0], fwd_recv.at[chunk, 0], (s, right))
        go(at_y(chunk, 2, 1), fwd_in.at[chunk, 1], fwd_recv.at[chunk, 1], (s, left))
        go(at_y(chunk, 1, 1), x_in.at[chunk, 0, 1], x_recv.at[chunk, 0, 1], (s, right))
        go(at_y(chunk, -1, 0), x_in.at[chunk, 1, 0], x_recv.at[chunk, 1, 0], (s, left))

    rows_of(0, False)
    for other in seqs:
        take(seq_got.at[other], row_recv.at[other])
    picked = jnp.sum(seq_got[...], axis=0)
    wide_send[...] = picked
    wide_got[v] = picked
    for other in others:
        go(wide_send, wide_got.at[v], wide_recv.at[v], (s, other))

    for p in range(2):
        arrive(2, 0, p, (near,))
    for p in range(2):
        arrive(-1, 1, p, ())
        arrive(1, 1, p, ())
    rows_of(-1, False)
    for other in others:
        take(wide_got.at[other], wide_recv.at[other])
    square = jnp.zeros((8, 1), F32)
    for k in range(8):
        square += jnp.sum(wide_got[k] * wide_got[k], axis=-1, keepdims=True)
    inverse = lax.rsqrt(square / 2048 + epsilon)
    normed[16, 16:32, :] = jnp.zeros((16, 2048), BF16)
    for k in range(8):
        one = wide_got[k] * inverse * gain[:, k * 256 : (k + 1) * 256]
        normed[16, 0:16, k * 256 : (k + 1) * 256] = jnp.concatenate([one, one], axis=0).astype(BF16)
    rows_of(1, True)

    group = lax.broadcasted_iota(jnp.int32, (16, 512), 0) // 4

    def packed(quarter):
        out = quarter(0)
        for q in range(1, 4):
            out = jnp.where(group == q, quarter(q), out)
        return out

    last = act[...]
    mine = packed(
        lambda q: jnp.dot(
            last, wd[:, q * 512 : (q + 1) * 512], preferred_element_type=F32
        )
    ).astype(BF16)
    last_send[...] = mine
    last_got[v] = mine
    for other in others:
        go(last_send, last_got.at[v], last_recv.at[v], (s, other))
    for p in range(2):
        arrive(2, 1, p, ())
    rows_of(2, False)

    def add_to(ref, *incoming):
        value = ref[...].astype(F32)
        for one in incoming:
            value += one[...].astype(F32)
        ref[...] = value.astype(BF16)

    def onward(dx, way):
        chunk = (x + dx + 4) % 4
        take(fwd_in.at[chunk, way], fwd_recv.at[chunk, way])
        ref = at_y(chunk, 1 if way == 0 else -1, way)
        add_to(ref, fwd_in.at[chunk, way])
        go(ref, x_in.at[chunk, way, way], x_recv.at[chunk, way, way], (s, right if way == 0 else left))

    for to_right, to_left in ((-1, 1), (2, 0), (0, 2), (1, -1)):
        onward(to_right, 0)
        onward(to_left, 1)

    for other in others:
        take(last_got.at[other], last_recv.at[other])

    def quarter_rows(q):
        one = jnp.concatenate([wide_got[2 * q], wide_got[2 * q + 1]], axis=1)
        return jnp.concatenate([one, one], axis=0)

    total = last_got[0].astype(F32)
    for k in range(1, 8):
        total += last_got[k].astype(F32)
    final = (packed(quarter_rows) + total).astype(BF16).astype(F32)
    square = jnp.broadcast_to(jnp.sum(final * final, axis=-1, keepdims=True), (16, 128))
    square = square + pltpu.roll(square, 8, axis=0)
    square = square + pltpu.roll(square, 4, axis=0)
    mean_square = square / 2048 + epsilon
    diagonal = lax.broadcasted_iota(jnp.int32, (16, 128), 0) == lax.broadcasted_iota(
        jnp.int32, (16, 128), 1
    )

    def along_lanes(value):
        return jnp.sum(jnp.where(diagonal, value, 0.0), axis=0, keepdims=True)

    rms_ref[...] = along_lanes(jnp.sqrt(mean_square))[:, :REQS]
    inverse = lax.rsqrt(mean_square)[:, 0:1]
    last_gain = wide_row(final_ref)
    spread = packed(
        lambda q: jnp.broadcast_to(last_gain[:, q * 512 : (q + 1) * 512], (16, 512))
    )
    final = final * inverse * spread
    loads[8].wait()
    logits = jnp.zeros((16, 360), F32)
    for q in range(4):
        turned = final if q == 0 else pltpu.roll(final, 16 - 4 * q, axis=0)
        logits += lax.dot_general(
            turned.astype(BF16), head[:, q * 512 : (q + 1) * 512], (((1,), (1,)), ((), ())),
            preferred_element_type=F32,
        )
    best = along_lanes(jnp.broadcast_to(jnp.max(logits, axis=-1, keepdims=True), (16, 128)))
    best = jnp.broadcast_to(best, (8, 128))
    max_send[0] = best
    seq_max[s] = best
    for other in seqs:
        go(max_send.at[0], seq_max.at[s], max_recv.at[s], (other, v))
    for dx in (0, -1, 1, 2):
        chunk = (x + dx + 4) % 4
        for way in range(2):
            take(x_in.at[chunk, way, 1 - y], x_recv.at[chunk, way, 1 - y])
        ref = part_of(chunk, 0, 1)
        add_to(ref, x_in.at[chunk, 0, 1 - y], x_in.at[chunk, 1, 1 - y])
        go(ref, y_in.at[chunk], y_recv.at[chunk], (s, near))

    for other in seqs:
        take(seq_max.at[other], max_recv.at[other])
    best = jnp.max(seq_max[...], axis=0)
    max_send[1] = best
    vocab_max[v] = best
    for other in others:
        go(max_send.at[1], vocab_max.at[v], top_recv.at[v], (s, other))

    for dx in (0, -1, 1, 2):
        chunk = (x + dx + 4) % 4
        for way in range(2):
            take(x_in.at[chunk, way, y], x_recv.at[chunk, way, y])
        take(y_in.at[chunk], y_recv.at[chunk])
        rows = pl.ds(pl.multiple_of(chunk * 128, 128), 128)
        total = tok_cols[rows, :].astype(F32)
        total += att_cols[pl.ds(2 * chunk, 2)].reshape(128, 256).astype(F32)
        total += part[chunk, v].astype(F32)
        total += x_in[chunk, 0, y].astype(F32)
        total += x_in[chunk, 1, y].astype(F32)
        total += y_in[chunk].astype(F32)
        out_ref[rows, :] = total.astype(BF16)
    for other in others:
        take(vocab_max.at[other], top_recv.at[other])
    top_ref[...] = jnp.max(vocab_max[...], axis=0)[0:1, :REQS]
    for copy in sent:
        copy.wait_send()


def hand_over_kernel(hidden_ref, rms_ref, top_ref, hidden_out, rms_out, top_out):
    hidden_out[...] = hidden_ref[...]
    rms_out[...] = rms_ref[...]
    top_out[...] = top_ref[...]


def per_device(
    tokens,
    attention_gain,
    query_weight,
    key_weight,
    value_weight,
    out_weight,
    forward_gain,
    gate_weight,
    up_weight,
    down_weight,
    final_gain,
    head_weight,
    segment_ids,
    token_order,
    live_blocks,
    cache_slots,
):
    shape = jax.ShapeDtypeStruct
    me = lax.axis_index("seq").astype(jnp.int32)
    request = jnp.arange(8, dtype=jnp.int32)
    starts = jnp.sum((segment_ids[None, :] < request[:, None]).astype(jnp.int32), axis=1)
    delta = (token_order[::256][:, None] - starts[None, :REQS]).reshape(8, 1).astype(F32)
    angle = delta * jnp.asarray(FREQUENCY.astype(np.float32))[None, :]

    query, cache, match, kv_all, q_other, w_all, tail = pl.pallas_call(
        gather_kernel,
        out_shape=(
            shape((528, 256), BF16), shape((512, 256), BF16), shape((8, 8, 64), BF16),
            shape((16, 528, 256), BF16), shape((528, 256), BF16), shape((4, 4, 64, 2048), BF16),
            shape((40, 128), jnp.int32),
        ),
        in_specs=[SM] * 3 + [VM] * 10 + [HB],
        out_specs=(VM, VM, VM, HB, HB, HB, VM),
        scratch_shapes=[
            pltpu.VMEM((528, 256), BF16),
            pltpu.VMEM((512, 2048), BF16),
            pltpu.VMEM((512, 128), F32),
            pltpu.VMEM((512, 128), F32),
            pltpu.VMEM((17, 16, 256), BF16),
            pltpu.SemaphoreType.DMA((2,)),
            pltpu.SemaphoreType.DMA((128,)),
            pltpu.SemaphoreType.DMA((16, 4)),
            pltpu.SemaphoreType.DMA((1,)),
            pltpu.SemaphoreType.DMA((4, 4)),
        ],
        compiler_params=params(0),
        name="gather",
    )(
        token_order, starts, live_blocks[0], tokens, attention_gain.reshape(16, 128), query_weight,
        key_weight, value_weight, jnp.asarray(STEP_COS), jnp.asarray(STEP_SIN), jnp.cos(angle),
        jnp.sin(angle), cache_slots[None], out_weight.reshape(4, 64, 2048),
    )

    heads, stats = pl.pallas_call(
        attend_kernel,
        out_shape=(shape((2, 4, 256, 128), BF16), shape((2, 4, 8, 128), F32)),
        in_specs=[SM] * 5 + [VM, VM, HB],
        out_specs=(VM, VM),
        scratch_shapes=[
            pltpu.VMEM((SLOTS, 256, 256), BF16),
            pltpu.SemaphoreType.DMA((SLOTS,)),
            pltpu.VMEM((4, 512, 128), BF16),
            pltpu.VMEM((4, 1, 512), F32),
            pltpu.VMEM((4, 1, 512), F32),
            pltpu.VMEM((4, 128, 512), F32),
            pltpu.VMEM((256, 512), F32),
            pltpu.VMEM((256, 512), F32),
            pltpu.VMEM((256, 512), BF16),
            pltpu.VMEM((256, 512), BF16),
            pltpu.VMEM((1, 512), F32),
            pltpu.VMEM((1, 512), F32),
            pltpu.SMEM((64,), jnp.int32),
            pltpu.SMEM((32,), jnp.int32),
            pltpu.SMEM((32,), jnp.int32),
            pltpu.SMEM((65,), jnp.int32),
        ],
        compiler_params=params(),
        name="attend",
    )(tail, token_order, starts, live_blocks[0], me[None], query, q_other, kv_all)

    dma = pltpu.SemaphoreType.DMA
    hidden, rms, top = pl.pallas_call(
        middle_kernel,
        out_shape=(shape((512, 256), BF16), shape((1, REQS), F32), shape((1, REQS), F32)),
        in_specs=[VM, VM, HB, HB, HB, VM, HB, HB, HB, VM, VM, HB],
        out_specs=(VM, VM, VM),
        scratch_shapes=[
            pltpu.VMEM((4, 2, 256, 128), BF16),
            pltpu.VMEM((4, 2, 8, 128), F32),
            pltpu.VMEM((4, 256, 128), BF16),
            pltpu.VMEM((4, 64, 512), BF16),
            pltpu.VMEM((4, 64, 512), BF16),
            pltpu.VMEM((4, 256, 2048), BF16),
            pltpu.VMEM((64, 2048), BF16),
            pltpu.VMEM((512, 256), BF16),
            pltpu.VMEM((2048, 512), BF16),
            pltpu.VMEM((2048, 512), BF16),
            pltpu.VMEM((512, 2048), BF16),
            pltpu.VMEM((64, 2048), F32),
            pltpu.VMEM((8, 64, 256), BF16),
            pltpu.VMEM((8, 64, 256), BF16),
            pltpu.VMEM((17, 32, 2048), BF16),
            pltpu.VMEM((16, 512), BF16),
            pltpu.VMEM((4, 8, 128, 256), BF16),
            pltpu.VMEM((4, 2, 128, 256), BF16),
            pltpu.VMEM((4, 2, 2, 128, 256), BF16),
            pltpu.VMEM((4, 128, 256), BF16),
            pltpu.VMEM((360, 2048), BF16),
            pltpu.VMEM((8, 256), F32),
            pltpu.VMEM((32, 8, 256), F32),
            pltpu.VMEM((8, 256), F32),
            pltpu.VMEM((8, 8, 256), F32),
            pltpu.VMEM((16, 512), BF16),
            pltpu.VMEM((8, 16, 512), BF16),
            pltpu.VMEM((2, 8, 128), F32),
            pltpu.VMEM((32, 8, 128), F32),
            pltpu.VMEM((8, 8, 128), F32),
            dma((13,)), dma((192,)), dma((4, 2)), dma((4, 2)), dma((4,)), dma((8, 2)), dma((8,)), dma((4, 2)), dma((4, 2, 2)), dma((4,)),
            dma((32,)), dma((8,)), dma((8,)), dma((32,)), dma((8,)),
        ],
        compiler_params=params(1),
        name="middle",
    )(
        heads, stats, w_all.reshape(4, 256, 2048), out_weight, tokens, forward_gain.reshape(16, 128), gate_weight, up_weight,
        down_weight, match, final_gain.reshape(16, 128), head_weight,
    )
    hidden, rms, top = pl.pallas_call(
        hand_over_kernel,
        out_shape=(shape((512, 256), BF16), shape((1, REQS), F32), shape((1, REQS), F32)),
        in_specs=[VM, VM, VM],
        out_specs=(VM, VM, VM),
        compiler_params=params(),
        name="hand_over",
    )(hidden, rms, top)
    return (hidden, cache.reshape(512, 2, 128), rms.reshape(REQS), top.reshape(REQS))


def solution(mesh):
    return jax.shard_map(
        per_device,
        mesh=mesh,
        in_specs=(
            P("seq", None),
            P(),
            P(None, "vocab"),
            P(None, "vocab"),
            P(None, "vocab"),
            P("vocab", None),
            P(),
            P(None, "vocab"),
            P(None, "vocab"),
            P("vocab", None),
            P(),
            P(("seq", "vocab"), None),
            P(),
            P("seq"),
            P("seq", None),
            P("seq"),
        ),
        out_specs=(P("seq", "vocab"), P("seq", None, "vocab"), P(), P()),
        check_vma=False,
    )
```

```python
import functools

import jax
import jax.numpy as jnp
import numpy as np
from jax import lax
from jax.experimental import pallas as pl
from jax.experimental.pallas import tpu as pltpu
from jax.sharding import PartitionSpec as P

MESH = pl.DeviceIdType.MESH
HD = 128
REQS = 4
epsilon = 1e-06
rope_base = 1000000.0
neg_fill = -1e30
VM = pl.BlockSpec(memory_space=pltpu.VMEM)
SM = pl.BlockSpec(memory_space=pltpu.SMEM)
HB = pl.BlockSpec(memory_space=pl.ANY)
F32 = jnp.float32
BF16 = jnp.bfloat16
LIMIT = 62 * 1024 * 1024
SCALE = HD ** (-0.5) * 1.4426950408889634


def params(cid=None):
    if cid is None:
        return pltpu.CompilerParams(vmem_limit_bytes=LIMIT)
    return pltpu.CompilerParams(
        collective_id=cid, has_side_effects=True, vmem_limit_bytes=LIMIT
    )


def seq_at(s, dz, dy, dc):
    z, y, c = s // 4, (s // 2) % 2, s % 2
    return ((z + dz + 8) % 8) * 4 + ((y + dy) % 2) * 2 + (c + dc) % 2


def vocab_at(v, dx, dy):
    x, y = v // 2, v % 2
    return ((x + dx + 4) % 4) * 2 + (y + dy) % 2


def wide_row(ref):
    rows = ref[...].astype(F32)
    return jnp.concatenate([rows[i : i + 1] for i in range(16)], axis=1)


def greet(peers):
    barrier = pltpu.get_barrier_semaphore()
    for peer in peers:
        pl.semaphore_signal(barrier, inc=1, device_id=peer, device_id_type=MESH)
    pl.semaphore_wait(barrier, len(peers))


FREQUENCY = rope_base ** (-(np.arange(128) % 64) * 2.0 / 128)
STEP_COS = np.cos(np.arange(256)[:, None] * FREQUENCY[None, :]).astype(np.float32)
STEP_SIN = np.sin(np.arange(256)[:, None] * FREQUENCY[None, :]).astype(np.float32)
FAR_COS = np.cos(256 * np.arange(64)[:, None] * FREQUENCY[None, :]).astype(np.float32)
FAR_SIN = np.sin(256 * np.arange(64)[:, None] * FREQUENCY[None, :]).astype(np.float32)


PIECE_ROWS = ((0, 128), (128, 128), (256, 128), (384, 144))


def gather_kernel(
    base_ref, starts_ref, live_ref, tok_ref, gain_ref, wq_ref, wk_ref, wv_ref,
    step_cos, step_sin, far_cos, far_sin, slot_ref, w_ref,
    q_ref, cache_ref, match_ref, kv_all, q_all, w_all, tail_ref,
    kv_ref, normed, cosines, sines, tails, own_sem, send_sem, kv_sem, q_sem, w_sem,
):
    s = lax.axis_index("seq")
    v = lax.axis_index("vocab")
    z, c, x = s // 4, s % 2, v // 2
    up = (seq_at(s, 1, 0, 0), v)
    down = (seq_at(s, -1, 0, 0), v)
    side = (seq_at(s, 0, 1, 0), v)
    core = (seq_at(s, 0, 0, 1), v)
    right = (s, vocab_at(v, 1, 0))
    left = (s, vocab_at(v, -1, 0))
    barrier = pltpu.get_barrier_semaphore()
    for peer in (up, down, side, core, right, left):
        pl.semaphore_signal(barrier, inc=1, device_id=peer, device_id_type=MESH)
    gain = wide_row(gain_ref)
    lane = lax.broadcasted_iota(jnp.int32, (128, 128), 1)

    def turn(u, i):
        rows = pl.ds(i * 128, 128)
        return u * cosines[rows, :] + pltpu.roll(u, 64, axis=1) * sines[rows, :]

    def keys_values(i):
        rows = pl.ds(i * 128, 128)
        values = tok_ref[rows, :].astype(F32)
        scale = lax.rsqrt(jnp.mean(values * values, axis=-1, keepdims=True) + epsilon)
        values = (values * scale * gain).astype(BF16)
        normed[rows, :] = values
        r = i // 2
        steps = pl.ds((i % 2) * 128, 128)
        order = base_ref[r * 256] + (i % 2) * 128 + lax.broadcasted_iota(jnp.int32, (128, 128), 0)
        for req in range(REQS):
            start = starts_ref[req]
            runs = jnp.maximum(base_ref[r * 256] // 256 - start // 256, 0)
            far_c, far_s = far_cos[pl.ds(runs, 1), :], far_sin[pl.ds(runs, 1), :]
            off_c, off_s = step_cos[pl.ds(start % 256, 1), :], step_sin[pl.ds(start % 256, 1), :]
            run_c = jnp.broadcast_to(far_c * off_c + far_s * off_s, (128, 128))
            run_s = jnp.broadcast_to(far_s * off_c - far_c * off_s, (128, 128))
            later = order >= start
            near_cos = jnp.where(later, run_c, near_cos) if req else run_c
            near_sin = jnp.where(later, run_s, near_sin) if req else run_s
        cosines[rows, :] = step_cos[steps, :] * near_cos - step_sin[steps, :] * near_sin
        sine = step_sin[steps, :] * near_cos + step_cos[steps, :] * near_sin
        sines[rows, :] = jnp.where(lane < 64, -sine, sine)
        key = jnp.dot(values, wk_ref[...], preferred_element_type=F32)
        kv_ref[rows, 0:128] = turn(key, i).astype(BF16)
        value = jnp.dot(values, wv_ref[...], preferred_element_type=F32)
        kv_ref[rows, 128:256] = value.astype(BF16)

    half = lax.broadcasted_iota(jnp.int32, (16, 256), 1)
    run = jnp.where(half < 128, base_ref[0] // 256, base_ref[256] // 256).astype(F32)
    kv_ref[512:528, :] = run.astype(BF16)
    keys_values(0)
    pl.semaphore_wait(barrier, 6)
    started = []

    def go(src, dst, recv, peer):
        copy = pltpu.make_async_remote_copy(
            src_ref=src, dst_ref=dst, send_sem=send_sem.at[len(started)], recv_sem=recv,
            device_id=peer, device_id_type=MESH,
        )
        copy.start()
        started.append(copy)

    def take(dst, recv):
        pltpu.make_async_remote_copy(
            src_ref=dst, dst_ref=dst, send_sem=send_sem.at[0], recv_sem=recv,
            device_id=core, device_id_type=MESH,
        ).wait_recv()

    def kv_view(block, p):
        low, count = PIECE_ROWS[p]
        return kv_all.at[block, pl.ds(low, count), :]

    def kv_take(dz, p, peers):
        block = ((z + dz + 8) % 8) * 2 + c
        take(kv_view(block, p), kv_sem.at[block, p])
        for peer in peers:
            go(kv_view(block, p), kv_view(block, p), kv_sem.at[block, p], peer)

    def w_take(dx, p, peers):
        shard, piece = (x + dx + 4) % 4, 2 * c + p
        take(w_all.at[shard, piece], w_sem.at[shard, piece])
        for peer in peers:
            go(w_all.at[shard, piece], w_all.at[shard, piece], w_sem.at[shard, piece], peer)

    mine = z * 2 + c
    for p in range(4):
        if p:
            keys_values(p)
        low, count = PIECE_ROWS[p]
        for peer in (up, down, core):
            go(kv_ref.at[pl.ds(low, count), :], kv_view(mine, p), kv_sem.at[mine, p], peer)
        if p < 2:
            piece = 2 * c + p
            for peer in (right, left):
                go(w_ref.at[piece], w_all.at[x, piece], w_sem.at[x, piece], peer)
    own = pltpu.make_async_copy(kv_ref, kv_all.at[mine], own_sem.at[0])
    own.start()
    for p in range(4):
        rows = pl.ds(p * 128, 128)
        query = jnp.dot(normed[rows, :], wq_ref[...], preferred_element_type=F32)
        q_ref[rows, 0:128] = (turn(query[:, 0:128], p) * SCALE).astype(BF16)
        q_ref[rows, 128:256] = (turn(query[:, 128:256], p) * SCALE).astype(BF16)
    row = lax.broadcasted_iota(jnp.int32, (16, 256), 0)
    for i in range(32):
        run = jnp.where((row == 1) & (half == i), live_ref[i].astype(F32), run)
    q_ref[512:528, :] = run.astype(BF16)
    go(q_ref, q_all, q_sem.at[0], side)

    for d in (1, 2):
        for p in range(4):
            kv_take(-d, p, (up, core))
            kv_take(d, p, (down, core))
        if d == 1:
            w_take(-1, 0, (right, core))
            w_take(1, 0, (core,))
    w_take(-1, 1, (core,))
    w_take(1, 1, (left, core))
    slots = slot_ref[...]
    for i in range(4):
        row = i * 128 + lax.broadcasted_iota(jnp.int32, (128, 512), 0)
        pick = jnp.where(row == slots, 1.0, 0.0).astype(BF16)
        moved = jnp.dot(pick, kv_ref[0:512, :], preferred_element_type=F32)
        cache_ref[i * 128 : (i + 1) * 128, :] = moved.astype(BF16)
    request = lax.broadcasted_iota(jnp.int32, (8, 64), 0) % REQS
    last = jnp.full((8, 64), starts_ref[1] - 1, jnp.int32)
    for req in range(1, REQS):
        last = jnp.where(request == req, starts_ref[req + 1] - 1, last)
    for i in range(8):
        order = base_ref[256 * (i // 4)] + (i % 4) * 64 + lax.broadcasted_iota(jnp.int32, (8, 64), 1)
        match_ref[i] = jnp.where(order == last, 1.0, 0.0).astype(BF16)
    for p in range(4):
        kv_take(-3, p, (up, core) if p < 2 else (core,))
        kv_take(3, p, (down, core) if p >= 2 else (core,))
    for p in range(2):
        w_take(2, p, (core,))
    for p in range(4):
        kv_take(4, p, (core,))

    for dz in range(8):
        for p in range(4):
            block = ((z + dz) % 8) * 2 + 1 - c
            take(kv_view(block, p), kv_sem.at[block, p])
    take(q_all, q_sem.at[0])
    own.wait()
    ends = [
        pltpu.make_async_copy(kv_all.at[:, pl.ds(512, 16), :], tails.at[pl.ds(0, 16)], own_sem.at[0]),
        pltpu.make_async_copy(q_all.at[pl.ds(512, 16), :], tails.at[16], own_sem.at[1]),
    ]
    for copy in ends:
        copy.start()
    for dx in range(1, 4):
        for p in range(2):
            shard, piece = (x + dx) % 4, 2 * (1 - c) + p
            take(w_all.at[shard, piece], w_sem.at[shard, piece])
    for copy in ends:
        copy.wait()
    rows = tails[0:16].astype(F32)[:, 0, :].astype(jnp.int32)
    tail_ref[0:16, :] = rows[:, 0:128]
    tail_ref[16:32, :] = rows[:, 128:256]
    rows = tails[16].astype(F32)[0:8, :].astype(jnp.int32)
    tail_ref[32:33, :] = rows[0:1, 0:128]
    tail_ref[33:34, :] = rows[0:1, 128:256]
    tail_ref[34:35, :] = rows[1:2, 0:128]
    tail_ref[35:40, :] = jnp.zeros((5, 128), jnp.int32)
    for copy in started:
        copy.wait_send()


SLOTS = 8


def attend_kernel(
    tail_ref, base_ref, starts_ref, live_ref, me_ref, q_ref, other_ref, kv_ref, o_ref, st_ref,
    buf, sem, q_rows, top, total, acc, scores0, scores1, probs0, probs1, keep0, keep1,
    table, sorted_run, sorted_entry, before,
):
    me = me_ref[0]
    my_y = (me // 2) % 2
    other = me + 2 - 4 * my_y
    all_scores, all_probs, all_keep = (scores0, scores1), (probs0, probs1), (keep0, keep1)
    q_run = [base_ref[0] // 256, base_ref[256] // 256, tail_ref[32, 0], tail_ref[33, 0]]

    def clear(i, carry):
        table[i] = -1
        return carry

    def enter(i, carry):
        table[tail_ref[i, 0]] = i
        return carry

    def gather_up(i, count):
        before[i] = count
        entry = table[i]

        @pl.when(entry >= 0)
        def _():
            sorted_run[count] = i
            sorted_entry[count] = entry

        return jnp.where(entry >= 0, count + 1, count)

    lax.fori_loop(0, 64, clear, 0)
    lax.fori_loop(0, 32, enter, 0)
    before[64] = lax.fori_loop(0, 64, gather_up, 0)

    def low_of(position):
        low = starts_ref[0]
        for r in range(1, REQS):
            low = jnp.where(starts_ref[r] <= position, starts_ref[r], low)
        return low

    lasts, shifts, offsets = [], [], [0]
    for r in range(4):
        first = before[low_of(q_run[r] * 256) // 256]
        lasts.append(low_of(q_run[r] * 256 + 255))
        shifts.append(first - offsets[-1])
        offsets.append(offsets[-1] + before[q_run[r] + 1] - first)
    n = offsets[4]

    def choose(i, values):
        out = values[0]
        for r in range(1, 4):
            out = jnp.where(i >= offsets[r], values[r], out)
        return out

    def half(i):
        return choose(i, [0, 1, 2, 3])

    def place(i):
        return jnp.clip(i + choose(i, shifts), 0, 31)

    def key_run(i):
        return sorted_run[place(i)]

    def fetch(i):
        entry = sorted_entry[place(i)]
        slot = i % SLOTS
        return pltpu.make_async_copy(
            kv_ref.at[entry % 16, pl.ds((entry // 16) * 256, 256), :], buf.at[slot], sem.at[slot]
        )

    for i in range(SLOTS - 2):

        @pl.when(i < n)
        def _():
            fetch(i).start()

    for r in range(4):
        source = q_ref if r < 2 else other_ref
        for h in range(2):
            q_rows[r, pl.ds(h * 256, 256), :] = source[
                pl.ds((r % 2) * 256, 256), pl.ds(h * 128, 128)
            ]
    top[...] = jnp.full_like(top, neg_fill)
    total[...] = jnp.zeros_like(total)
    acc[...] = jnp.zeros_like(acc)
    buf[SLOTS - 1] = jnp.zeros((256, 256), BF16)
    probs1[...] = jnp.zeros_like(probs1)
    keep1[...] = jnp.ones_like(keep1)

    def score(i, into):
        into[...] = lax.dot_general(
            buf[i % SLOTS, :, 0:128], q_rows[half(i)],
            (((1,), (1,)), ((), ())), preferred_element_type=F32,
        )

    def collect(i, parity):
        r = half(i)
        added = lax.dot_general(
            buf[(i + SLOTS) % SLOTS, :, 128:256], all_probs[parity][...],
            (((0,), (0,)), ((), ())), preferred_element_type=F32,
        )
        acc[r] = acc[r] * all_keep[parity][...] + added

    def weigh(i, parity, masked, base):
        r = half(i)
        scores = all_scores[parity][...]
        if masked:
            lane = lax.broadcasted_iota(jnp.int32, (1, 512), 1)
            q_pos = base + (lane % 256)
            low = jnp.full((1, 512), starts_ref[0], jnp.int32)
            for req in range(1, REQS):
                low = jnp.where(starts_ref[req] <= q_pos, starts_ref[req], low)
            k_pos = key_run(i) * 256 + lax.broadcasted_iota(jnp.int32, (256, 512), 0)
            allowed = (k_pos <= q_pos) & (k_pos >= low)
            scores = jnp.where(allowed, scores, neg_fill)
        old = top[r]
        new = jnp.maximum(old, jnp.max(scores, axis=0, keepdims=True))
        probs = jnp.exp2(scores - new)
        if masked:
            probs = jnp.where(allowed, probs, 0.0)
        keep = jnp.exp2(old - new)
        top[r] = new
        total[r] = total[r] * keep + jnp.sum(probs, axis=0, keepdims=True)
        all_keep[parity][...] = keep
        all_probs[parity][...] = probs.astype(BF16)

    def stage(i, parity):
        @pl.when(i + SLOTS - 2 < n)
        def _():
            fetch(i + SLOTS - 2).start()

        @pl.when(i + 1 < n)
        def _():
            fetch(i + 1).wait()

        run = key_run(i)
        base = choose(i, q_run) * 256
        last_low = choose(i, lasts)
        slot = sorted_entry[place(i)] % 16
        block = (slot // 2) * 4 + my_y * 2 + slot % 2
        live = jnp.where(
            i < offsets[2], live_ref[(me - block + 32) % 32], tail_ref[34, (other - block + 32) % 32]
        ) > 0
        whole = (run * 256 < base) & (run * 256 >= last_low)

        @pl.when(live & whole)
        def _():
            weigh(i, parity, False, base)
            score(i + 1, all_scores[1 - parity])
            collect(i - 1, 1 - parity)

        @pl.when(live & jnp.logical_not(whole))
        def _():
            weigh(i, parity, True, base)
            score(i + 1, all_scores[1 - parity])
            collect(i - 1, 1 - parity)

        @pl.when(jnp.logical_not(live))
        def _():
            score(i + 1, all_scores[1 - parity])
            collect(i - 1, 1 - parity)
            all_keep[parity][...] = jnp.ones((1, 512), F32)
            all_probs[parity][...] = jnp.zeros((256, 512), BF16)

    def pair(k, carry):
        stage(2 * k, 0)

        @pl.when(2 * k + 1 < n)
        def _():
            stage(2 * k + 1, 1)

        return carry

    fetch(0).wait()
    score(0, scores0)
    lax.fori_loop(0, (n + 1) // 2, pair, 0)

    @pl.when(n % 2 == 1)
    def _():
        collect(n - 1, 0)

    @pl.when(n % 2 == 0)
    def _():
        collect(n - 1, 1)

    for r in range(4):
        weight = total[r]
        done = (acc[r] * jnp.where(weight > 0, 1.0 / weight, 0.0)).astype(BF16)
        for part in range(2):
            k = 2 * (r % 2) + part
            for h in range(2):
                low = h * 256 + part * 128
                o_ref[r // 2, k, h * 128 : (h + 1) * 128, :] = done[:, low : low + 128]
                st_ref[r // 2, k, h : h + 1, :] = top[r, :, low : low + 128]
                st_ref[r // 2, k, 2 + h : 3 + h, :] = weight[:, low : low + 128]


def middle_kernel(
    heads_ref, stats_ref, w_ref, w_own, tok_ref, gain_ref, wg_ref, wu_ref, wd_ref, match_ref, final_ref, head_ref,
    out_ref, rms_ref, top_ref,
    heads, stats, joined, near_send, near_got, w, tok_rows, tok_cols, wg, wu, wd, att, att_send, att_cols, normed, act, part, fwd_in,
    x_in, y_in, head, row_send, seq_got, wide_send, wide_got, last_send, last_got, max_send, seq_max, vocab_max,
    load_sem, send_sem, head_recv, stat_recv, near_recv, norm_recv, att_recv, fwd_recv, x_recv, y_recv,
    row_recv, wide_recv, last_recv, max_recv, top_recv,
):
    s = lax.axis_index("seq")
    v = lax.axis_index("vocab")
    others = [(v + r) % 8 for r in range(1, 8)]
    seqs = [(s + r) % 32 for r in range(1, 32)]
    cols = pl.ds(pl.multiple_of(v * 256, 256), 256)
    rows = pl.ds(pl.multiple_of(v * 64, 64), 64)
    loads = [
        pltpu.make_async_copy(w_own, w.at[v // 2], load_sem.at[0]),
        pltpu.make_async_copy(tok_ref.at[rows, :], tok_rows, load_sem.at[1]),
        pltpu.make_async_copy(tok_ref.at[:, cols], tok_cols, load_sem.at[2]),
        pltpu.make_async_copy(wg_ref, wg, load_sem.at[3]),
        pltpu.make_async_copy(wu_ref, wu, load_sem.at[4]),
        pltpu.make_async_copy(wd_ref, wd, load_sem.at[5]),
        pltpu.make_async_copy(heads_ref.at[0, v // 2], heads.at[v // 2, (s // 2) % 2], load_sem.at[6]),
        pltpu.make_async_copy(stats_ref.at[0, v // 2], stats.at[v // 2, (s // 2) % 2], load_sem.at[9]),
        pltpu.make_async_copy(head_ref, head, load_sem.at[8]),
    ] + [
        pltpu.make_async_copy(
            w_ref.at[(v // 2 + d) % 4], w.at[(v // 2 + d) % 4], load_sem.at[9 + d]
        )
        for d in range(1, 4)
    ]
    for copy in loads:
        copy.start()
    x = v // 2
    y = v % 2
    my_y = (s // 2) % 2
    across = seq_at(s, 0, 1, 0)
    greet(
        [(s, other) for other in others]
        + [(other, v) for other in seqs]
        + [(across, vocab_at(v, dx, 0)) for dx in range(1, 4)]
    )
    sent = []

    def go(src, dst, recv, peer):
        copy = pltpu.make_async_remote_copy(
            src_ref=src, dst_ref=dst, send_sem=send_sem.at[len(sent)], recv_sem=recv,
            device_id=peer, device_id_type=MESH,
        )
        copy.start()
        sent.append(copy)

    def take(dst, recv):
        pltpu.make_async_remote_copy(
            src_ref=dst, dst_ref=dst, send_sem=send_sem.at[0], recv_sem=recv,
            device_id=(s, others[0]), device_id_type=MESH,
        ).wait_recv()

    for dx in (2, 1, 3, 0):
        target = (x + dx) % 4
        for which in (1, 0):
            if (dx, which) != (0, 0):
                peer = (across if which else s, vocab_at(v, dx, 0))
                go(heads_ref.at[which, target], heads.at[x, my_y], head_recv.at[x, my_y], peer)
                go(stats_ref.at[which, target], stats.at[x, my_y], stat_recv.at[x, my_y], peer)
    for i in (0, 1, 6, 7, 9, 10, 11):
        loads[i].wait()
    for dx in range(4):
        source = (x + dx) % 4
        for which in range(2):
            if (dx, which) != (0, 0):
                held = (my_y + which) % 2
                take(heads.at[source, held], head_recv.at[source, held])
                take(stats.at[source, held], stat_recv.at[source, held])
    for k in range(4):
        for h in range(2):
            tops = [stats[k, i, h : h + 1, :] for i in range(2)]
            best = jnp.maximum(tops[0], tops[1])
            weights = [stats[k, i, 2 + h : 3 + h, :] * jnp.exp2(tops[i] - best) for i in range(2)]
            scale = 1.0 / (weights[0] + weights[1])
            span = pl.ds(h * 128, 128)
            joined[k, span, :] = (
                heads[k, 0, span, :].astype(F32) * (weights[0] * scale)
                + heads[k, 1, span, :].astype(F32) * (weights[1] * scale)
            ).astype(BF16)

    near = vocab_at(v, 0, 1)
    for j in range(4):
        total = jnp.zeros((128, 512), F32)
        for k in range(4):
            total += lax.dot_general(
                joined[k], w[k, :, j * 512 : (j + 1) * 512],
                (((0,), (0,)), ((), ())), preferred_element_type=F32,
            )
        att[:, j * 512 : (j + 1) * 512] = jnp.where(y == 0, total[0:64], total[64:128])
        near_send[j] = jnp.where(y == 0, total[64:128], total[0:64]).astype(BF16)
        go(near_send.at[j], near_got.at[j], near_recv.at[j], (s, near))
    for j in range(4):
        take(near_got.at[j], near_recv.at[j])

    def project(j, square):
        wide = pl.ds(pl.multiple_of(j * 512, 512), 512)
        total = att[:, wide] + near_got[j].astype(F32)
        att_send[2 * j] = total[:, 0:256].astype(BF16)
        att_send[2 * j + 1] = total[:, 256:512].astype(BF16)
        residual = tok_rows[:, wide].astype(F32) + total
        att[:, wide] = residual
        return square + jnp.sum(residual * residual, axis=-1, keepdims=True)

    square = lax.fori_loop(0, 4, project, jnp.zeros((64, 1), F32))
    gain = wide_row(gain_ref)
    mine = (att[...] * lax.rsqrt(square / 2048 + epsilon) * gain).astype(BF16)
    normed[2 * v] = mine[0:32]
    normed[2 * v + 1] = mine[32:64]

    right, left = vocab_at(v, 1, 0), vocab_at(v, -1, 0)

    def pass_on(owner, p, other):
        view = normed.at[2 * owner + p]
        go(view, view, norm_recv.at[owner, p], (s, other))

    def arrive(dx, dy, p, peers):
        owner = vocab_at(v, dx, dy)
        take(normed.at[2 * owner + p], norm_recv.at[owner, p])
        for peer in peers:
            pass_on(owner, p, peer)

    for other in others:
        go(att_send.at[other], att_cols.at[v], att_recv.at[v], (s, other))
    for p in range(2):
        for peer in (right, left, near):
            pass_on(v, p, peer)
    own_cols = pltpu.make_async_copy(att_send.at[v], att_cols.at[v], load_sem.at[7])
    own_cols.start()

    loads[2].wait()
    own_cols.wait()
    for other in others:
        take(att_cols.at[other], att_recv.at[other])
    picked = jnp.zeros((8, 256), F32)
    for i in range(8):
        residual = tok_cols[i * 64 : (i + 1) * 64, :].astype(F32) + att_cols[i].astype(F32)
        high = residual.astype(BF16)
        low = (residual - high.astype(F32)).astype(BF16)
        picked += jnp.dot(match_ref[i], high, preferred_element_type=F32)
        picked += jnp.dot(match_ref[i], low, preferred_element_type=F32)
    row_send[...] = picked
    seq_got[s] = picked
    for other in seqs:
        go(row_send, seq_got.at[s], row_recv.at[s], (other, v))

    for p in range(2):
        arrive(-1, 0, p, (right,) if p == 0 else ())
        arrive(1, 0, p, (left,) if p == 1 else ())
        arrive(0, 1, p, (right, left))

    for i in (3, 4, 5):
        loads[i].wait()
    def feed(values):
        gate = jnp.dot(values, wg[...], preferred_element_type=F32)
        upward = jnp.dot(values, wu[...], preferred_element_type=F32)
        return (gate / (1.0 + jnp.exp(-gate)) * upward).astype(BF16)

    def part_of(chunk, dx, dy):
        return part.at[chunk, vocab_at(v, dx, dy)]

    def at_y(chunk, dx, lane):
        return part.at[chunk, ((x + dx + 4) % 4) * 2 + lane]

    def rows_of(dx, extra):
        chunk = (x + dx + 4) % 4
        values = normed[pl.ds(4 * chunk, 4)].reshape(128, 2048)
        if extra:
            values = jnp.concatenate([values, normed[16]], axis=0)
        active = feed(values)
        if extra:
            act[...] = active[128:144]
            active = active[0:128]
        for t in range(8):
            part[chunk, t] = jnp.dot(
                active, wd[:, t * 256 : (t + 1) * 256], preferred_element_type=F32
            ).astype(BF16)
        go(at_y(chunk, 2, 0), fwd_in.at[chunk, 0], fwd_recv.at[chunk, 0], (s, right))
        go(at_y(chunk, 2, 1), fwd_in.at[chunk, 1], fwd_recv.at[chunk, 1], (s, left))
        go(at_y(chunk, 1, 1), x_in.at[chunk, 0, 1], x_recv.at[chunk, 0, 1], (s, right))
        go(at_y(chunk, -1, 0), x_in.at[chunk, 1, 0], x_recv.at[chunk, 1, 0], (s, left))

    rows_of(0, False)
    for other in seqs:
        take(seq_got.at[other], row_recv.at[other])
    picked = jnp.sum(seq_got[...], axis=0)
    wide_send[...] = picked
    wide_got[v] = picked
    for other in others:
        go(wide_send, wide_got.at[v], wide_recv.at[v], (s, other))

    for p in range(2):
        arrive(2, 0, p, (near,))
    for p in range(2):
        arrive(-1, 1, p, ())
        arrive(1, 1, p, ())
    rows_of(-1, False)
    for other in others:
        take(wide_got.at[other], wide_recv.at[other])
    square = jnp.zeros((8, 1), F32)
    for k in range(8):
        square += jnp.sum(wide_got[k] * wide_got[k], axis=-1, keepdims=True)
    inverse = lax.rsqrt(square / 2048 + epsilon)
    normed[16, 16:32, :] = jnp.zeros((16, 2048), BF16)
    for k in range(8):
        one = wide_got[k] * inverse * gain[:, k * 256 : (k + 1) * 256]
        normed[16, 0:16, k * 256 : (k + 1) * 256] = jnp.concatenate([one, one], axis=0).astype(BF16)
    rows_of(1, True)

    group = lax.broadcasted_iota(jnp.int32, (16, 512), 0) // 4

    def packed(quarter):
        out = quarter(0)
        for q in range(1, 4):
            out = jnp.where(group == q, quarter(q), out)
        return out

    last = act[...]
    mine = packed(
        lambda q: jnp.dot(
            last, wd[:, q * 512 : (q + 1) * 512], preferred_element_type=F32
        )
    ).astype(BF16)
    last_send[...] = mine
    last_got[v] = mine
    for other in others:
        go(last_send, last_got.at[v], last_recv.at[v], (s, other))
    for p in range(2):
        arrive(2, 1, p, ())
    rows_of(2, False)

    def add_to(ref, *incoming):
        value = ref[...].astype(F32)
        for one in incoming:
            value += one[...].astype(F32)
        ref[...] = value.astype(BF16)

    def onward(dx, way):
        chunk = (x + dx + 4) % 4
        take(fwd_in.at[chunk, way], fwd_recv.at[chunk, way])
        ref = at_y(chunk, 1 if way == 0 else -1, way)
        add_to(ref, fwd_in.at[chunk, way])
        go(ref, x_in.at[chunk, way, way], x_recv.at[chunk, way, way], (s, right if way == 0 else left))

    for to_right, to_left in ((-1, 1), (2, 0)):
        onward(to_right, 0)
        onward(to_left, 1)

    for other in others:
        take(last_got.at[other], last_recv.at[other])

    def quarter_rows(q):
        one = jnp.concatenate([wide_got[2 * q], wide_got[2 * q + 1]], axis=1)
        return jnp.concatenate([one, one], axis=0)

    total = last_got[0].astype(F32)
    for k in range(1, 8):
        total += last_got[k].astype(F32)
    final = (packed(quarter_rows) + total).astype(BF16).astype(F32)
    square = jnp.broadcast_to(jnp.sum(final * final, axis=-1, keepdims=True), (16, 128))
    square = square + pltpu.roll(square, 8, axis=0)
    square = square + pltpu.roll(square, 4, axis=0)
    mean_square = square / 2048 + epsilon
    diagonal = lax.broadcasted_iota(jnp.int32, (16, 128), 0) == lax.broadcasted_iota(
        jnp.int32, (16, 128), 1
    )

    def along_lanes(value):
        return jnp.sum(jnp.where(diagonal, value, 0.0), axis=0, keepdims=True)

    rms_ref[...] = along_lanes(jnp.sqrt(mean_square))[:, :REQS]
    inverse = lax.rsqrt(mean_square)[:, 0:1]
    last_gain = wide_row(final_ref)
    spread = packed(
        lambda q: jnp.broadcast_to(last_gain[:, q * 512 : (q + 1) * 512], (16, 512))
    )
    final = final * inverse * spread
    loads[8].wait()
    logits = jnp.zeros((16, 360), F32)
    for q in range(4):
        turned = final if q == 0 else pltpu.roll(final, 16 - 4 * q, axis=0)
        logits += lax.dot_general(
            turned.astype(BF16), head[:, q * 512 : (q + 1) * 512], (((1,), (1,)), ((), ())),
            preferred_element_type=F32,
        )
    best = along_lanes(jnp.broadcast_to(jnp.max(logits, axis=-1, keepdims=True), (16, 128)))
    best = jnp.broadcast_to(best, (8, 128))
    max_send[0] = best
    seq_max[s] = best
    for other in seqs:
        go(max_send.at[0], seq_max.at[s], max_recv.at[s], (other, v))
    for to_right, to_left in ((0, 2), (1, -1)):
        onward(to_right, 0)
        onward(to_left, 1)

    for dx in (0, -1, 1, 2):
        chunk = (x + dx + 4) % 4
        for way in range(2):
            take(x_in.at[chunk, way, 1 - y], x_recv.at[chunk, way, 1 - y])
        ref = part_of(chunk, 0, 1)
        add_to(ref, x_in.at[chunk, 0, 1 - y], x_in.at[chunk, 1, 1 - y])
        go(ref, y_in.at[chunk], y_recv.at[chunk], (s, near))

    for other in seqs:
        take(seq_max.at[other], max_recv.at[other])
    best = jnp.max(seq_max[...], axis=0)
    max_send[1] = best
    vocab_max[v] = best
    for other in others:
        go(max_send.at[1], vocab_max.at[v], top_recv.at[v], (s, other))

    for dx in (0, -1, 1, 2):
        chunk = (x + dx + 4) % 4
        for way in range(2):
            take(x_in.at[chunk, way, y], x_recv.at[chunk, way, y])
        take(y_in.at[chunk], y_recv.at[chunk])
        rows = pl.ds(pl.multiple_of(chunk * 128, 128), 128)
        total = tok_cols[rows, :].astype(F32)
        total += att_cols[pl.ds(2 * chunk, 2)].reshape(128, 256).astype(F32)
        total += part[chunk, v].astype(F32)
        total += x_in[chunk, 0, y].astype(F32)
        total += x_in[chunk, 1, y].astype(F32)
        total += y_in[chunk].astype(F32)
        out_ref[rows, :] = total.astype(BF16)
    for other in others:
        take(vocab_max.at[other], top_recv.at[other])
    top_ref[...] = jnp.max(vocab_max[...], axis=0)[0:1, :REQS]
    for copy in sent:
        copy.wait_send()


def hand_over_kernel(hidden_ref, rms_ref, top_ref, hidden_out, rms_out, top_out):
    hidden_out[...] = hidden_ref[...]
    rms_out[...] = rms_ref[...]
    top_out[...] = top_ref[...]


def per_device(
    tokens,
    attention_gain,
    query_weight,
    key_weight,
    value_weight,
    out_weight,
    forward_gain,
    gate_weight,
    up_weight,
    down_weight,
    final_gain,
    head_weight,
    segment_ids,
    token_order,
    live_blocks,
    cache_slots,
):
    shape = jax.ShapeDtypeStruct
    me = lax.axis_index("seq").astype(jnp.int32)
    request = jnp.arange(8, dtype=jnp.int32)
    starts = jnp.sum((segment_ids[None, :] < request[:, None]).astype(jnp.int32), axis=1)
    query, cache, match, kv_all, q_other, w_all, tail = pl.pallas_call(
        gather_kernel,
        out_shape=(
            shape((528, 256), BF16), shape((512, 256), BF16), shape((8, 8, 64), BF16),
            shape((16, 528, 256), BF16), shape((528, 256), BF16), shape((4, 4, 64, 2048), BF16),
            shape((40, 128), jnp.int32),
        ),
        in_specs=[SM] * 3 + [VM] * 10 + [HB],
        out_specs=(VM, VM, VM, HB, HB, HB, VM),
        scratch_shapes=[
            pltpu.VMEM((528, 256), BF16),
            pltpu.VMEM((512, 2048), BF16),
            pltpu.VMEM((512, 128), F32),
            pltpu.VMEM((512, 128), F32),
            pltpu.VMEM((17, 16, 256), BF16),
            pltpu.SemaphoreType.DMA((2,)),
            pltpu.SemaphoreType.DMA((128,)),
            pltpu.SemaphoreType.DMA((16, 4)),
            pltpu.SemaphoreType.DMA((1,)),
            pltpu.SemaphoreType.DMA((4, 4)),
        ],
        compiler_params=params(0),
        name="gather",
    )(
        token_order, starts, live_blocks[0], tokens, attention_gain.reshape(16, 128), query_weight,
        key_weight, value_weight, jnp.asarray(STEP_COS), jnp.asarray(STEP_SIN), jnp.asarray(FAR_COS),
        jnp.asarray(FAR_SIN), cache_slots[None], out_weight.reshape(4, 64, 2048),
    )

    heads, stats = pl.pallas_call(
        attend_kernel,
        out_shape=(shape((2, 4, 256, 128), BF16), shape((2, 4, 8, 128), F32)),
        in_specs=[SM] * 5 + [VM, VM, HB],
        out_specs=(VM, VM),
        scratch_shapes=[
            pltpu.VMEM((SLOTS, 256, 256), BF16),
            pltpu.SemaphoreType.DMA((SLOTS,)),
            pltpu.VMEM((4, 512, 128), BF16),
            pltpu.VMEM((4, 1, 512), F32),
            pltpu.VMEM((4, 1, 512), F32),
            pltpu.VMEM((4, 128, 512), F32),
            pltpu.VMEM((256, 512), F32),
            pltpu.VMEM((256, 512), F32),
            pltpu.VMEM((256, 512), BF16),
            pltpu.VMEM((256, 512), BF16),
            pltpu.VMEM((1, 512), F32),
            pltpu.VMEM((1, 512), F32),
            pltpu.SMEM((64,), jnp.int32),
            pltpu.SMEM((32,), jnp.int32),
            pltpu.SMEM((32,), jnp.int32),
            pltpu.SMEM((65,), jnp.int32),
        ],
        compiler_params=params(),
        name="attend",
    )(tail, token_order, starts, live_blocks[0], me[None], query, q_other, kv_all)

    dma = pltpu.SemaphoreType.DMA
    hidden, rms, top = pl.pallas_call(
        middle_kernel,
        out_shape=(shape((512, 256), BF16), shape((1, REQS), F32), shape((1, REQS), F32)),
        in_specs=[VM, VM, HB, HB, HB, VM, HB, HB, HB, VM, VM, HB],
        out_specs=(VM, VM, VM),
        scratch_shapes=[
            pltpu.VMEM((4, 2, 256, 128), BF16),
            pltpu.VMEM((4, 2, 8, 128), F32),
            pltpu.VMEM((4, 256, 128), BF16),
            pltpu.VMEM((4, 64, 512), BF16),
            pltpu.VMEM((4, 64, 512), BF16),
            pltpu.VMEM((4, 256, 2048), BF16),
            pltpu.VMEM((64, 2048), BF16),
            pltpu.VMEM((512, 256), BF16),
            pltpu.VMEM((2048, 512), BF16),
            pltpu.VMEM((2048, 512), BF16),
            pltpu.VMEM((512, 2048), BF16),
            pltpu.VMEM((64, 2048), F32),
            pltpu.VMEM((8, 64, 256), BF16),
            pltpu.VMEM((8, 64, 256), BF16),
            pltpu.VMEM((17, 32, 2048), BF16),
            pltpu.VMEM((16, 512), BF16),
            pltpu.VMEM((4, 8, 128, 256), BF16),
            pltpu.VMEM((4, 2, 128, 256), BF16),
            pltpu.VMEM((4, 2, 2, 128, 256), BF16),
            pltpu.VMEM((4, 128, 256), BF16),
            pltpu.VMEM((360, 2048), BF16),
            pltpu.VMEM((8, 256), F32),
            pltpu.VMEM((32, 8, 256), F32),
            pltpu.VMEM((8, 256), F32),
            pltpu.VMEM((8, 8, 256), F32),
            pltpu.VMEM((16, 512), BF16),
            pltpu.VMEM((8, 16, 512), BF16),
            pltpu.VMEM((2, 8, 128), F32),
            pltpu.VMEM((32, 8, 128), F32),
            pltpu.VMEM((8, 8, 128), F32),
            dma((13,)), dma((192,)), dma((4, 2)), dma((4, 2)), dma((4,)), dma((8, 2)), dma((8,)), dma((4, 2)), dma((4, 2, 2)), dma((4,)),
            dma((32,)), dma((8,)), dma((8,)), dma((32,)), dma((8,)),
        ],
        compiler_params=params(1),
        name="middle",
    )(
        heads, stats, w_all.reshape(4, 256, 2048), out_weight, tokens, forward_gain.reshape(16, 128), gate_weight, up_weight,
        down_weight, match, final_gain.reshape(16, 128), head_weight,
    )
    hidden, rms, top = pl.pallas_call(
        hand_over_kernel,
        out_shape=(shape((512, 256), BF16), shape((1, REQS), F32), shape((1, REQS), F32)),
        in_specs=[VM, VM, VM],
        out_specs=(VM, VM, VM),
        compiler_params=params(),
        name="hand_over",
    )(hidden, rms, top)
    return (hidden, cache.reshape(512, 2, 128), rms.reshape(REQS), top.reshape(REQS))


def solution(mesh):
    return jax.shard_map(
        per_device,
        mesh=mesh,
        in_specs=(
            P("seq", None),
            P(),
            P(None, "vocab"),
            P(None, "vocab"),
            P(None, "vocab"),
            P("vocab", None),
            P(),
            P(None, "vocab"),
            P(None, "vocab"),
            P("vocab", None),
            P(),
            P(("seq", "vocab"), None),
            P(),
            P("seq"),
            P("seq", None),
            P("seq"),
        ),
        out_specs=(P("seq", "vocab"), P("seq", None, "vocab"), P(), P()),
        check_vma=False,
    )
```

```python
import functools

import jax
import jax.numpy as jnp
import numpy as np
from jax import lax
from jax.experimental import pallas as pl
from jax.experimental.pallas import tpu as pltpu
from jax.sharding import PartitionSpec as P

MESH = pl.DeviceIdType.MESH
HD = 128
REQS = 4
epsilon = 1e-06
rope_base = 1000000.0
neg_fill = -1e30
VM = pl.BlockSpec(memory_space=pltpu.VMEM)
SM = pl.BlockSpec(memory_space=pltpu.SMEM)
HB = pl.BlockSpec(memory_space=pl.ANY)
F32 = jnp.float32
BF16 = jnp.bfloat16
LIMIT = 62 * 1024 * 1024
SCALE = HD ** (-0.5) * 1.4426950408889634


def params(cid=None):
    if cid is None:
        return pltpu.CompilerParams(vmem_limit_bytes=LIMIT)
    return pltpu.CompilerParams(
        collective_id=cid, has_side_effects=True, vmem_limit_bytes=LIMIT
    )


def seq_at(s, dz, dy, dc):
    z, y, c = s // 4, (s // 2) % 2, s % 2
    return ((z + dz + 8) % 8) * 4 + ((y + dy) % 2) * 2 + (c + dc) % 2


def vocab_at(v, dx, dy):
    x, y = v // 2, v % 2
    return ((x + dx + 4) % 4) * 2 + (y + dy) % 2


def wide_row(ref):
    rows = ref[...].astype(F32)
    return jnp.concatenate([rows[i : i + 1] for i in range(16)], axis=1)


def greet(peers):
    barrier = pltpu.get_barrier_semaphore()
    for peer in peers:
        pl.semaphore_signal(barrier, inc=1, device_id=peer, device_id_type=MESH)
    pl.semaphore_wait(barrier, len(peers))


FREQUENCY = rope_base ** (-(np.arange(128) % 64) * 2.0 / 128)
STEP_COS = np.cos(np.arange(256)[:, None] * FREQUENCY[None, :]).astype(np.float32)
STEP_SIN = np.sin(np.arange(256)[:, None] * FREQUENCY[None, :]).astype(np.float32)
FAR_COS = np.cos(256 * np.arange(64)[:, None] * FREQUENCY[None, :]).astype(np.float32)
FAR_SIN = np.sin(256 * np.arange(64)[:, None] * FREQUENCY[None, :]).astype(np.float32)


PIECE_ROWS = ((0, 128), (128, 128), (256, 128), (384, 144))


def gather_kernel(
    base_ref, starts_ref, live_ref, tok_ref, gain_ref, wq_ref, wk_ref, wv_ref,
    step_cos, step_sin, far_cos, far_sin, slot_ref, w_ref,
    q_ref, cache_ref, match_ref, kv_all, q_all, w_all, tail_ref,
    kv_ref, normed, cosines, sines, tails, own_sem, send_sem, kv_sem, q_sem, w_sem,
):
    s = lax.axis_index("seq")
    v = lax.axis_index("vocab")
    z, c, x = s // 4, s % 2, v // 2
    up = (seq_at(s, 1, 0, 0), v)
    down = (seq_at(s, -1, 0, 0), v)
    side = (seq_at(s, 0, 1, 0), v)
    core = (seq_at(s, 0, 0, 1), v)
    right = (s, vocab_at(v, 1, 0))
    left = (s, vocab_at(v, -1, 0))
    barrier = pltpu.get_barrier_semaphore()
    for peer in (up, down, side, core, right, left):
        pl.semaphore_signal(barrier, inc=1, device_id=peer, device_id_type=MESH)
    gain = wide_row(gain_ref)
    lane = lax.broadcasted_iota(jnp.int32, (128, 128), 1)

    def turn(u, i):
        rows = pl.ds(i * 128, 128)
        return u * cosines[rows, :] + pltpu.roll(u, 64, axis=1) * sines[rows, :]

    def keys_values(i):
        rows = pl.ds(i * 128, 128)
        values = tok_ref[rows, :].astype(F32)
        scale = lax.rsqrt(jnp.mean(values * values, axis=-1, keepdims=True) + epsilon)
        values = (values * scale * gain).astype(BF16)
        normed[rows, :] = values
        r = i // 2
        steps = pl.ds((i % 2) * 128, 128)
        order = base_ref[r * 256] + (i % 2) * 128 + lax.broadcasted_iota(jnp.int32, (128, 128), 0)
        for req in range(REQS):
            start = starts_ref[req]
            runs = jnp.maximum(base_ref[r * 256] // 256 - start // 256, 0)
            far_c, far_s = far_cos[pl.ds(runs, 1), :], far_sin[pl.ds(runs, 1), :]
            off_c, off_s = step_cos[pl.ds(start % 256, 1), :], step_sin[pl.ds(start % 256, 1), :]
            run_c = jnp.broadcast_to(far_c * off_c + far_s * off_s, (128, 128))
            run_s = jnp.broadcast_to(far_s * off_c - far_c * off_s, (128, 128))
            later = order >= start
            near_cos = jnp.where(later, run_c, near_cos) if req else run_c
            near_sin = jnp.where(later, run_s, near_sin) if req else run_s
        cosines[rows, :] = step_cos[steps, :] * near_cos - step_sin[steps, :] * near_sin
        sine = step_sin[steps, :] * near_cos + step_cos[steps, :] * near_sin
        sines[rows, :] = jnp.where(lane < 64, -sine, sine)
        key = jnp.dot(values, wk_ref[...], preferred_element_type=F32)
        kv_ref[rows, 0:128] = turn(key, i).astype(BF16)
        value = jnp.dot(values, wv_ref[...], preferred_element_type=F32)
        kv_ref[rows, 128:256] = value.astype(BF16)

    half = lax.broadcasted_iota(jnp.int32, (16, 256), 1)
    run = jnp.where(half < 128, base_ref[0] // 256, base_ref[256] // 256).astype(F32)
    kv_ref[512:528, :] = run.astype(BF16)
    keys_values(0)
    pl.semaphore_wait(barrier, 6)
    started = []

    def go(src, dst, recv, peer):
        copy = pltpu.make_async_remote_copy(
            src_ref=src, dst_ref=dst, send_sem=send_sem.at[len(started)], recv_sem=recv,
            device_id=peer, device_id_type=MESH,
        )
        copy.start()
        started.append(copy)

    def take(dst, recv):
        pltpu.make_async_remote_copy(
            src_ref=dst, dst_ref=dst, send_sem=send_sem.at[0], recv_sem=recv,
            device_id=core, device_id_type=MESH,
        ).wait_recv()

    def kv_view(block, p):
        low, count = PIECE_ROWS[p]
        return kv_all.at[block, pl.ds(low, count), :]

    def kv_take(dz, p, peers):
        block = ((z + dz + 8) % 8) * 2 + c
        take(kv_view(block, p), kv_sem.at[block, p])
        for peer in peers:
            go(kv_view(block, p), kv_view(block, p), kv_sem.at[block, p], peer)

    def w_take(dx, p, peers):
        shard, piece = (x + dx + 4) % 4, 2 * c + p
        take(w_all.at[shard, piece], w_sem.at[shard, piece])
        for peer in peers:
            go(w_all.at[shard, piece], w_all.at[shard, piece], w_sem.at[shard, piece], peer)

    mine = z * 2 + c
    for p in range(4):
        if p:
            keys_values(p)
        low, count = PIECE_ROWS[p]
        for peer in (up, down, core):
            go(kv_ref.at[pl.ds(low, count), :], kv_view(mine, p), kv_sem.at[mine, p], peer)
        if p < 2:
            piece = 2 * c + p
            for peer in (right, left):
                go(w_ref.at[piece], w_all.at[x, piece], w_sem.at[x, piece], peer)
    own = pltpu.make_async_copy(kv_ref, kv_all.at[mine], own_sem.at[0])
    own.start()
    for p in range(4):
        rows = pl.ds(p * 128, 128)
        query = jnp.dot(normed[rows, :], wq_ref[...], preferred_element_type=F32)
        q_ref[rows, 0:128] = (turn(query[:, 0:128], p) * SCALE).astype(BF16)
        q_ref[rows, 128:256] = (turn(query[:, 128:256], p) * SCALE).astype(BF16)
    row = lax.broadcasted_iota(jnp.int32, (16, 256), 0)
    for i in range(32):
        run = jnp.where((row == 1) & (half == i), live_ref[i].astype(F32), run)
    q_ref[512:528, :] = run.astype(BF16)
    go(q_ref, q_all, q_sem.at[0], side)

    for d in (1, 2):
        for p in range(4):
            kv_take(-d, p, (up, core))
            kv_take(d, p, (down, core))
        if d == 1:
            w_take(-1, 0, (right, core))
            w_take(1, 0, (core,))
    w_take(-1, 1, (core,))
    w_take(1, 1, (left, core))
    slots = slot_ref[...]
    for i in range(4):
        row = i * 128 + lax.broadcasted_iota(jnp.int32, (128, 512), 0)
        pick = jnp.where(row == slots, 1.0, 0.0).astype(BF16)
        moved = jnp.dot(pick, kv_ref[0:512, :], preferred_element_type=F32)
        cache_ref[i * 128 : (i + 1) * 128, :] = moved.astype(BF16)
    request = lax.broadcasted_iota(jnp.int32, (8, 64), 0) % REQS
    last = jnp.full((8, 64), starts_ref[1] - 1, jnp.int32)
    for req in range(1, REQS):
        last = jnp.where(request == req, starts_ref[req + 1] - 1, last)
    for i in range(8):
        order = base_ref[256 * (i // 4)] + (i % 4) * 64 + lax.broadcasted_iota(jnp.int32, (8, 64), 1)
        match_ref[i] = jnp.where(order == last, 1.0, 0.0).astype(BF16)
    for p in range(4):
        kv_take(-3, p, (up, core) if p < 2 else (core,))
        kv_take(3, p, (down, core) if p >= 2 else (core,))
    for p in range(2):
        w_take(2, p, (core,))
    for p in range(4):
        kv_take(4, p, (core,))

    for dz in range(8):
        for p in range(4):
            block = ((z + dz) % 8) * 2 + 1 - c
            take(kv_view(block, p), kv_sem.at[block, p])
    take(q_all, q_sem.at[0])
    own.wait()
    ends = [
        pltpu.make_async_copy(kv_all.at[:, pl.ds(512, 16), :], tails.at[pl.ds(0, 16)], own_sem.at[0]),
        pltpu.make_async_copy(q_all.at[pl.ds(512, 16), :], tails.at[16], own_sem.at[1]),
    ]
    for copy in ends:
        copy.start()
    for dx in range(1, 4):
        for p in range(2):
            shard, piece = (x + dx) % 4, 2 * (1 - c) + p
            take(w_all.at[shard, piece], w_sem.at[shard, piece])
    for copy in ends:
        copy.wait()
    rows = tails[0:16].astype(F32)[:, 0, :].astype(jnp.int32)
    tail_ref[0:16, :] = rows[:, 0:128]
    tail_ref[16:32, :] = rows[:, 128:256]
    rows = tails[16].astype(F32)[0:8, :].astype(jnp.int32)
    tail_ref[32:33, :] = rows[0:1, 0:128]
    tail_ref[33:34, :] = rows[0:1, 128:256]
    tail_ref[34:35, :] = rows[1:2, 0:128]
    tail_ref[35:40, :] = jnp.zeros((5, 128), jnp.int32)
    for copy in started:
        copy.wait_send()


SLOTS = 8


def attend_kernel(
    tail_ref, base_ref, starts_ref, live_ref, me_ref, q_ref, other_ref, kv_ref, o_ref, st_ref,
    buf, sem, q_rows, top, total, acc, scores0, scores1, probs0, probs1, keep0, keep1,
    table, sorted_run, sorted_entry, before,
):
    me = me_ref[0]
    my_y = (me // 2) % 2
    other = me + 2 - 4 * my_y
    all_scores, all_probs, all_keep = (scores0, scores1), (probs0, probs1), (keep0, keep1)
    q_run = [base_ref[0] // 256, base_ref[256] // 256, tail_ref[32, 0], tail_ref[33, 0]]

    def clear(i, carry):
        table[i] = -1
        return carry

    def enter(i, carry):
        table[tail_ref[i, 0]] = i
        return carry

    def gather_up(i, count):
        before[i] = count
        entry = table[i]

        @pl.when(entry >= 0)
        def _():
            sorted_run[count] = i
            sorted_entry[count] = entry

        return jnp.where(entry >= 0, count + 1, count)

    lax.fori_loop(0, 64, clear, 0)
    lax.fori_loop(0, 32, enter, 0)
    before[64] = lax.fori_loop(0, 64, gather_up, 0)

    def low_of(position):
        low = starts_ref[0]
        for r in range(1, REQS):
            low = jnp.where(starts_ref[r] <= position, starts_ref[r], low)
        return low

    lasts, shifts, offsets = [], [], [0]
    for r in range(4):
        first = before[low_of(q_run[r] * 256) // 256]
        lasts.append(low_of(q_run[r] * 256 + 255))
        shifts.append(first - offsets[-1])
        offsets.append(offsets[-1] + before[q_run[r] + 1] - first)
    n = offsets[4]

    def choose(i, values):
        out = values[0]
        for r in range(1, 4):
            out = jnp.where(i >= offsets[r], values[r], out)
        return out

    def half(i):
        return choose(i, [0, 1, 2, 3])

    def place(i):
        return (i + choose(i, shifts)) & 31

    def key_run(i):
        return sorted_run[place(i)]

    def fetch(i):
        entry = sorted_entry[place(i)]
        slot = i & (SLOTS - 1)
        return pltpu.make_async_copy(
            kv_ref.at[entry & 15, pl.ds(pl.multiple_of((entry >> 4) * 256, 256), 256), :], buf.at[slot], sem.at[slot]
        )

    for i in range(SLOTS - 2):

        @pl.when(i < n)
        def _():
            fetch(i).start()

    for r in range(4):
        source = q_ref if r < 2 else other_ref
        for h in range(2):
            q_rows[r, pl.ds(h * 256, 256), :] = source[
                pl.ds((r % 2) * 256, 256), pl.ds(h * 128, 128)
            ]
    top[...] = jnp.full_like(top, neg_fill)
    total[...] = jnp.zeros_like(total)
    acc[...] = jnp.zeros_like(acc)
    buf[SLOTS - 1] = jnp.zeros((256, 256), BF16)
    probs1[...] = jnp.zeros_like(probs1)
    keep1[...] = jnp.ones_like(keep1)

    def score(i, into):
        into[...] = lax.dot_general(
            buf[i & (SLOTS - 1), :, 0:128], q_rows[half(i)],
            (((1,), (1,)), ((), ())), preferred_element_type=F32,
        )

    def collect(i, parity):
        r = half(i)
        added = lax.dot_general(
            buf[(i + SLOTS) & (SLOTS - 1), :, 128:256], all_probs[parity][...],
            (((0,), (0,)), ((), ())), preferred_element_type=F32,
        )
        acc[r] = acc[r] * all_keep[parity][...] + added

    def weigh(i, parity, masked, base):
        r = half(i)
        scores = all_scores[parity][...]
        if masked:
            lane = lax.broadcasted_iota(jnp.int32, (1, 512), 1)
            q_pos = base + (lane & 255)
            low = jnp.full((1, 512), starts_ref[0], jnp.int32)
            for req in range(1, REQS):
                low = jnp.where(starts_ref[req] <= q_pos, starts_ref[req], low)
            k_pos = key_run(i) * 256 + lax.broadcasted_iota(jnp.int32, (256, 512), 0)
            allowed = (k_pos <= q_pos) & (k_pos >= low)
            scores = jnp.where(allowed, scores, neg_fill)
        old = top[r]
        new = jnp.maximum(old, jnp.max(scores, axis=0, keepdims=True))
        probs = jnp.exp2(scores - new)
        if masked:
            probs = jnp.where(allowed, probs, 0.0)
        keep = jnp.exp2(old - new)
        top[r] = new
        total[r] = total[r] * keep + jnp.sum(probs, axis=0, keepdims=True)
        all_keep[parity][...] = keep
        all_probs[parity][...] = probs.astype(BF16)

    def stage(i, parity):
        @pl.when(i + SLOTS - 2 < n)
        def _():
            fetch(i + SLOTS - 2).start()

        @pl.when(i + 1 < n)
        def _():
            fetch(i + 1).wait()

        run = key_run(i)
        base = choose(i, q_run) * 256
        last_low = choose(i, lasts)
        slot = sorted_entry[place(i)] & 15
        block = (slot >> 1) * 4 + my_y * 2 + (slot & 1)
        live = jnp.where(
            i < offsets[2], live_ref[(me - block) & 31], tail_ref[34, (other - block) & 31]
        ) > 0
        whole = (run * 256 < base) & (run * 256 >= last_low)

        @pl.when(live & whole)
        def _():
            weigh(i, parity, False, base)
            score(i + 1, all_scores[1 - parity])
            collect(i - 1, 1 - parity)

        @pl.when(live & jnp.logical_not(whole))
        def _():
            weigh(i, parity, True, base)
            score(i + 1, all_scores[1 - parity])
            collect(i - 1, 1 - parity)

        @pl.when(jnp.logical_not(live))
        def _():
            score(i + 1, all_scores[1 - parity])
            collect(i - 1, 1 - parity)
            all_keep[parity][...] = jnp.ones((1, 512), F32)
            all_probs[parity][...] = jnp.zeros((256, 512), BF16)

    def pair(k, carry):
        stage(2 * k, 0)

        @pl.when(2 * k + 1 < n)
        def _():
            stage(2 * k + 1, 1)

        return carry

    fetch(0).wait()
    score(0, scores0)
    lax.fori_loop(0, (n + 1) // 2, pair, 0)

    @pl.when(n % 2 == 1)
    def _():
        collect(n - 1, 0)

    @pl.when(n % 2 == 0)
    def _():
        collect(n - 1, 1)

    for r in range(4):
        weight = total[r]
        done = (acc[r] * jnp.where(weight > 0, 1.0 / weight, 0.0)).astype(BF16)
        for part in range(2):
            k = 2 * (r % 2) + part
            for h in range(2):
                low = h * 256 + part * 128
                o_ref[r // 2, k, h * 128 : (h + 1) * 128, :] = done[:, low : low + 128]
                st_ref[r // 2, k, h : h + 1, :] = top[r, :, low : low + 128]
                st_ref[r // 2, k, 2 + h : 3 + h, :] = weight[:, low : low + 128]


def middle_kernel(
    heads_ref, stats_ref, w_ref, w_own, tok_ref, gain_ref, wg_ref, wu_ref, wd_ref, match_ref, final_ref, head_ref,
    out_ref, rms_ref, top_ref,
    heads, stats, joined, near_send, near_got, w, tok_rows, tok_cols, wg, wu, wd, att, att_send, att_cols, normed, act, part, fwd_in,
    x_in, y_in, head, row_send, seq_got, wide_send, wide_got, last_send, last_got, max_send, seq_max, vocab_max,
    load_sem, send_sem, head_recv, stat_recv, near_recv, norm_recv, att_recv, fwd_recv, x_recv, y_recv,
    row_recv, wide_recv, last_recv, max_recv, top_recv,
):
    s = lax.axis_index("seq")
    v = lax.axis_index("vocab")
    others = [(v + r) % 8 for r in range(1, 8)]
    seqs = [(s + r) % 32 for r in range(1, 32)]
    cols = pl.ds(pl.multiple_of(v * 256, 256), 256)
    rows = pl.ds(pl.multiple_of(v * 64, 64), 64)
    loads = [
        pltpu.make_async_copy(w_own, w.at[v // 2], load_sem.at[0]),
        pltpu.make_async_copy(tok_ref.at[rows, :], tok_rows, load_sem.at[1]),
        pltpu.make_async_copy(tok_ref.at[:, cols], tok_cols, load_sem.at[2]),
        pltpu.make_async_copy(wg_ref, wg, load_sem.at[3]),
        pltpu.make_async_copy(wu_ref, wu, load_sem.at[4]),
        pltpu.make_async_copy(wd_ref, wd, load_sem.at[5]),
        pltpu.make_async_copy(heads_ref.at[0, v // 2], heads.at[v // 2, (s // 2) % 2], load_sem.at[6]),
        pltpu.make_async_copy(stats_ref.at[0, v // 2], stats.at[v // 2, (s // 2) % 2], load_sem.at[9]),
        pltpu.make_async_copy(head_ref, head, load_sem.at[8]),
    ] + [
        pltpu.make_async_copy(
            w_ref.at[(v // 2 + d) % 4], w.at[(v // 2 + d) % 4], load_sem.at[9 + d]
        )
        for d in range(1, 4)
    ]
    for copy in loads:
        copy.start()
    x = v // 2
    y = v % 2
    my_y = (s // 2) % 2
    across = seq_at(s, 0, 1, 0)
    greet(
        [(s, other) for other in others]
        + [(other, v) for other in seqs]
        + [(across, vocab_at(v, dx, 0)) for dx in range(1, 4)]
    )
    sent = []

    def go(src, dst, recv, peer):
        copy = pltpu.make_async_remote_copy(
            src_ref=src, dst_ref=dst, send_sem=send_sem.at[len(sent)], recv_sem=recv,
            device_id=peer, device_id_type=MESH,
        )
        copy.start()
        sent.append(copy)

    def take(dst, recv):
        pltpu.make_async_remote_copy(
            src_ref=dst, dst_ref=dst, send_sem=send_sem.at[0], recv_sem=recv,
            device_id=(s, others[0]), device_id_type=MESH,
        ).wait_recv()

    for dx in (2, 1, 3, 0):
        target = (x + dx) % 4
        for which in (1, 0):
            if (dx, which) != (0, 0):
                peer = (across if which else s, vocab_at(v, dx, 0))
                go(heads_ref.at[which, target], heads.at[x, my_y], head_recv.at[x, my_y], peer)
                go(stats_ref.at[which, target], stats.at[x, my_y], stat_recv.at[x, my_y], peer)
    for i in (0, 1, 6, 7, 9, 10, 11):
        loads[i].wait()
    for dx in range(4):
        source = (x + dx) % 4
        for which in range(2):
            if (dx, which) != (0, 0):
                held = (my_y + which) % 2
                take(heads.at[source, held], head_recv.at[source, held])
                take(stats.at[source, held], stat_recv.at[source, held])
    for k in range(4):
        for h in range(2):
            tops = [stats[k, i, h : h + 1, :] for i in range(2)]
            best = jnp.maximum(tops[0], tops[1])
            weights = [stats[k, i, 2 + h : 3 + h, :] * jnp.exp2(tops[i] - best) for i in range(2)]
            scale = 1.0 / (weights[0] + weights[1])
            span = pl.ds(h * 128, 128)
            joined[k, span, :] = (
                heads[k, 0, span, :].astype(F32) * (weights[0] * scale)
                + heads[k, 1, span, :].astype(F32) * (weights[1] * scale)
            ).astype(BF16)

    near = vocab_at(v, 0, 1)
    for j in range(4):
        total = jnp.zeros((128, 512), F32)
        for k in range(4):
            total += lax.dot_general(
                joined[k], w[k, :, j * 512 : (j + 1) * 512],
                (((0,), (0,)), ((), ())), preferred_element_type=F32,
            )
        att[:, j * 512 : (j + 1) * 512] = jnp.where(y == 0, total[0:64], total[64:128])
        near_send[j] = jnp.where(y == 0, total[64:128], total[0:64]).astype(BF16)
        go(near_send.at[j], near_got.at[j], near_recv.at[j], (s, near))
    for j in range(4):
        take(near_got.at[j], near_recv.at[j])

    def project(j, square):
        wide = pl.ds(pl.multiple_of(j * 512, 512), 512)
        total = att[:, wide] + near_got[j].astype(F32)
        att_send[2 * j] = total[:, 0:256].astype(BF16)
        att_send[2 * j + 1] = total[:, 256:512].astype(BF16)
        residual = tok_rows[:, wide].astype(F32) + total
        att[:, wide] = residual
        return square + jnp.sum(residual * residual, axis=-1, keepdims=True)

    square = lax.fori_loop(0, 4, project, jnp.zeros((64, 1), F32))
    gain = wide_row(gain_ref)
    mine = (att[...] * lax.rsqrt(square / 2048 + epsilon) * gain).astype(BF16)
    normed[2 * v] = mine[0:32]
    normed[2 * v + 1] = mine[32:64]

    right, left = vocab_at(v, 1, 0), vocab_at(v, -1, 0)

    def pass_on(owner, p, other):
        view = normed.at[2 * owner + p]
        go(view, view, norm_recv.at[owner, p], (s, other))

    def arrive(dx, dy, p, peers):
        owner = vocab_at(v, dx, dy)
        take(normed.at[2 * owner + p], norm_recv.at[owner, p])
        for peer in peers:
            pass_on(owner, p, peer)

    for other in others:
        go(att_send.at[other], att_cols.at[v], att_recv.at[v], (s, other))
    for p in range(2):
        for peer in (right, left, near):
            pass_on(v, p, peer)
    own_cols = pltpu.make_async_copy(att_send.at[v], att_cols.at[v], load_sem.at[7])
    own_cols.start()

    loads[2].wait()
    own_cols.wait()
    for other in others:
        take(att_cols.at[other], att_recv.at[other])
    picked = jnp.zeros((8, 256), F32)
    for i in range(8):
        residual = tok_cols[i * 64 : (i + 1) * 64, :].astype(F32) + att_cols[i].astype(F32)
        high = residual.astype(BF16)
        low = (residual - high.astype(F32)).astype(BF16)
        picked += jnp.dot(match_ref[i], high, preferred_element_type=F32)
        picked += jnp.dot(match_ref[i], low, preferred_element_type=F32)
    row_send[...] = picked
    seq_got[s] = picked
    for other in seqs:
        go(row_send, seq_got.at[s], row_recv.at[s], (other, v))

    for p in range(2):
        arrive(-1, 0, p, (right,) if p == 0 else ())
        arrive(1, 0, p, (left,) if p == 1 else ())
        arrive(0, 1, p, (right, left))

    for i in (3, 4, 5):
        loads[i].wait()
    def feed(values):
        gate = jnp.dot(values, wg[...], preferred_element_type=F32)
        upward = jnp.dot(values, wu[...], preferred_element_type=F32)
        return (gate / (1.0 + jnp.exp(-gate)) * upward).astype(BF16)

    def part_of(chunk, dx, dy):
        return part.at[chunk, vocab_at(v, dx, dy)]

    def at_y(chunk, dx, lane):
        return part.at[chunk, ((x + dx + 4) % 4) * 2 + lane]

    def rows_of(dx, extra):
        chunk = (x + dx + 4) % 4
        values = normed[pl.ds(4 * chunk, 4)].reshape(128, 2048)
        if extra:
            values = jnp.concatenate([values, normed[16]], axis=0)
        active = feed(values)
        if extra:
            act[...] = active[128:144]
            active = active[0:128]
        for t in range(8):
            part[chunk, t] = jnp.dot(
                active, wd[:, t * 256 : (t + 1) * 256], preferred_element_type=F32
            ).astype(BF16)
        go(at_y(chunk, 2, 0), fwd_in.at[chunk, 0], fwd_recv.at[chunk, 0], (s, right))
        go(at_y(chunk, 2, 1), fwd_in.at[chunk, 1], fwd_recv.at[chunk, 1], (s, left))
        go(at_y(chunk, 1, 1), x_in.at[chunk, 0, 1], x_recv.at[chunk, 0, 1], (s, right))
        go(at_y(chunk, -1, 0), x_in.at[chunk, 1, 0], x_recv.at[chunk, 1, 0], (s, left))

    rows_of(0, False)
    for other in seqs:
        take(seq_got.at[other], row_recv.at[other])
    picked = jnp.sum(seq_got[...], axis=0)
    wide_send[...] = picked
    wide_got[v] = picked
    for other in others:
        go(wide_send, wide_got.at[v], wide_recv.at[v], (s, other))

    for p in range(2):
        arrive(2, 0, p, (near,))
    for p in range(2):
        arrive(-1, 1, p, ())
        arrive(1, 1, p, ())
    rows_of(-1, False)
    for other in others:
        take(wide_got.at[other], wide_recv.at[other])
    square = jnp.zeros((8, 1), F32)
    for k in range(8):
        square += jnp.sum(wide_got[k] * wide_got[k], axis=-1, keepdims=True)
    inverse = lax.rsqrt(square / 2048 + epsilon)
    normed[16, 16:32, :] = jnp.zeros((16, 2048), BF16)
    for k in range(8):
        one = wide_got[k] * inverse * gain[:, k * 256 : (k + 1) * 256]
        normed[16, 0:16, k * 256 : (k + 1) * 256] = jnp.concatenate([one, one], axis=0).astype(BF16)
    rows_of(1, True)

    group = lax.broadcasted_iota(jnp.int32, (16, 512), 0) // 4

    def packed(quarter):
        out = quarter(0)
        for q in range(1, 4):
            out = jnp.where(group == q, quarter(q), out)
        return out

    last = act[...]
    mine = packed(
        lambda q: jnp.dot(
            last, wd[:, q * 512 : (q + 1) * 512], preferred_element_type=F32
        )
    ).astype(BF16)
    last_send[...] = mine
    last_got[v] = mine
    for other in others:
        go(last_send, last_got.at[v], last_recv.at[v], (s, other))
    for p in range(2):
        arrive(2, 1, p, ())
    rows_of(2, False)

    def add_to(ref, *incoming):
        value = ref[...].astype(F32)
        for one in incoming:
            value += one[...].astype(F32)
        ref[...] = value.astype(BF16)

    def onward(dx, way):
        chunk = (x + dx + 4) % 4
        take(fwd_in.at[chunk, way], fwd_recv.at[chunk, way])
        ref = at_y(chunk, 1 if way == 0 else -1, way)
        add_to(ref, fwd_in.at[chunk, way])
        go(ref, x_in.at[chunk, way, way], x_recv.at[chunk, way, way], (s, right if way == 0 else left))

    for to_right, to_left in ((-1, 1), (2, 0)):
        onward(to_right, 0)
        onward(to_left, 1)

    for other in others:
        take(last_got.at[other], last_recv.at[other])

    def quarter_rows(q):
        one = jnp.concatenate([wide_got[2 * q], wide_got[2 * q + 1]], axis=1)
        return jnp.concatenate([one, one], axis=0)

    total = last_got[0].astype(F32)
    for k in range(1, 8):
        total += last_got[k].astype(F32)
    final = (packed(quarter_rows) + total).astype(BF16).astype(F32)
    square = jnp.broadcast_to(jnp.sum(final * final, axis=-1, keepdims=True), (16, 128))
    square = square + pltpu.roll(square, 8, axis=0)
    square = square + pltpu.roll(square, 4, axis=0)
    mean_square = square / 2048 + epsilon
    diagonal = lax.broadcasted_iota(jnp.int32, (16, 128), 0) == lax.broadcasted_iota(
        jnp.int32, (16, 128), 1
    )

    def along_lanes(value):
        return jnp.sum(jnp.where(diagonal, value, 0.0), axis=0, keepdims=True)

    rms_ref[...] = along_lanes(jnp.sqrt(mean_square))[:, :REQS]
    inverse = lax.rsqrt(mean_square)[:, 0:1]
    last_gain = wide_row(final_ref)
    spread = packed(
        lambda q: jnp.broadcast_to(last_gain[:, q * 512 : (q + 1) * 512], (16, 512))
    )
    final = final * inverse * spread
    loads[8].wait()
    logits = jnp.zeros((16, 360), F32)
    for q in range(4):
        turned = final if q == 0 else pltpu.roll(final, 16 - 4 * q, axis=0)
        logits += lax.dot_general(
            turned.astype(BF16), head[:, q * 512 : (q + 1) * 512], (((1,), (1,)), ((), ())),
            preferred_element_type=F32,
        )
    best = along_lanes(jnp.broadcast_to(jnp.max(logits, axis=-1, keepdims=True), (16, 128)))
    best = jnp.broadcast_to(best, (8, 128))
    max_send[0] = best
    seq_max[s] = best
    for other in seqs:
        go(max_send.at[0], seq_max.at[s], max_recv.at[s], (other, v))
    for to_right, to_left in ((0, 2), (1, -1)):
        onward(to_right, 0)
        onward(to_left, 1)

    for dx in (0, -1, 1, 2):
        chunk = (x + dx + 4) % 4
        for way in range(2):
            take(x_in.at[chunk, way, 1 - y], x_recv.at[chunk, way, 1 - y])
        ref = part_of(chunk, 0, 1)
        add_to(ref, x_in.at[chunk, 0, 1 - y], x_in.at[chunk, 1, 1 - y])
        go(ref, y_in.at[chunk], y_recv.at[chunk], (s, near))

    for other in seqs:
        take(seq_max.at[other], max_recv.at[other])
    best = jnp.max(seq_max[...], axis=0)
    max_send[1] = best
    vocab_max[v] = best
    for other in others:
        go(max_send.at[1], vocab_max.at[v], top_recv.at[v], (s, other))

    for dx in (0, -1, 1, 2):
        chunk = (x + dx + 4) % 4
        for way in range(2):
            take(x_in.at[chunk, way, y], x_recv.at[chunk, way, y])
        take(y_in.at[chunk], y_recv.at[chunk])
        rows = pl.ds(pl.multiple_of(chunk * 128, 128), 128)
        total = tok_cols[rows, :].astype(F32)
        total += att_cols[pl.ds(2 * chunk, 2)].reshape(128, 256).astype(F32)
        total += part[chunk, v].astype(F32)
        total += x_in[chunk, 0, y].astype(F32)
        total += x_in[chunk, 1, y].astype(F32)
        total += y_in[chunk].astype(F32)
        out_ref[rows, :] = total.astype(BF16)
    for other in others:
        take(vocab_max.at[other], top_recv.at[other])
    top_ref[...] = jnp.max(vocab_max[...], axis=0)[0:1, :REQS]
    for copy in sent:
        copy.wait_send()


def hand_over_kernel(hidden_ref, rms_ref, top_ref, hidden_out, rms_out, top_out):
    hidden_out[...] = hidden_ref[...]
    rms_out[...] = rms_ref[...]
    top_out[...] = top_ref[...]


def per_device(
    tokens,
    attention_gain,
    query_weight,
    key_weight,
    value_weight,
    out_weight,
    forward_gain,
    gate_weight,
    up_weight,
    down_weight,
    final_gain,
    head_weight,
    segment_ids,
    token_order,
    live_blocks,
    cache_slots,
):
    shape = jax.ShapeDtypeStruct
    me = lax.axis_index("seq").astype(jnp.int32)
    request = jnp.arange(8, dtype=jnp.int32)
    starts = jnp.sum((segment_ids[None, :] < request[:, None]).astype(jnp.int32), axis=1)
    query, cache, match, kv_all, q_other, w_all, tail = pl.pallas_call(
        gather_kernel,
        out_shape=(
            shape((528, 256), BF16), shape((512, 256), BF16), shape((8, 8, 64), BF16),
            shape((16, 528, 256), BF16), shape((528, 256), BF16), shape((4, 4, 64, 2048), BF16),
            shape((40, 128), jnp.int32),
        ),
        in_specs=[SM] * 3 + [VM] * 10 + [HB],
        out_specs=(VM, VM, VM, HB, HB, HB, VM),
        scratch_shapes=[
            pltpu.VMEM((528, 256), BF16),
            pltpu.VMEM((512, 2048), BF16),
            pltpu.VMEM((512, 128), F32),
            pltpu.VMEM((512, 128), F32),
            pltpu.VMEM((17, 16, 256), BF16),
            pltpu.SemaphoreType.DMA((2,)),
            pltpu.SemaphoreType.DMA((128,)),
            pltpu.SemaphoreType.DMA((16, 4)),
            pltpu.SemaphoreType.DMA((1,)),
            pltpu.SemaphoreType.DMA((4, 4)),
        ],
        compiler_params=params(0),
        name="gather",
    )(
        token_order, starts, live_blocks[0], tokens, attention_gain.reshape(16, 128), query_weight,
        key_weight, value_weight, jnp.asarray(STEP_COS), jnp.asarray(STEP_SIN), jnp.asarray(FAR_COS),
        jnp.asarray(FAR_SIN), cache_slots[None], out_weight.reshape(4, 64, 2048),
    )

    heads, stats = pl.pallas_call(
        attend_kernel,
        out_shape=(shape((2, 4, 256, 128), BF16), shape((2, 4, 8, 128), F32)),
        in_specs=[SM] * 5 + [VM, VM, HB],
        out_specs=(VM, VM),
        scratch_shapes=[
            pltpu.VMEM((SLOTS, 256, 256), BF16),
            pltpu.SemaphoreType.DMA((SLOTS,)),
            pltpu.VMEM((4, 512, 128), BF16),
            pltpu.VMEM((4, 1, 512), F32),
            pltpu.VMEM((4, 1, 512), F32),
            pltpu.VMEM((4, 128, 512), F32),
            pltpu.VMEM((256, 512), F32),
            pltpu.VMEM((256, 512), F32),
            pltpu.VMEM((256, 512), BF16),
            pltpu.VMEM((256, 512), BF16),
            pltpu.VMEM((1, 512), F32),
            pltpu.VMEM((1, 512), F32),
            pltpu.SMEM((64,), jnp.int32),
            pltpu.SMEM((32,), jnp.int32),
            pltpu.SMEM((32,), jnp.int32),
            pltpu.SMEM((65,), jnp.int32),
        ],
        compiler_params=params(),
        name="attend",
    )(tail, token_order, starts, live_blocks[0], me[None], query, q_other, kv_all)

    dma = pltpu.SemaphoreType.DMA
    hidden, rms, top = pl.pallas_call(
        middle_kernel,
        out_shape=(shape((512, 256), BF16), shape((1, REQS), F32), shape((1, REQS), F32)),
        in_specs=[VM, VM, HB, HB, HB, VM, HB, HB, HB, VM, VM, HB],
        out_specs=(VM, VM, VM),
        scratch_shapes=[
            pltpu.VMEM((4, 2, 256, 128), BF16),
            pltpu.VMEM((4, 2, 8, 128), F32),
            pltpu.VMEM((4, 256, 128), BF16),
            pltpu.VMEM((4, 64, 512), BF16),
            pltpu.VMEM((4, 64, 512), BF16),
            pltpu.VMEM((4, 256, 2048), BF16),
            pltpu.VMEM((64, 2048), BF16),
            pltpu.VMEM((512, 256), BF16),
            pltpu.VMEM((2048, 512), BF16),
            pltpu.VMEM((2048, 512), BF16),
            pltpu.VMEM((512, 2048), BF16),
            pltpu.VMEM((64, 2048), F32),
            pltpu.VMEM((8, 64, 256), BF16),
            pltpu.VMEM((8, 64, 256), BF16),
            pltpu.VMEM((17, 32, 2048), BF16),
            pltpu.VMEM((16, 512), BF16),
            pltpu.VMEM((4, 8, 128, 256), BF16),
            pltpu.VMEM((4, 2, 128, 256), BF16),
            pltpu.VMEM((4, 2, 2, 128, 256), BF16),
            pltpu.VMEM((4, 128, 256), BF16),
            pltpu.VMEM((360, 2048), BF16),
            pltpu.VMEM((8, 256), F32),
            pltpu.VMEM((32, 8, 256), F32),
            pltpu.VMEM((8, 256), F32),
            pltpu.VMEM((8, 8, 256), F32),
            pltpu.VMEM((16, 512), BF16),
            pltpu.VMEM((8, 16, 512), BF16),
            pltpu.VMEM((2, 8, 128), F32),
            pltpu.VMEM((32, 8, 128), F32),
            pltpu.VMEM((8, 8, 128), F32),
            dma((13,)), dma((192,)), dma((4, 2)), dma((4, 2)), dma((4,)), dma((8, 2)), dma((8,)), dma((4, 2)), dma((4, 2, 2)), dma((4,)),
            dma((32,)), dma((8,)), dma((8,)), dma((32,)), dma((8,)),
        ],
        compiler_params=params(1),
        name="middle",
    )(
        heads, stats, w_all.reshape(4, 256, 2048), out_weight, tokens, forward_gain.reshape(16, 128), gate_weight, up_weight,
        down_weight, match, final_gain.reshape(16, 128), head_weight,
    )
    hidden, rms, top = pl.pallas_call(
        hand_over_kernel,
        out_shape=(shape((512, 256), BF16), shape((1, REQS), F32), shape((1, REQS), F32)),
        in_specs=[VM, VM, VM],
        out_specs=(VM, VM, VM),
        compiler_params=params(),
        name="hand_over",
    )(hidden, rms, top)
    return (hidden, cache.reshape(512, 2, 128), rms.reshape(REQS), top.reshape(REQS))


def solution(mesh):
    return jax.shard_map(
        per_device,
        mesh=mesh,
        in_specs=(
            P("seq", None),
            P(),
            P(None, "vocab"),
            P(None, "vocab"),
            P(None, "vocab"),
            P("vocab", None),
            P(),
            P(None, "vocab"),
            P(None, "vocab"),
            P("vocab", None),
            P(),
            P(("seq", "vocab"), None),
            P(),
            P("seq"),
            P("seq", None),
            P("seq"),
        ),
        out_specs=(P("seq", "vocab"), P("seq", None, "vocab"), P(), P()),
        check_vma=False,
    )
```

```python
import functools

import jax
import jax.numpy as jnp
import numpy as np
from jax import lax
from jax.experimental import pallas as pl
from jax.experimental.pallas import tpu as pltpu
from jax.sharding import PartitionSpec as P

MESH = pl.DeviceIdType.MESH
HD = 128
REQS = 4
epsilon = 1e-06
rope_base = 1000000.0
neg_fill = -1e30
VM = pl.BlockSpec(memory_space=pltpu.VMEM)
SM = pl.BlockSpec(memory_space=pltpu.SMEM)
HB = pl.BlockSpec(memory_space=pl.ANY)
F32 = jnp.float32
BF16 = jnp.bfloat16
LIMIT = 62 * 1024 * 1024
SCALE = HD ** (-0.5) * 1.4426950408889634


def params(cid=None):
    if cid is None:
        return pltpu.CompilerParams(vmem_limit_bytes=LIMIT)
    return pltpu.CompilerParams(
        collective_id=cid, has_side_effects=True, vmem_limit_bytes=LIMIT
    )


def seq_at(s, dz, dy, dc):
    z, y, c = s // 4, (s // 2) % 2, s % 2
    return ((z + dz + 8) % 8) * 4 + ((y + dy) % 2) * 2 + (c + dc) % 2


def vocab_at(v, dx, dy):
    x, y = v // 2, v % 2
    return ((x + dx + 4) % 4) * 2 + (y + dy) % 2


def wide_row(ref):
    rows = ref[...].astype(F32)
    return jnp.concatenate([rows[i : i + 1] for i in range(16)], axis=1)


def greet(peers):
    barrier = pltpu.get_barrier_semaphore()
    for peer in peers:
        pl.semaphore_signal(barrier, inc=1, device_id=peer, device_id_type=MESH)
    pl.semaphore_wait(barrier, len(peers))


FREQUENCY = rope_base ** (-(np.arange(128) % 64) * 2.0 / 128)
STEP_COS = np.cos(np.arange(256)[:, None] * FREQUENCY[None, :]).astype(np.float32)
STEP_SIN = np.sin(np.arange(256)[:, None] * FREQUENCY[None, :]).astype(np.float32)
FAR_COS = np.cos(256 * np.arange(64)[:, None] * FREQUENCY[None, :]).astype(np.float32)
FAR_SIN = np.sin(256 * np.arange(64)[:, None] * FREQUENCY[None, :]).astype(np.float32)


PIECE_ROWS = ((0, 128), (128, 128), (256, 128), (384, 144))


def gather_kernel(
    base_ref, starts_ref, live_ref, tok_in, gain_ref, wq_in, wk_ref, wv_ref,
    step_cos, step_sin, far_cos, far_sin, slot_ref, w_ref,
    q_ref, cache_ref, match_ref, kv_all, q_all, w_all, tail_ref,
    tok_ref, wq_ref, load_sem, kv_ref, normed, cosines, sines, tails, own_sem, send_sem, kv_sem, q_sem, w_sem,
):
    s = lax.axis_index("seq")
    v = lax.axis_index("vocab")
    z, c, x = s // 4, s % 2, v // 2
    up = (seq_at(s, 1, 0, 0), v)
    down = (seq_at(s, -1, 0, 0), v)
    side = (seq_at(s, 0, 1, 0), v)
    core = (seq_at(s, 0, 0, 1), v)
    right = (s, vocab_at(v, 1, 0))
    left = (s, vocab_at(v, -1, 0))
    loads = [
        pltpu.make_async_copy(
            tok_in.at[pl.ds(i * 128, 128), :], tok_ref.at[pl.ds(i * 128, 128), :], load_sem.at[i]
        )
        for i in range(4)
    ]
    loads.append(pltpu.make_async_copy(wq_in, wq_ref, load_sem.at[4]))
    for copy in loads:
        copy.start()
    barrier = pltpu.get_barrier_semaphore()
    for peer in (up, down, side, core, right, left):
        pl.semaphore_signal(barrier, inc=1, device_id=peer, device_id_type=MESH)
    gain = wide_row(gain_ref)
    lane = lax.broadcasted_iota(jnp.int32, (128, 128), 1)

    def turn(u, i):
        rows = pl.ds(i * 128, 128)
        return u * cosines[rows, :] + pltpu.roll(u, 64, axis=1) * sines[rows, :]

    def keys_values(i):
        rows = pl.ds(i * 128, 128)
        loads[i].wait()
        values = tok_ref[rows, :].astype(F32)
        scale = lax.rsqrt(jnp.mean(values * values, axis=-1, keepdims=True) + epsilon)
        values = (values * scale * gain).astype(BF16)
        normed[rows, :] = values
        r = i // 2
        steps = pl.ds((i % 2) * 128, 128)
        order = base_ref[r * 256] + (i % 2) * 128 + lax.broadcasted_iota(jnp.int32, (128, 128), 0)
        for req in range(REQS):
            start = starts_ref[req]
            runs = jnp.maximum(base_ref[r * 256] // 256 - start // 256, 0)
            far_c, far_s = far_cos[pl.ds(runs, 1), :], far_sin[pl.ds(runs, 1), :]
            off_c, off_s = step_cos[pl.ds(start % 256, 1), :], step_sin[pl.ds(start % 256, 1), :]
            run_c = jnp.broadcast_to(far_c * off_c + far_s * off_s, (128, 128))
            run_s = jnp.broadcast_to(far_s * off_c - far_c * off_s, (128, 128))
            later = order >= start
            near_cos = jnp.where(later, run_c, near_cos) if req else run_c
            near_sin = jnp.where(later, run_s, near_sin) if req else run_s
        cosines[rows, :] = step_cos[steps, :] * near_cos - step_sin[steps, :] * near_sin
        sine = step_sin[steps, :] * near_cos + step_cos[steps, :] * near_sin
        sines[rows, :] = jnp.where(lane < 64, -sine, sine)
        key = jnp.dot(values, wk_ref[...], preferred_element_type=F32)
        kv_ref[rows, 0:128] = turn(key, i).astype(BF16)
        value = jnp.dot(values, wv_ref[...], preferred_element_type=F32)
        kv_ref[rows, 128:256] = value.astype(BF16)

    half = lax.broadcasted_iota(jnp.int32, (16, 256), 1)
    run = jnp.where(half < 128, base_ref[0] // 256, base_ref[256] // 256).astype(F32)
    kv_ref[512:528, :] = run.astype(BF16)
    keys_values(0)
    pl.semaphore_wait(barrier, 6)
    started = []

    def go(src, dst, recv, peer):
        copy = pltpu.make_async_remote_copy(
            src_ref=src, dst_ref=dst, send_sem=send_sem.at[len(started)], recv_sem=recv,
            device_id=peer, device_id_type=MESH,
        )
        copy.start()
        started.append(copy)

    def take(dst, recv):
        pltpu.make_async_remote_copy(
            src_ref=dst, dst_ref=dst, send_sem=send_sem.at[0], recv_sem=recv,
            device_id=core, device_id_type=MESH,
        ).wait_recv()

    def kv_view(block, p):
        low, count = PIECE_ROWS[p]
        return kv_all.at[block, pl.ds(low, count), :]

    def kv_take(dz, p, peers):
        block = ((z + dz + 8) % 8) * 2 + c
        take(kv_view(block, p), kv_sem.at[block, p])
        for peer in peers:
            go(kv_view(block, p), kv_view(block, p), kv_sem.at[block, p], peer)

    def w_take(dx, p, peers):
        shard, piece = (x + dx + 4) % 4, 2 * c + p
        take(w_all.at[shard, piece], w_sem.at[shard, piece])
        for peer in peers:
            go(w_all.at[shard, piece], w_all.at[shard, piece], w_sem.at[shard, piece], peer)

    mine = z * 2 + c
    for p in range(4):
        if p:
            keys_values(p)
        low, count = PIECE_ROWS[p]
        for peer in (up, down, core):
            go(kv_ref.at[pl.ds(low, count), :], kv_view(mine, p), kv_sem.at[mine, p], peer)
        if p < 2:
            piece = 2 * c + p
            for peer in (right, left):
                go(w_ref.at[piece], w_all.at[x, piece], w_sem.at[x, piece], peer)
    own = pltpu.make_async_copy(kv_ref, kv_all.at[mine], own_sem.at[0])
    own.start()
    loads[4].wait()
    for p in range(4):
        rows = pl.ds(p * 128, 128)
        query = jnp.dot(normed[rows, :], wq_ref[...], preferred_element_type=F32)
        q_ref[rows, 0:128] = (turn(query[:, 0:128], p) * SCALE).astype(BF16)
        q_ref[rows, 128:256] = (turn(query[:, 128:256], p) * SCALE).astype(BF16)
    row = lax.broadcasted_iota(jnp.int32, (16, 256), 0)
    for i in range(32):
        run = jnp.where((row == 1) & (half == i), live_ref[i].astype(F32), run)
    q_ref[512:528, :] = run.astype(BF16)
    go(q_ref, q_all, q_sem.at[0], side)

    for d in (1, 2):
        for p in range(4):
            kv_take(-d, p, (up, core))
            kv_take(d, p, (down, core))
        if d == 1:
            w_take(-1, 0, (right, core))
            w_take(1, 0, (core,))
    w_take(-1, 1, (core,))
    w_take(1, 1, (left, core))
    slots = slot_ref[...]
    for i in range(4):
        row = i * 128 + lax.broadcasted_iota(jnp.int32, (128, 512), 0)
        pick = jnp.where(row == slots, 1.0, 0.0).astype(BF16)
        moved = jnp.dot(pick, kv_ref[0:512, :], preferred_element_type=F32)
        cache_ref[i * 128 : (i + 1) * 128, :] = moved.astype(BF16)
    request = lax.broadcasted_iota(jnp.int32, (8, 64), 0) % REQS
    last = jnp.full((8, 64), starts_ref[1] - 1, jnp.int32)
    for req in range(1, REQS):
        last = jnp.where(request == req, starts_ref[req + 1] - 1, last)
    for i in range(8):
        order = base_ref[256 * (i // 4)] + (i % 4) * 64 + lax.broadcasted_iota(jnp.int32, (8, 64), 1)
        match_ref[i] = jnp.where(order == last, 1.0, 0.0).astype(BF16)
    for p in range(4):
        kv_take(-3, p, (up, core) if p < 2 else (core,))
        kv_take(3, p, (down, core) if p >= 2 else (core,))
    for p in range(2):
        w_take(2, p, (core,))
    for p in range(4):
        kv_take(4, p, (core,))

    for dz in range(8):
        for p in range(4):
            block = ((z + dz) % 8) * 2 + 1 - c
            take(kv_view(block, p), kv_sem.at[block, p])
    take(q_all, q_sem.at[0])
    own.wait()
    ends = [
        pltpu.make_async_copy(kv_all.at[:, pl.ds(512, 16), :], tails.at[pl.ds(0, 16)], own_sem.at[0]),
        pltpu.make_async_copy(q_all.at[pl.ds(512, 16), :], tails.at[16], own_sem.at[1]),
    ]
    for copy in ends:
        copy.start()
    for dx in range(1, 4):
        for p in range(2):
            shard, piece = (x + dx) % 4, 2 * (1 - c) + p
            take(w_all.at[shard, piece], w_sem.at[shard, piece])
    for copy in ends:
        copy.wait()
    rows = tails[0:16].astype(F32)[:, 0, :].astype(jnp.int32)
    tail_ref[0:16, :] = rows[:, 0:128]
    tail_ref[16:32, :] = rows[:, 128:256]
    rows = tails[16].astype(F32)[0:8, :].astype(jnp.int32)
    tail_ref[32:33, :] = rows[0:1, 0:128]
    tail_ref[33:34, :] = rows[0:1, 128:256]
    tail_ref[34:35, :] = rows[1:2, 0:128]
    tail_ref[35:40, :] = jnp.zeros((5, 128), jnp.int32)
    for copy in started:
        copy.wait_send()


SLOTS = 8


def attend_kernel(
    tail_ref, base_ref, starts_ref, live_ref, me_ref, q_ref, other_ref, kv_ref, o_ref, st_ref,
    buf, sem, q_rows, top, total, acc, scores0, scores1, probs0, probs1, keep0, keep1,
    table, sorted_run, sorted_entry, before,
):
    me = me_ref[0]
    my_y = (me // 2) % 2
    other = me + 2 - 4 * my_y
    all_scores, all_probs, all_keep = (scores0, scores1), (probs0, probs1), (keep0, keep1)
    q_run = [base_ref[0] // 256, base_ref[256] // 256, tail_ref[32, 0], tail_ref[33, 0]]

    def clear(i, carry):
        table[i] = -1
        return carry

    def enter(i, carry):
        table[tail_ref[i, 0]] = i
        return carry

    def gather_up(i, count):
        before[i] = count
        entry = table[i]
        sorted_run[count] = i
        sorted_entry[count] = entry
        return jnp.where(entry >= 0, count + 1, count)

    lax.fori_loop(0, 64, clear, 0, unroll=8)
    lax.fori_loop(0, 32, enter, 0, unroll=8)
    before[64] = lax.fori_loop(0, 64, gather_up, 0, unroll=8)

    def low_of(position):
        low = starts_ref[0]
        for r in range(1, REQS):
            low = jnp.where(starts_ref[r] <= position, starts_ref[r], low)
        return low

    lasts, shifts, offsets = [], [], [0]
    for r in range(4):
        first = before[low_of(q_run[r] * 256) // 256]
        lasts.append(low_of(q_run[r] * 256 + 255))
        shifts.append(first - offsets[-1])
        offsets.append(offsets[-1] + before[q_run[r] + 1] - first)
    n = offsets[4]

    def choose(i, values):
        out = values[0]
        for r in range(1, 4):
            out = jnp.where(i >= offsets[r], values[r], out)
        return out

    def half(i):
        return choose(i, [0, 1, 2, 3])

    def place(i):
        return (i + choose(i, shifts)) & 31

    def key_run(i):
        return sorted_run[place(i)]

    def fetch(i):
        entry = sorted_entry[place(i)]
        slot = i & (SLOTS - 1)
        return pltpu.make_async_copy(
            kv_ref.at[entry & 15, pl.ds(pl.multiple_of((entry >> 4) * 256, 256), 256), :], buf.at[slot], sem.at[slot]
        )

    for i in range(SLOTS - 2):

        @pl.when(i < n)
        def _():
            fetch(i).start()

    for r in range(4):
        source = q_ref if r < 2 else other_ref
        for h in range(2):
            q_rows[r, pl.ds(h * 256, 256), :] = source[
                pl.ds((r % 2) * 256, 256), pl.ds(h * 128, 128)
            ]
    top[...] = jnp.full_like(top, neg_fill)
    total[...] = jnp.zeros_like(total)
    acc[...] = jnp.zeros_like(acc)
    buf[SLOTS - 1] = jnp.zeros((256, 256), BF16)
    probs1[...] = jnp.zeros_like(probs1)
    keep1[...] = jnp.ones_like(keep1)

    def score(i, into):
        into[...] = lax.dot_general(
            buf[i & (SLOTS - 1), :, 0:128], q_rows[half(i)],
            (((1,), (1,)), ((), ())), preferred_element_type=F32,
        )

    def collect(i, parity):
        r = half(i)
        added = lax.dot_general(
            buf[(i + SLOTS) & (SLOTS - 1), :, 128:256], all_probs[parity][...],
            (((0,), (0,)), ((), ())), preferred_element_type=F32,
        )
        acc[r] = acc[r] * all_keep[parity][...] + added

    def weigh(i, parity, masked, base):
        r = half(i)
        scores = all_scores[parity][...]
        if masked:
            lane = lax.broadcasted_iota(jnp.int32, (1, 512), 1)
            q_pos = base + (lane & 255)
            low = jnp.full((1, 512), starts_ref[0], jnp.int32)
            for req in range(1, REQS):
                low = jnp.where(starts_ref[req] <= q_pos, starts_ref[req], low)
            k_pos = key_run(i) * 256 + lax.broadcasted_iota(jnp.int32, (256, 512), 0)
            allowed = (k_pos <= q_pos) & (k_pos >= low)
            scores = jnp.where(allowed, scores, neg_fill)
        old = top[r]
        new = jnp.maximum(old, jnp.max(scores, axis=0, keepdims=True))
        probs = jnp.exp2(scores - new)
        if masked:
            probs = jnp.where(allowed, probs, 0.0)
        keep = jnp.exp2(old - new)
        top[r] = new
        total[r] = total[r] * keep + jnp.sum(probs, axis=0, keepdims=True)
        all_keep[parity][...] = keep
        all_probs[parity][...] = probs.astype(BF16)

    def stage(i, parity):
        @pl.when(i + SLOTS - 2 < n)
        def _():
            fetch(i + SLOTS - 2).start()

        @pl.when(i + 1 < n)
        def _():
            fetch(i + 1).wait()

        run = key_run(i)
        base = choose(i, q_run) * 256
        last_low = choose(i, lasts)
        slot = sorted_entry[place(i)] & 15
        block = (slot >> 1) * 4 + my_y * 2 + (slot & 1)
        live = jnp.where(
            i < offsets[2], live_ref[(me - block) & 31], tail_ref[34, (other - block) & 31]
        ) > 0
        whole = (run * 256 < base) & (run * 256 >= last_low)

        @pl.when(live & whole)
        def _():
            weigh(i, parity, False, base)
            score(i + 1, all_scores[1 - parity])
            collect(i - 1, 1 - parity)

        @pl.when(live & jnp.logical_not(whole))
        def _():
            weigh(i, parity, True, base)
            score(i + 1, all_scores[1 - parity])
            collect(i - 1, 1 - parity)

        @pl.when(jnp.logical_not(live))
        def _():
            score(i + 1, all_scores[1 - parity])
            collect(i - 1, 1 - parity)
            all_keep[parity][...] = jnp.ones((1, 512), F32)
            all_probs[parity][...] = jnp.zeros((256, 512), BF16)

    def pair(k, carry):
        stage(2 * k, 0)

        @pl.when(2 * k + 1 < n)
        def _():
            stage(2 * k + 1, 1)

        return carry

    fetch(0).wait()
    score(0, scores0)
    lax.fori_loop(0, (n + 1) // 2, pair, 0)

    @pl.when(n % 2 == 1)
    def _():
        collect(n - 1, 0)

    @pl.when(n % 2 == 0)
    def _():
        collect(n - 1, 1)

    for r in range(4):
        weight = total[r]
        done = (acc[r] * jnp.where(weight > 0, 1.0 / weight, 0.0)).astype(BF16)
        for part in range(2):
            k = 2 * (r % 2) + part
            for h in range(2):
                low = h * 256 + part * 128
                o_ref[r // 2, k, h * 128 : (h + 1) * 128, :] = done[:, low : low + 128]
                st_ref[r // 2, k, h : h + 1, :] = top[r, :, low : low + 128]
                st_ref[r // 2, k, 2 + h : 3 + h, :] = weight[:, low : low + 128]


def middle_kernel(
    heads_ref, stats_ref, w_ref, w_own, tok_ref, gain_ref, wg_ref, wu_ref, wd_ref, match_ref, final_ref, head_ref,
    out_ref, rms_ref, top_ref,
    heads, stats, joined, near_send, near_got, w, tok_rows, tok_cols, wg, wu, wd, att, att_send, att_cols, normed, act, part, fwd_in,
    x_in, y_in, head, row_send, seq_got, wide_send, wide_got, last_send, last_got, max_send, seq_max, vocab_max,
    load_sem, send_sem, head_recv, stat_recv, near_recv, norm_recv, att_recv, fwd_recv, x_recv, y_recv,
    row_recv, wide_recv, last_recv, max_recv, top_recv,
):
    s = lax.axis_index("seq")
    v = lax.axis_index("vocab")
    others = [(v + r) % 8 for r in range(1, 8)]
    seqs = [(s + r) % 32 for r in range(1, 32)]
    cols = pl.ds(pl.multiple_of(v * 256, 256), 256)
    rows = pl.ds(pl.multiple_of(v * 64, 64), 64)
    loads = [
        pltpu.make_async_copy(w_own, w.at[v // 2], load_sem.at[0]),
        pltpu.make_async_copy(tok_ref.at[rows, :], tok_rows, load_sem.at[1]),
        pltpu.make_async_copy(tok_ref.at[:, cols], tok_cols, load_sem.at[2]),
        pltpu.make_async_copy(wg_ref, wg, load_sem.at[3]),
        pltpu.make_async_copy(wu_ref, wu, load_sem.at[4]),
        pltpu.make_async_copy(wd_ref, wd, load_sem.at[5]),
        pltpu.make_async_copy(heads_ref.at[0, v // 2], heads.at[v // 2, (s // 2) % 2], load_sem.at[6]),
        pltpu.make_async_copy(stats_ref.at[0, v // 2], stats.at[v // 2, (s // 2) % 2], load_sem.at[9]),
        pltpu.make_async_copy(head_ref, head, load_sem.at[8]),
    ] + [
        pltpu.make_async_copy(
            w_ref.at[(v // 2 + d) % 4], w.at[(v // 2 + d) % 4], load_sem.at[9 + d]
        )
        for d in range(1, 4)
    ]
    for copy in loads:
        copy.start()
    x = v // 2
    y = v % 2
    my_y = (s // 2) % 2
    across = seq_at(s, 0, 1, 0)
    greet(
        [(s, other) for other in others]
        + [(other, v) for other in seqs]
        + [(across, vocab_at(v, dx, 0)) for dx in range(1, 4)]
    )
    sent = []

    def go(src, dst, recv, peer):
        copy = pltpu.make_async_remote_copy(
            src_ref=src, dst_ref=dst, send_sem=send_sem.at[len(sent)], recv_sem=recv,
            device_id=peer, device_id_type=MESH,
        )
        copy.start()
        sent.append(copy)

    def take(dst, recv):
        pltpu.make_async_remote_copy(
            src_ref=dst, dst_ref=dst, send_sem=send_sem.at[0], recv_sem=recv,
            device_id=(s, others[0]), device_id_type=MESH,
        ).wait_recv()

    for dx in (2, 1, 3, 0):
        target = (x + dx) % 4
        for which in (1, 0):
            if (dx, which) != (0, 0):
                peer = (across if which else s, vocab_at(v, dx, 0))
                go(heads_ref.at[which, target], heads.at[x, my_y], head_recv.at[x, my_y], peer)
                go(stats_ref.at[which, target], stats.at[x, my_y], stat_recv.at[x, my_y], peer)
    for i in (0, 1, 6, 7, 9, 10, 11):
        loads[i].wait()
    for dx in range(4):
        source = (x + dx) % 4
        for which in range(2):
            if (dx, which) != (0, 0):
                held = (my_y + which) % 2
                take(heads.at[source, held], head_recv.at[source, held])
                take(stats.at[source, held], stat_recv.at[source, held])
    for k in range(4):
        for h in range(2):
            tops = [stats[k, i, h : h + 1, :] for i in range(2)]
            best = jnp.maximum(tops[0], tops[1])
            weights = [stats[k, i, 2 + h : 3 + h, :] * jnp.exp2(tops[i] - best) for i in range(2)]
            scale = 1.0 / (weights[0] + weights[1])
            span = pl.ds(h * 128, 128)
            joined[k, span, :] = (
                heads[k, 0, span, :].astype(F32) * (weights[0] * scale)
                + heads[k, 1, span, :].astype(F32) * (weights[1] * scale)
            ).astype(BF16)

    near = vocab_at(v, 0, 1)
    for j in range(4):
        total = jnp.zeros((128, 512), F32)
        for k in range(4):
            total += lax.dot_general(
                joined[k], w[k, :, j * 512 : (j + 1) * 512],
                (((0,), (0,)), ((), ())), preferred_element_type=F32,
            )
        att[:, j * 512 : (j + 1) * 512] = jnp.where(y == 0, total[0:64], total[64:128])
        near_send[j] = jnp.where(y == 0, total[64:128], total[0:64]).astype(BF16)
        go(near_send.at[j], near_got.at[j], near_recv.at[j], (s, near))
    for j in range(4):
        take(near_got.at[j], near_recv.at[j])

    def project(j, square):
        wide = pl.ds(pl.multiple_of(j * 512, 512), 512)
        total = att[:, wide] + near_got[j].astype(F32)
        att_send[2 * j] = total[:, 0:256].astype(BF16)
        att_send[2 * j + 1] = total[:, 256:512].astype(BF16)
        residual = tok_rows[:, wide].astype(F32) + total
        att[:, wide] = residual
        return square + jnp.sum(residual * residual, axis=-1, keepdims=True)

    square = lax.fori_loop(0, 4, project, jnp.zeros((64, 1), F32))
    gain = wide_row(gain_ref)
    mine = (att[...] * lax.rsqrt(square / 2048 + epsilon) * gain).astype(BF16)
    normed[2 * v] = mine[0:32]
    normed[2 * v + 1] = mine[32:64]

    right, left = vocab_at(v, 1, 0), vocab_at(v, -1, 0)

    def pass_on(owner, p, other):
        view = normed.at[2 * owner + p]
        go(view, view, norm_recv.at[owner, p], (s, other))

    def arrive(dx, dy, p, peers):
        owner = vocab_at(v, dx, dy)
        take(normed.at[2 * owner + p], norm_recv.at[owner, p])
        for peer in peers:
            pass_on(owner, p, peer)

    for other in others:
        go(att_send.at[other], att_cols.at[v], att_recv.at[v], (s, other))
    for p in range(2):
        for peer in (right, left, near):
            pass_on(v, p, peer)
    own_cols = pltpu.make_async_copy(att_send.at[v], att_cols.at[v], load_sem.at[7])
    own_cols.start()

    loads[2].wait()
    own_cols.wait()
    for other in others:
        take(att_cols.at[other], att_recv.at[other])
    picked = jnp.zeros((8, 256), F32)
    for i in range(8):
        residual = tok_cols[i * 64 : (i + 1) * 64, :].astype(F32) + att_cols[i].astype(F32)
        high = residual.astype(BF16)
        low = (residual - high.astype(F32)).astype(BF16)
        picked += jnp.dot(match_ref[i], high, preferred_element_type=F32)
        picked += jnp.dot(match_ref[i], low, preferred_element_type=F32)
    row_send[...] = picked
    seq_got[s] = picked
    for other in seqs:
        go(row_send, seq_got.at[s], row_recv.at[s], (other, v))

    for p in range(2):
        arrive(-1, 0, p, (right,) if p == 0 else ())
        arrive(1, 0, p, (left,) if p == 1 else ())
        arrive(0, 1, p, (right, left))

    for i in (3, 4, 5):
        loads[i].wait()
    def feed(values):
        gate = jnp.dot(values, wg[...], preferred_element_type=F32)
        upward = jnp.dot(values, wu[...], preferred_element_type=F32)
        return (gate / (1.0 + jnp.exp(-gate)) * upward).astype(BF16)

    def part_of(chunk, dx, dy):
        return part.at[chunk, vocab_at(v, dx, dy)]

    def at_y(chunk, dx, lane):
        return part.at[chunk, ((x + dx + 4) % 4) * 2 + lane]

    def rows_of(dx, extra):
        chunk = (x + dx + 4) % 4
        values = normed[pl.ds(4 * chunk, 4)].reshape(128, 2048)
        if extra:
            values = jnp.concatenate([values, normed[16]], axis=0)
        active = feed(values)
        if extra:
            act[...] = active[128:144]
            active = active[0:128]
        for t in range(8):
            part[chunk, t] = jnp.dot(
                active, wd[:, t * 256 : (t + 1) * 256], preferred_element_type=F32
            ).astype(BF16)
        go(at_y(chunk, 2, 0), fwd_in.at[chunk, 0], fwd_recv.at[chunk, 0], (s, right))
        go(at_y(chunk, 2, 1), fwd_in.at[chunk, 1], fwd_recv.at[chunk, 1], (s, left))
        go(at_y(chunk, 1, 1), x_in.at[chunk, 0, 1], x_recv.at[chunk, 0, 1], (s, right))
        go(at_y(chunk, -1, 0), x_in.at[chunk, 1, 0], x_recv.at[chunk, 1, 0], (s, left))

    rows_of(0, False)
    for other in seqs:
        take(seq_got.at[other], row_recv.at[other])
    picked = jnp.sum(seq_got[...], axis=0)
    wide_send[...] = picked
    wide_got[v] = picked
    for other in others:
        go(wide_send, wide_got.at[v], wide_recv.at[v], (s, other))

    for p in range(2):
        arrive(2, 0, p, (near,))
    for p in range(2):
        arrive(-1, 1, p, ())
        arrive(1, 1, p, ())
    rows_of(-1, False)
    for other in others:
        take(wide_got.at[other], wide_recv.at[other])
    square = jnp.zeros((8, 1), F32)
    for k in range(8):
        square += jnp.sum(wide_got[k] * wide_got[k], axis=-1, keepdims=True)
    inverse = lax.rsqrt(square / 2048 + epsilon)
    normed[16, 16:32, :] = jnp.zeros((16, 2048), BF16)
    for k in range(8):
        one = wide_got[k] * inverse * gain[:, k * 256 : (k + 1) * 256]
        normed[16, 0:16, k * 256 : (k + 1) * 256] = jnp.concatenate([one, one], axis=0).astype(BF16)
    rows_of(1, True)

    group = lax.broadcasted_iota(jnp.int32, (16, 512), 0) // 4

    def packed(quarter):
        out = quarter(0)
        for q in range(1, 4):
            out = jnp.where(group == q, quarter(q), out)
        return out

    last = act[...]
    mine = packed(
        lambda q: jnp.dot(
            last, wd[:, q * 512 : (q + 1) * 512], preferred_element_type=F32
        )
    ).astype(BF16)
    last_send[...] = mine
    last_got[v] = mine
    for other in others:
        go(last_send, last_got.at[v], last_recv.at[v], (s, other))
    for p in range(2):
        arrive(2, 1, p, ())
    rows_of(2, False)

    def add_to(ref, *incoming):
        value = ref[...].astype(F32)
        for one in incoming:
            value += one[...].astype(F32)
        ref[...] = value.astype(BF16)

    def onward(dx, way):
        chunk = (x + dx + 4) % 4
        take(fwd_in.at[chunk, way], fwd_recv.at[chunk, way])
        ref = at_y(chunk, 1 if way == 0 else -1, way)
        add_to(ref, fwd_in.at[chunk, way])
        go(ref, x_in.at[chunk, way, way], x_recv.at[chunk, way, way], (s, right if way == 0 else left))

    for to_right, to_left in ((-1, 1), (2, 0)):
        onward(to_right, 0)
        onward(to_left, 1)

    for other in others:
        take(last_got.at[other], last_recv.at[other])

    def quarter_rows(q):
        one = jnp.concatenate([wide_got[2 * q], wide_got[2 * q + 1]], axis=1)
        return jnp.concatenate([one, one], axis=0)

    total = last_got[0].astype(F32)
    for k in range(1, 8):
        total += last_got[k].astype(F32)
    final = (packed(quarter_rows) + total).astype(BF16).astype(F32)
    square = jnp.broadcast_to(jnp.sum(final * final, axis=-1, keepdims=True), (16, 128))
    square = square + pltpu.roll(square, 8, axis=0)
    square = square + pltpu.roll(square, 4, axis=0)
    mean_square = square / 2048 + epsilon
    diagonal = lax.broadcasted_iota(jnp.int32, (16, 128), 0) == lax.broadcasted_iota(
        jnp.int32, (16, 128), 1
    )

    def along_lanes(value):
        return jnp.sum(jnp.where(diagonal, value, 0.0), axis=0, keepdims=True)

    rms_ref[...] = along_lanes(jnp.sqrt(mean_square))[:, :REQS]
    inverse = lax.rsqrt(mean_square)[:, 0:1]
    last_gain = wide_row(final_ref)
    spread = packed(
        lambda q: jnp.broadcast_to(last_gain[:, q * 512 : (q + 1) * 512], (16, 512))
    )
    final = final * inverse * spread
    loads[8].wait()
    logits = jnp.zeros((16, 360), F32)
    for q in range(4):
        turned = final if q == 0 else pltpu.roll(final, 16 - 4 * q, axis=0)
        logits += lax.dot_general(
            turned.astype(BF16), head[:, q * 512 : (q + 1) * 512], (((1,), (1,)), ((), ())),
            preferred_element_type=F32,
        )
    best = along_lanes(jnp.broadcast_to(jnp.max(logits, axis=-1, keepdims=True), (16, 128)))
    best = jnp.broadcast_to(best, (8, 128))
    max_send[0] = best
    seq_max[s] = best
    for other in seqs:
        go(max_send.at[0], seq_max.at[s], max_recv.at[s], (other, v))
    for to_right, to_left in ((0, 2), (1, -1)):
        onward(to_right, 0)
        onward(to_left, 1)

    for dx in (0, -1, 1, 2):
        chunk = (x + dx + 4) % 4
        for way in range(2):
            take(x_in.at[chunk, way, 1 - y], x_recv.at[chunk, way, 1 - y])
        ref = part_of(chunk, 0, 1)
        add_to(ref, x_in.at[chunk, 0, 1 - y], x_in.at[chunk, 1, 1 - y])
        go(ref, y_in.at[chunk], y_recv.at[chunk], (s, near))

    for other in seqs:
        take(seq_max.at[other], max_recv.at[other])
    best = jnp.max(seq_max[...], axis=0)
    max_send[1] = best
    vocab_max[v] = best
    for other in others:
        go(max_send.at[1], vocab_max.at[v], top_recv.at[v], (s, other))

    for dx in (0, -1, 1, 2):
        chunk = (x + dx + 4) % 4
        for way in range(2):
            take(x_in.at[chunk, way, y], x_recv.at[chunk, way, y])
        take(y_in.at[chunk], y_recv.at[chunk])
        rows = pl.ds(pl.multiple_of(chunk * 128, 128), 128)
        total = tok_cols[rows, :].astype(F32)
        total += att_cols[pl.ds(2 * chunk, 2)].reshape(128, 256).astype(F32)
        total += part[chunk, v].astype(F32)
        total += x_in[chunk, 0, y].astype(F32)
        total += x_in[chunk, 1, y].astype(F32)
        total += y_in[chunk].astype(F32)
        out_ref[rows, :] = total.astype(BF16)
    for other in others:
        take(vocab_max.at[other], top_recv.at[other])
    top_ref[...] = jnp.max(vocab_max[...], axis=0)[0:1, :REQS]
    for copy in sent:
        copy.wait_send()


def hand_over_kernel(hidden_ref, rms_ref, top_ref, hidden_out, rms_out, top_out):
    hidden_out[...] = hidden_ref[...]
    rms_out[...] = rms_ref[...]
    top_out[...] = top_ref[...]


def per_device(
    tokens,
    attention_gain,
    query_weight,
    key_weight,
    value_weight,
    out_weight,
    forward_gain,
    gate_weight,
    up_weight,
    down_weight,
    final_gain,
    head_weight,
    segment_ids,
    token_order,
    live_blocks,
    cache_slots,
):
    shape = jax.ShapeDtypeStruct
    me = lax.axis_index("seq").astype(jnp.int32)
    request = jnp.arange(8, dtype=jnp.int32)
    starts = jnp.sum((segment_ids[None, :] < request[:, None]).astype(jnp.int32), axis=1)
    query, cache, match, kv_all, q_other, w_all, tail = pl.pallas_call(
        gather_kernel,
        out_shape=(
            shape((528, 256), BF16), shape((512, 256), BF16), shape((8, 8, 64), BF16),
            shape((16, 528, 256), BF16), shape((528, 256), BF16), shape((4, 4, 64, 2048), BF16),
            shape((40, 128), jnp.int32),
        ),
        in_specs=[SM] * 3 + [HB, VM, HB] + [VM] * 7 + [HB],
        out_specs=(VM, VM, VM, HB, HB, HB, VM),
        scratch_shapes=[
            pltpu.VMEM((512, 2048), BF16),
            pltpu.VMEM((2048, 256), BF16),
            pltpu.SemaphoreType.DMA((5,)),
            pltpu.VMEM((528, 256), BF16),
            pltpu.VMEM((512, 2048), BF16),
            pltpu.VMEM((512, 128), F32),
            pltpu.VMEM((512, 128), F32),
            pltpu.VMEM((17, 16, 256), BF16),
            pltpu.SemaphoreType.DMA((2,)),
            pltpu.SemaphoreType.DMA((128,)),
            pltpu.SemaphoreType.DMA((16, 4)),
            pltpu.SemaphoreType.DMA((1,)),
            pltpu.SemaphoreType.DMA((4, 4)),
        ],
        compiler_params=params(0),
        name="gather",
    )(
        token_order, starts, live_blocks[0], tokens, attention_gain.reshape(16, 128), query_weight,
        key_weight, value_weight, jnp.asarray(STEP_COS), jnp.asarray(STEP_SIN), jnp.asarray(FAR_COS),
        jnp.asarray(FAR_SIN), cache_slots[None], out_weight.reshape(4, 64, 2048),
    )

    heads, stats = pl.pallas_call(
        attend_kernel,
        out_shape=(shape((2, 4, 256, 128), BF16), shape((2, 4, 8, 128), F32)),
        in_specs=[SM] * 5 + [VM, VM, HB],
        out_specs=(VM, VM),
        scratch_shapes=[
            pltpu.VMEM((SLOTS, 256, 256), BF16),
            pltpu.SemaphoreType.DMA((SLOTS,)),
            pltpu.VMEM((4, 512, 128), BF16),
            pltpu.VMEM((4, 1, 512), F32),
            pltpu.VMEM((4, 1, 512), F32),
            pltpu.VMEM((4, 128, 512), F32),
            pltpu.VMEM((256, 512), F32),
            pltpu.VMEM((256, 512), F32),
            pltpu.VMEM((256, 512), BF16),
            pltpu.VMEM((256, 512), BF16),
            pltpu.VMEM((1, 512), F32),
            pltpu.VMEM((1, 512), F32),
            pltpu.SMEM((64,), jnp.int32),
            pltpu.SMEM((33,), jnp.int32),
            pltpu.SMEM((33,), jnp.int32),
            pltpu.SMEM((65,), jnp.int32),
        ],
        compiler_params=params(),
        name="attend",
    )(tail, token_order, starts, live_blocks[0], me[None], query, q_other, kv_all)

    dma = pltpu.SemaphoreType.DMA
    hidden, rms, top = pl.pallas_call(
        middle_kernel,
        out_shape=(shape((512, 256), BF16), shape((1, REQS), F32), shape((1, REQS), F32)),
        in_specs=[VM, VM, HB, HB, HB, VM, HB, HB, HB, VM, VM, HB],
        out_specs=(VM, VM, VM),
        scratch_shapes=[
            pltpu.VMEM((4, 2, 256, 128), BF16),
            pltpu.VMEM((4, 2, 8, 128), F32),
            pltpu.VMEM((4, 256, 128), BF16),
            pltpu.VMEM((4, 64, 512), BF16),
            pltpu.VMEM((4, 64, 512), BF16),
            pltpu.VMEM((4, 256, 2048), BF16),
            pltpu.VMEM((64, 2048), BF16),
            pltpu.VMEM((512, 256), BF16),
            pltpu.VMEM((2048, 512), BF16),
            pltpu.VMEM((2048, 512), BF16),
            pltpu.VMEM((512, 2048), BF16),
            pltpu.VMEM((64, 2048), F32),
            pltpu.VMEM((8, 64, 256), BF16),
            pltpu.VMEM((8, 64, 256), BF16),
            pltpu.VMEM((17, 32, 2048), BF16),
            pltpu.VMEM((16, 512), BF16),
            pltpu.VMEM((4, 8, 128, 256), BF16),
            pltpu.VMEM((4, 2, 128, 256), BF16),
            pltpu.VMEM((4, 2, 2, 128, 256), BF16),
            pltpu.VMEM((4, 128, 256), BF16),
            pltpu.VMEM((360, 2048), BF16),
            pltpu.VMEM((8, 256), F32),
            pltpu.VMEM((32, 8, 256), F32),
            pltpu.VMEM((8, 256), F32),
            pltpu.VMEM((8, 8, 256), F32),
            pltpu.VMEM((16, 512), BF16),
            pltpu.VMEM((8, 16, 512), BF16),
            pltpu.VMEM((2, 8, 128), F32),
            pltpu.VMEM((32, 8, 128), F32),
            pltpu.VMEM((8, 8, 128), F32),
            dma((13,)), dma((192,)), dma((4, 2)), dma((4, 2)), dma((4,)), dma((8, 2)), dma((8,)), dma((4, 2)), dma((4, 2, 2)), dma((4,)),
            dma((32,)), dma((8,)), dma((8,)), dma((32,)), dma((8,)),
        ],
        compiler_params=params(1),
        name="middle",
    )(
        heads, stats, w_all.reshape(4, 256, 2048), out_weight, tokens, forward_gain.reshape(16, 128), gate_weight, up_weight,
        down_weight, match, final_gain.reshape(16, 128), head_weight,
    )
    hidden, rms, top = pl.pallas_call(
        hand_over_kernel,
        out_shape=(shape((512, 256), BF16), shape((1, REQS), F32), shape((1, REQS), F32)),
        in_specs=[VM, VM, VM],
        out_specs=(VM, VM, VM),
        compiler_params=params(),
        name="hand_over",
    )(hidden, rms, top)
    return (hidden, cache.reshape(512, 2, 128), rms.reshape(REQS), top.reshape(REQS))


def solution(mesh):
    return jax.shard_map(
        per_device,
        mesh=mesh,
        in_specs=(
            P("seq", None),
            P(),
            P(None, "vocab"),
            P(None, "vocab"),
            P(None, "vocab"),
            P("vocab", None),
            P(),
            P(None, "vocab"),
            P(None, "vocab"),
            P("vocab", None),
            P(),
            P(("seq", "vocab"), None),
            P(),
            P("seq"),
            P("seq", None),
            P("seq"),
        ),
        out_specs=(P("seq", "vocab"), P("seq", None, "vocab"), P(), P()),
        check_vma=False,
    )
```
